128 devices in a mesh: ctx: 32 (over x, z, y_hi), tp: 4 (over y_lo, core).
Axes of the slice: x: 4, y: 4 (y_hi: 2, y_lo: 2; y = y_hi * 2 + y_lo), z: 4, core: 2. Of those that a mesh axis runs over, the one named last changes fastest.
Arguments:
- queries: bfloat16 [24576, 2048], P('ctx', 'tp'), may hold values from -24 to 24
- keyvals: bfloat16 [24576, 2, 2048], P('ctx', None, 'tp'), may hold values from -6 to 6
- residual: bfloat16 [24576, 4096], P('ctx', 'tp'), may hold values from -6 to 6
- out_weight: bfloat16 [2048, 4096], P('tp'), may hold values from -0.125 to 0.125
- norm_gain: bfloat16 [4096], P('tp'), may hold values from 0.5 to 1.5
- norm_bias: bfloat16 [4096], P('tp'), may hold values from -3 to 3
- cross_weight: bfloat16 [4096, 2, 2048], P(None, None, 'tp'), may hold values from -0.09375 to 0.09375
- window_reach: int32 [16], P('tp'), may hold values from 1 to 3, as said below
- global_blocks: int32 [2], replicated, may hold values from 0 to 383, as said below
- random_blocks: int32 [384, 3], replicated, may hold values from 0 to 383, as said below
Outputs:
- encoded: bfloat16 [24576, 4096], P('ctx', 'tp')
- cross_kv: bfloat16 [24576, 2, 2048], P('ctx', None, 'tp')
The draws below stay inside these ranges and needn't reach their ends.
Inputs may be any that keep to these rules, and one draw needn't show every extreme that they name: `window_reach`: some head has reach 3 and some head reach 1. `global_blocks`: 2 distinct block numbers; one of them is the document's last block. `random_blocks`: for the query blocks s*12 to (s+1)*12 - 1 of any index s of ctx, at most 3 of their 36 random entries name blocks of one index of ctx (block number // 12); for every s exactly 3 do for some index.
All inputs are finite; a program needn't handle non-finite values.
Results may differ from the reference program's by a relative error of at most 0.0056.
Values may be sent and summed in bfloat16 or wider, within the bound.
A program may use at most 192 MiB of HBM per device.

```python
import math
import jax
import jax.numpy as jnp
from jax import lax

D = 4096
HEADS = 16
HD = 128
BLOCK = 64
MAXR = 3
G = 2
R = 3
HQ = 2048
BPD = 12
NB = 384
TOKENS = 24576
REQ = 36


def paired_draw(key):
    base_key = jax.random.fold_in(key, 7)
    key_query, key_keys, key_values = jax.random.split(base_key, 3)
    key_signs = jax.random.fold_in(base_key, 91)
    table_shape = (TOKENS, HQ)
    row_ids = jnp.arange(TOKENS)
    ramp = 3.0 * (row_ids.astype(jnp.float32) + 0.5) / TOKENS - 1.5
    column_signs = jnp.where(jax.random.bernoulli(key_signs, 0.5, (HQ,)), 1.0, -1.0)
    value_noise = jnp.clip(jax.random.normal(key_values, table_shape, jnp.float32), -4.5, 4.5)
    value_table = jnp.clip(value_noise + ramp[:, None] * column_signs[None, :], -6.0, 6.0)
    query_table = jnp.clip(jax.random.normal(key_query, table_shape, jnp.float32), -6.0, 6.0)
    key_table = jnp.clip(jax.random.normal(key_keys, table_shape, jnp.float32), -6.0, 6.0)
    return (query_table, key_table, value_table)


def draw_queries(key, part):
    query_table, key_table, value_table = paired_draw(key)
    return query_table.astype(jnp.bfloat16)


def draw_keyvals(key, part):
    query_table, key_table, value_table = paired_draw(key)
    return jnp.stack([key_table, value_table], axis=1).astype(jnp.bfloat16)


def draw_residual(key, part):
    key_main = jax.random.fold_in(jax.random.fold_in(key, 31), 0)
    column_scale = 0.03 * jnp.power(10.0, jnp.arange(D, dtype=jnp.float32) / (D - 1))
    table = jnp.clip(jax.random.normal(key_main, (TOKENS, D), jnp.float32), -6.0, 6.0) * column_scale[None, :]
    return jnp.clip(table, -6.0, 6.0).astype(jnp.bfloat16)


def draw_window_reach(key, part):
    key_reach, key_first, key_second = jax.random.split(jax.random.fold_in(key, 41), 3)
    reach = jax.random.randint(key_reach, (HEADS,), 1, MAXR + 1)
    first = jax.random.randint(key_first, (), 0, HEADS)
    second = (first + 1 + jax.random.randint(key_second, (), 0, HEADS - 1)) % HEADS
    reach = reach.at[first].set(MAXR).at[second].set(1)
    return reach.astype(jnp.int32)


def draw_global_blocks(key, part):
    key_rest, key_order = jax.random.split(jax.random.fold_in(key, 21), 2)
    others = jax.random.permutation(key_rest, NB - 1)[:G - 1]
    chosen = jnp.concatenate([jnp.full((1,), NB - 1, jnp.int32), others.astype(jnp.int32)])
    return jax.random.permutation(key_order, chosen).astype(jnp.int32)


def draw_random_blocks(key, part):
    device_count = NB // BPD
    positions = jnp.arange(REQ)
    order_keys = jax.random.split(jax.random.fold_in(key, 11), device_count)

    def owner_order(subkey):
        return jax.random.permutation(subkey, device_count)
    orders = jax.vmap(owner_order)(order_keys)
    picks = jnp.where(positions == 0, 0, (positions - 1) % device_count)
    owners = orders[:, picks]
    shuffle_keys = jax.random.split(jax.random.fold_in(key, 12), device_count)

    def entry_order(subkey):
        return jax.random.permutation(subkey, REQ)
    shuffles = jax.vmap(entry_order)(shuffle_keys)
    owners = jnp.take_along_axis(owners, shuffles, axis=1)
    local_ids = jax.random.randint(jax.random.fold_in(key, 13), (device_count, REQ), 0, BPD)
    return (owners * BPD + local_ids).reshape(NB, R).astype(jnp.int32)


def shard_levels(stream_key, extent, pieces, low, high):
    def one(position, shards_of):
        steps = jax.random.uniform(jax.random.fold_in(jax.random.fold_in(stream_key, 6), position), (shards_of,), jnp.float32, low / len(pieces), high / len(pieces))
        return jnp.repeat(jnp.exp(steps), extent[position] // shards_of).reshape((-1,) + (1,) * (len(extent) - position - 1))

    factor_of = one(*pieces[0])
    for cut in pieces[1:]:
        factor_of = factor_of * one(*cut)
    return factor_of


def noise(rng, extent, deviation, limit, cuts=(), kind=jnp.bfloat16):
    values = jax.random.normal(rng, extent, jnp.float32) * deviation
    if len(cuts) > 0:
        values = shard_levels(rng, extent, cuts, -0.22, 0.18) * values
    return jnp.clip(values, min=-limit, max=limit).astype(kind)


def setup_inputs(seed: int = 0) -> dict:
    key_of = jax.random.split(jax.random.key(seed), 11)
    return {
        "queries": draw_queries(jax.random.fold_in(key_of[10], 71), 0),
        "keyvals": draw_keyvals(jax.random.fold_in(key_of[10], 71), 0),
        "residual": draw_residual(jax.random.fold_in(key_of[10], 71), 0),
        "out_weight": noise(key_of[3], (HQ, D), HQ ** -0.5, 0.125, ((0, 4),)),
        "norm_gain": jnp.clip(1.0 + 0.1 * jax.random.normal(key_of[4], (D,), jnp.float32), 0.5, 1.5).astype(jnp.bfloat16),
        "norm_bias": noise(key_of[5], (D,), 0.5, 3.0, ((0, 4),)),
        "cross_weight": noise(key_of[6], (D, 2, HQ), D ** -0.5, 0.09375, ((2, 4),)),
        "window_reach": draw_window_reach(jax.random.fold_in(key_of[10], 71), 0),
        "global_blocks": draw_global_blocks(jax.random.fold_in(key_of[10], 71), 0),
        "random_blocks": draw_random_blocks(jax.random.fold_in(key_of[10], 71), 0),
    }


norm_eps = 1e-05

def reference(queries, keyvals, residual, out_weight, norm_gain, norm_bias, cross_weight, window_reach, global_blocks, random_blocks):
    score_scale = 1.0 / math.sqrt(HD)
    block_ids = jnp.arange(NB, dtype=jnp.int32)
    offsets = jnp.arange(2 * MAXR + 1, dtype=jnp.int32) - MAXR
    window_ids = block_ids[:, None] + offsets[None, :]
    inside = (window_ids >= 0) & (window_ids < NB)
    window_ids = jnp.clip(window_ids, 0, NB - 1).astype(jnp.int32)
    listed = jnp.concatenate([window_ids, jnp.broadcast_to(global_blocks[None, :], (NB, G)).astype(jnp.int32), random_blocks.astype(jnp.int32)], axis=1)
    key_table = keyvals[:, 0, :]
    value_table = keyvals[:, 1, :]

    def one_head(head):
        begin = (head * HD).astype(jnp.int32)
        single_query_head = lax.dynamic_slice_in_dim(queries, begin, HD, 1).astype(jnp.float32).reshape(NB, BLOCK, HD)
        key_head = lax.dynamic_slice_in_dim(key_table, begin, HD, 1).astype(jnp.float32).reshape(NB, BLOCK, HD)
        value_head = lax.dynamic_slice_in_dim(value_table, begin, HD, 1).astype(jnp.float32).reshape(NB, BLOCK, HD)
        reach = window_reach[head]
        usable = jnp.concatenate([inside & (jnp.abs(offsets)[None, :] <= reach), jnp.ones((NB, G + R), dtype=bool)], axis=1)
        gathered_keys = key_head[listed]
        gathered_values = value_head[listed]
        logit_scores = jnp.einsum('cro,ceso->cres', single_query_head, gathered_keys) * score_scale
        logit_scores = jnp.where(usable[:, None, :, None], logit_scores, -jnp.inf)
        peak = lax.optimization_barrier(jnp.max(logit_scores, axis=(2, 3), keepdims=True))
        weights = jnp.exp(logit_scores - peak)
        softmax_totals = lax.optimization_barrier(jnp.sum(weights, axis=(2, 3)))
        rounded_output = lax.optimization_barrier(weights.astype(jnp.bfloat16)).astype(jnp.float32)
        sparse_output = jnp.einsum('ivze,izep->ivp', rounded_output, gathered_values) / softmax_totals[..., None]
        key_flat = key_head.reshape(TOKENS, HD)
        value_flat = value_head.reshape(TOKENS, HD)
        for index_g in range(G):
            block_id = global_blocks[index_g]
            full_scores = jnp.dot(single_query_head[block_id], key_flat.T, precision=lax.Precision.HIGHEST) * score_scale
            full_weights = jnp.exp(full_scores - lax.optimization_barrier(jnp.max(full_scores, axis=1, keepdims=True)))
            full_total = lax.optimization_barrier(jnp.sum(full_weights, axis=1, keepdims=True))
            full_rounded = lax.optimization_barrier(full_weights.astype(jnp.bfloat16)).astype(jnp.float32)
            full_out = jnp.dot(full_rounded, value_flat, precision=lax.Precision.HIGHEST) / full_total
            sparse_output = sparse_output.at[block_id].set(full_out)
        return sparse_output.reshape(TOKENS, HD)
    head_outs = lax.map(one_head, jnp.arange(HEADS, dtype=jnp.int32))
    attended = jnp.transpose(head_outs, (1, 0, 2)).reshape(TOKENS, HQ).astype(jnp.bfloat16)
    mixed = residual.astype(jnp.float32) + jnp.dot(attended, out_weight, preferred_element_type=jnp.float32)
    row_mean = lax.optimization_barrier(jnp.mean(mixed, axis=1, keepdims=True))
    centered = mixed - row_mean
    variance = lax.optimization_barrier(jnp.mean(centered * centered, axis=1, keepdims=True))
    encoded = (centered * lax.rsqrt(variance + norm_eps) * norm_gain.astype(jnp.float32) + norm_bias.astype(jnp.float32)).astype(jnp.bfloat16)
    projected = jnp.dot(encoded, cross_weight.reshape(D, 2 * HQ), preferred_element_type=jnp.float32).astype(jnp.bfloat16).reshape(TOKENS, 2, HQ)
    cross_kv = jnp.roll(projected, TOKENS // 2, axis=0)
    return (encoded, cross_kv)
```

```python
import functools
import math

import jax
import jax.numpy as jnp
from jax import lax
from jax.experimental import pallas as pl
from jax.experimental.pallas import tpu as pltpu
from jax.sharding import PartitionSpec as P

D = 4096
BLOCK = 64
MAXR = 3
G = 2
R = 3
SPAN = 2 * MAXR + 1
MESH = pl.DeviceIdType.MESH
VMEM = pltpu.VMEM
SMEM = pltpu.SMEM

norm_eps = 1e-05


def greet(axis, count):
    me = lax.axis_index(axis)
    barrier = pltpu.get_barrier_semaphore()

    def signal(k, carry):
        pl.semaphore_signal(
            barrier, inc=1, device_id={axis: lax.rem(me + k, count)}, device_id_type=MESH
        )
        return carry

    lax.fori_loop(1, count, signal, 0)
    pl.semaphore_wait(barrier, count - 1)


def edges_kernel(
    count,
    place_ref,
    kv_ref,
    q_ref,
    ext_ref,
    gkv_ref,
    gq_ref,
    cand,
    got,
    full,
    halo_send,
    halo_recv,
    send1,
    recv1,
    send2,
    recv2,
):
    me = lax.axis_index("ctx")
    blocks = kv_ref.shape[0]
    wide = kv_ref.shape[2]
    half = q_ref.shape[2]
    part = (wide + half) // 4
    greet("ctx", count)
    after = lax.rem(me + 1, count)
    before = lax.rem(me + count - 1, count)
    to_after = pltpu.make_async_remote_copy(
        src_ref=kv_ref.at[pl.ds(blocks - MAXR, MAXR)],
        dst_ref=ext_ref.at[pl.ds(0, MAXR)],
        send_sem=halo_send.at[0],
        recv_sem=halo_recv.at[0],
        device_id={"ctx": after},
        device_id_type=MESH,
    )
    to_before = pltpu.make_async_remote_copy(
        src_ref=kv_ref.at[pl.ds(0, MAXR)],
        dst_ref=ext_ref.at[pl.ds(blocks + MAXR, MAXR)],
        send_sem=halo_send.at[1],
        recv_sem=halo_recv.at[1],
        device_id={"ctx": before},
        device_id_type=MESH,
    )
    for g in range(G):
        local = place_ref[G + g]
        row = jnp.concatenate([kv_ref[local], q_ref[local]], axis=1)
        for r in range(4):
            for c in range(4):
                cand[(g * 4 + r) * 4 + c] = row[r * 16 : r * 16 + 16, c * part : (c + 1) * part]

    def first(k):
        to = lax.rem(me + k, count)
        return pltpu.make_async_remote_copy(
            src_ref=cand.at[to],
            dst_ref=got.at[me],
            send_sem=send1.at[k],
            recv_sem=recv1.at[k],
            device_id={"ctx": to},
            device_id_type=MESH,
        )

    def second(k):
        to = lax.rem(me + k, count)
        return pltpu.make_async_remote_copy(
            src_ref=full.at[me],
            dst_ref=full.at[me],
            send_sem=send2.at[k],
            recv_sem=recv2.at[k],
            device_id={"ctx": to},
            device_id_type=MESH,
        )

    def each(action):
        def body(k, carry):
            action(k)
            return carry

        lax.fori_loop(1, count, body, 0)

    each(lambda k: first(k).start())
    to_after.start()
    to_before.start()
    got[me] = cand[me]
    ext_ref[pl.ds(MAXR, blocks)] = kv_ref[...]
    each(lambda k: first(k).wait())
    full[me] = got[place_ref[me // (count // G)]]
    each(lambda k: second(k).start())
    each(lambda k: second(k).wait())
    for g in range(G):
        for r in range(4):
            row = jnp.concatenate([full[(g * 4 + r) * 4 + c] for c in range(4)], axis=1)
            gkv_ref[g, r * 16 : r * 16 + 16, :] = row[:, :wide]
            gq_ref[g, r * 16 : r * 16 + 16, :] = row[:, wide:]
    to_after.wait()
    to_before.wait()


def edges(place, kv, q, count):
    blocks, rows, wide = kv.shape
    half = q.shape[2]
    part = (wide + half) // 4
    return pl.pallas_call(
        functools.partial(edges_kernel, count),
        name="edges",
        out_shape=(
            jax.ShapeDtypeStruct((blocks + 2 * MAXR, rows, wide), kv.dtype),
            jax.ShapeDtypeStruct((G, rows, wide), kv.dtype),
            jax.ShapeDtypeStruct((G, rows, half), kv.dtype),
        ),
        in_specs=[
            pl.BlockSpec(memory_space=SMEM),
            pl.BlockSpec(memory_space=VMEM),
            pl.BlockSpec(memory_space=VMEM),
        ],
        out_specs=(pl.BlockSpec(memory_space=VMEM),) * 3,
        scratch_shapes=[
            VMEM((count, 16, part), kv.dtype),
            VMEM((count, 16, part), kv.dtype),
            VMEM((count, 16, part), kv.dtype),
            pltpu.SemaphoreType.DMA((2,)),
            pltpu.SemaphoreType.DMA((2,)),
            pltpu.SemaphoreType.DMA((count,)),
            pltpu.SemaphoreType.DMA((count,)),
            pltpu.SemaphoreType.DMA((count,)),
            pltpu.SemaphoreType.DMA((count,)),
        ],
        compiler_params=pltpu.CompilerParams(
            collective_id=0, has_side_effects=True, vmem_limit_bytes=48 * 2**20
        ),
    )(place, kv, q)


def far_kernel(scale, head_count, gq_ref, kv_ref, out_ref):
    blocks, rows, wide = kv_ref.shape
    size = wide // (2 * head_count)
    for h in range(head_count):
        lanes = slice(h * size, (h + 1) * size)
        q = gq_ref[:, :, lanes].reshape(G * rows, size)
        k = kv_ref[:, :, lanes].reshape(blocks * rows, size)
        v = kv_ref[:, :, wide // 2 + h * size : wide // 2 + (h + 1) * size].reshape(
            blocks * rows, size
        )
        s = (
            lax.dot_general(q, k, (((1,), (1,)), ((), ())), preferred_element_type=jnp.float32)
            * scale
        )
        peak = jnp.max(s, axis=1, keepdims=True)
        p = jnp.exp(s - peak)
        total = jnp.sum(p, axis=1, keepdims=True)
        acc = jnp.dot(p.astype(jnp.bfloat16), v, preferred_element_type=jnp.float32)
        peak = jnp.broadcast_to(peak, acc.shape)
        total = jnp.broadcast_to(total, acc.shape)
        for r in range(8):
            cut = slice(r * 16, r * 16 + 16)
            out_ref[h * 8 + r, 0:16, :] = acc[cut]
            out_ref[h * 8 + r, 16:32, :] = peak[cut]
            out_ref[h * 8 + r, 32:48, :] = total[cut]


def far_partials(gq, kv, scale, head_count, count):
    size = gq.shape[2] // head_count
    return pl.pallas_call(
        functools.partial(far_kernel, scale, head_count),
        name="far_partials",
        out_shape=jax.ShapeDtypeStruct((count, 48, size), jnp.float32),
        in_specs=[pl.BlockSpec(memory_space=VMEM)] * 2,
        out_specs=pl.BlockSpec(memory_space=VMEM),
        compiler_params=pltpu.CompilerParams(vmem_limit_bytes=48 * 2**20),
    )(gq, kv)


def exchange_kernel(
    count,
    slots,
    source_ref,
    kv_ref,
    part_ref,
    random_ref,
    far_ref,
    stage,
    got,
    bulk_send,
    bulk_recv,
    send1,
    recv1,
    send2,
    recv2,
    own_sem,
):
    me = lax.axis_index("ctx")
    greet("ctx", count)

    def first(k):
        to = lax.rem(me + k, count)
        return pltpu.make_async_remote_copy(
            src_ref=part_ref.at[to],
            dst_ref=got.at[me],
            send_sem=send1.at[k],
            recv_sem=recv1.at[k],
            device_id={"ctx": to},
            device_id_type=MESH,
        )

    def second(k):
        to = lax.rem(me + k, count)
        return pltpu.make_async_remote_copy(
            src_ref=far_ref.at[me],
            dst_ref=far_ref.at[me],
            send_sem=send2.at[k],
            recv_sem=recv2.at[k],
            device_id={"ctx": to},
            device_id_type=MESH,
        )

    def bulk(k):
        to = lax.rem(me + k, count)
        return pltpu.make_async_remote_copy(
            src_ref=stage.at[pl.ds(to * slots, slots)],
            dst_ref=random_ref.at[pl.ds(me * slots, slots)],
            send_sem=bulk_send.at[k],
            recv_sem=bulk_recv.at[k],
            device_id={"ctx": to},
            device_id_type=MESH,
        )

    def each(action):
        def body(k, carry):
            action(k)
            return carry

        lax.fori_loop(1, count, body, 0)

    each(lambda k: first(k).start())
    got[me] = part_ref[me]

    def place(i, carry):
        stage[i] = kv_ref[source_ref[i]]
        return carry

    lax.fori_loop(0, count * slots, place, 0)
    each(lambda k: bulk(k).start())
    own = pltpu.make_async_copy(
        stage.at[pl.ds(me * slots, slots)], random_ref.at[pl.ds(me * slots, slots)], own_sem
    )
    own.start()
    each(lambda k: first(k).wait())

    def top(i, so_far):
        return jnp.maximum(so_far, got[i, 16:32, :])

    peak = lax.fori_loop(1, count, top, got[0, 16:32, :])

    def add(i, so_far):
        acc, total = so_far
        factor = jnp.exp(got[i, 16:32, :] - peak)
        return acc + got[i, 0:16, :] * factor, total + got[i, 32:48, :] * factor

    zero = jnp.zeros_like(peak)
    acc, total = lax.fori_loop(0, count, add, (zero, zero))
    far_ref[me] = (acc / total).astype(far_ref.dtype)
    each(lambda k: second(k).start())
    own.wait()
    each(lambda k: bulk(k).wait())
    each(lambda k: second(k).wait())


def exchange(source, kv, partials, count, slots):
    blocks, rows, wide = kv.shape
    size = partials.shape[2]
    dma = pltpu.SemaphoreType.DMA((count,))
    return pl.pallas_call(
        functools.partial(exchange_kernel, count, slots),
        name="exchange",
        out_shape=(
            jax.ShapeDtypeStruct((count * slots, rows, wide), kv.dtype),
            jax.ShapeDtypeStruct((count, 16, size), kv.dtype),
        ),
        in_specs=[
            pl.BlockSpec(memory_space=SMEM),
            pl.BlockSpec(memory_space=VMEM),
            pl.BlockSpec(memory_space=VMEM),
        ],
        out_specs=(pl.BlockSpec(memory_space=pl.ANY), pl.BlockSpec(memory_space=VMEM)),
        scratch_shapes=[
            VMEM((count * slots, rows, wide), kv.dtype),
            VMEM((count, 48, size), jnp.float32),
            dma,
            dma,
            dma,
            dma,
            dma,
            dma,
            pltpu.SemaphoreType.DMA,
        ],
        compiler_params=pltpu.CompilerParams(
            collective_id=1, has_side_effects=True, vmem_limit_bytes=56 * 2**20
        ),
    )(source, kv, partials)


def attention_kernel(
    scale,
    head_count,
    all_blocks,
    index_ref,
    info_ref,
    q_ref,
    ext_ref,
    gkv_ref,
    far_ref,
    rand0,
    rand1,
    rand2,
    out_ref,
):
    b = pl.program_id(0)
    rows = q_ref.shape[1]
    wide = gkv_ref.shape[2]
    half = wide // 2
    size = half // head_count
    me = lax.axis_index("ctx")
    block = me * pl.num_programs(0) + b
    replaced = info_ref[head_count + b]
    near = SPAN * rows
    spot = lax.broadcasted_iota(jnp.int32, (rows, near), 1) // rows - MAXR
    inside = (spot + block >= 0) & (spot + block < all_blocks)
    for h in range(head_count):
        kl = slice(h * size, (h + 1) * size)
        vl = slice(half + h * size, half + (h + 1) * size)
        reach = info_ref[h]
        q = q_ref[0, :, kl]

        def listed(lanes):
            return jnp.concatenate(
                [
                    gkv_ref[0, :, lanes],
                    gkv_ref[1, :, lanes],
                    rand0[0, :, lanes],
                    rand1[0, :, lanes],
                    rand2[0, :, lanes],
                ],
                axis=0,
            )

        def score(keys):
            return (
                lax.dot_general(
                    q, keys, (((1,), (1,)), ((), ())), preferred_element_type=jnp.float32
                )
                * scale
            )

        window_k = ext_ref[pl.ds(b, SPAN), :, kl].reshape(near, size)
        window_v = ext_ref[pl.ds(b, SPAN), :, vl].reshape(near, size)
        s1 = jnp.where(inside & (jnp.abs(spot) <= reach), score(window_k), -jnp.inf)
        s2 = score(listed(kl))
        peak = jnp.maximum(
            jnp.max(s1, axis=1, keepdims=True), jnp.max(s2, axis=1, keepdims=True)
        )
        p1 = jnp.exp(s1 - peak)
        p2 = jnp.exp(s2 - peak)
        total = jnp.sum(p1, axis=1, keepdims=True) + jnp.sum(p2, axis=1, keepdims=True)
        acc = jnp.dot(p1.astype(jnp.bfloat16), window_v, preferred_element_type=jnp.float32)
        acc = acc + jnp.dot(
            p2.astype(jnp.bfloat16), listed(vl), preferred_element_type=jnp.float32
        )
        out_ref[0, :, kl] = (acc / total).astype(out_ref.dtype)

    for g in range(G):

        @pl.when(replaced == g)
        def _():
            for h in range(head_count):
                for r in range(4):
                    out_ref[0, r * 16 : r * 16 + 16, h * size : (h + 1) * size] = far_ref[
                        h * 8 + g * 4 + r
                    ]


def attention(index, info, q, ext, gkv, far, random, scale, head_count, all_blocks):
    blocks, rows, half = q.shape
    wide = 2 * half

    def whole(x):
        return pl.BlockSpec(x.shape, lambda b, *_: (0,) * x.ndim)

    def pick(r):
        return pl.BlockSpec((1, rows, wide), lambda b, index, info: (index[b * R + r], 0, 0))

    one = pl.BlockSpec((1, rows, half), lambda b, *_: (b, 0, 0))
    return pl.pallas_call(
        functools.partial(attention_kernel, scale, head_count, all_blocks),
        name="attention",
        grid_spec=pltpu.PrefetchScalarGridSpec(
            num_scalar_prefetch=2,
            grid=(blocks,),
            in_specs=[one, whole(ext), whole(gkv), whole(far), pick(0), pick(1), pick(2)],
            out_specs=one,
        ),
        out_shape=jax.ShapeDtypeStruct(q.shape, q.dtype),
        compiler_params=pltpu.CompilerParams(vmem_limit_bytes=48 * 2**20),
    )(index, info, q, ext, gkv, far, random, random, random)


def shards(
    queries,
    keyvals,
    residual,
    out_weight,
    norm_gain,
    norm_bias,
    cross_weight,
    window_reach,
    global_blocks,
    random_blocks,
):
    tok_rows, head_cols = queries.shape
    head_count = window_reach.shape[0]
    head_size = head_cols // head_count
    ctx_count = lax.axis_size("ctx")
    me = lax.axis_index("ctx")
    block_count = tok_rows // BLOCK
    all_blocks = block_count * ctx_count
    scale = 1.0 / math.sqrt(head_size)
    q = queries.reshape(block_count, BLOCK, head_cols)
    kv = keyvals.reshape(block_count, BLOCK, 2 * head_cols)

    req_count = block_count * R
    slots = 1 + (req_count + ctx_count - 2) // ctx_count
    requests = random_blocks.reshape(ctx_count, req_count)
    owners = requests // block_count
    local_ids = requests % block_count
    positions = jnp.arange(req_count, dtype=jnp.int32)
    earlier = positions[None, :] < positions[:, None]
    ranks = jnp.sum(
        ((owners[:, :, None] == owners[:, None, :]) & earlier[None, :, :]).astype(jnp.int32), axis=2
    )
    slot_ids = jnp.arange(slots, dtype=jnp.int32)
    matches = (owners[:, None, :] == me) & (ranks[:, None, :] == slot_ids[None, :, None])
    source_ids = jnp.sum(jnp.where(matches, local_ids[:, None, :], 0), axis=2).reshape(-1)
    my_index = lax.dynamic_index_in_dim(owners * slots + ranks, me, 0, keepdims=False)
    place = jnp.concatenate([global_blocks // block_count, global_blocks % block_count])
    own_ids = me * block_count + jnp.arange(block_count, dtype=jnp.int32)
    replaced = jnp.where(
        own_ids == global_blocks[0], 0, jnp.where(own_ids == global_blocks[1], 1, -1)
    )
    info = jnp.concatenate([window_reach, replaced])

    ext, gkv, gq = edges(place, kv, q, ctx_count)
    partials = far_partials(gq, kv, scale, head_count, ctx_count)
    random, far = exchange(source_ids, kv, partials, ctx_count, slots)
    attended = attention(my_index, info, q, ext, gkv, far, random, scale, head_count, all_blocks)
    attended = attended.reshape(tok_rows, head_cols)
    summed = lax.psum_scatter(
        lax.dot_general(
            out_weight, attended, (((0,), (1,)), ((), ())), preferred_element_type=jnp.float32
        ),
        "tp",
        scatter_dimension=0,
        tiled=True,
    )
    mixed_part = summed.T
    mixed = residual.astype(jnp.float32) + mixed_part
    row_sum = jnp.sum(mixed, axis=1)
    row_square = jnp.sum(mixed * mixed, axis=1)
    total_sum, total_square = lax.psum((row_sum, row_square), "tp")
    row_mean = total_sum / D
    variance = total_square / D - row_mean * row_mean
    normalized = (mixed - row_mean[:, None]) * lax.rsqrt(variance[:, None] + norm_eps)
    encoded = (normalized * norm_gain.astype(jnp.float32) + norm_bias.astype(jnp.float32)).astype(
        jnp.bfloat16
    )
    flat_weight = cross_weight.reshape(D, 2 * head_cols)
    half_way = ctx_count // 2
    arrived = passed_along(encoded, "ctx", half_way)
    cross_kv = jnp.dot(
        lax.all_gather(arrived, "tp", axis=1, tiled=True),
        flat_weight,
        preferred_element_type=jnp.float32,
    ).astype(jnp.bfloat16)
    return (encoded, cross_kv.reshape(tok_rows, 2, head_cols))


def passed_along(value, axis, steps):
    count = lax.axis_size(axis)
    pairs = [(source, (source + steps) % count) for source in range(count)]
    return lax.ppermute(value, axis, pairs)


def solution(mesh):
    placed = (
        P("ctx", "tp"),
        P("ctx", None, "tp"),
        P("ctx", "tp"),
        P("tp", None),
        P("tp"),
        P("tp"),
        P(None, None, "tp"),
        P("tp"),
        P(),
        P(),
    )
    return jax.shard_map(
        shards,
        mesh=mesh,
        in_specs=placed,
        out_specs=(P("ctx", "tp"), P("ctx", None, "tp")),
        check_vma=False,
    )
```

```python
import functools
import math

import jax
import jax.numpy as jnp
from jax import lax
from jax.experimental import pallas as pl
from jax.experimental.pallas import tpu as pltpu
from jax.sharding import PartitionSpec as P

D = 4096
BLOCK = 64
MAXR = 3
G = 2
R = 3
SPAN = 2 * MAXR + 1
MESH = pl.DeviceIdType.MESH
VMEM = pltpu.VMEM
SMEM = pltpu.SMEM

norm_eps = 1e-05


def greet(axis, count):
    me = lax.axis_index(axis)
    barrier = pltpu.get_barrier_semaphore()

    def signal(k, carry):
        pl.semaphore_signal(
            barrier, inc=1, device_id={axis: lax.rem(me + k, count)}, device_id_type=MESH
        )
        return carry

    lax.fori_loop(1, count, signal, 0)
    pl.semaphore_wait(barrier, count - 1)


def edges_kernel(
    count,
    place_ref,
    kv_ref,
    q_ref,
    ext_ref,
    gkv_ref,
    gq_ref,
    cand,
    got,
    full,
    halo_send,
    halo_recv,
    send1,
    recv1,
    send2,
    recv2,
):
    me = lax.axis_index("ctx")
    blocks = kv_ref.shape[0]
    wide = kv_ref.shape[2]
    half = q_ref.shape[2]
    part = (wide + half) // 4
    greet("ctx", count)
    after = lax.rem(me + 1, count)
    before = lax.rem(me + count - 1, count)
    to_after = pltpu.make_async_remote_copy(
        src_ref=kv_ref.at[pl.ds(blocks - MAXR, MAXR)],
        dst_ref=ext_ref.at[pl.ds(0, MAXR)],
        send_sem=halo_send.at[0],
        recv_sem=halo_recv.at[0],
        device_id={"ctx": after},
        device_id_type=MESH,
    )
    to_before = pltpu.make_async_remote_copy(
        src_ref=kv_ref.at[pl.ds(0, MAXR)],
        dst_ref=ext_ref.at[pl.ds(blocks + MAXR, MAXR)],
        send_sem=halo_send.at[1],
        recv_sem=halo_recv.at[1],
        device_id={"ctx": before},
        device_id_type=MESH,
    )
    for g in range(G):
        local = place_ref[G + g]
        row = jnp.concatenate([kv_ref[local], q_ref[local]], axis=1)
        for r in range(4):
            for c in range(4):
                cand[(g * 4 + r) * 4 + c] = row[r * 16 : r * 16 + 16, c * part : (c + 1) * part]

    def first(k):
        to = lax.rem(me + k, count)
        return pltpu.make_async_remote_copy(
            src_ref=cand.at[to],
            dst_ref=got.at[me],
            send_sem=send1.at[k],
            recv_sem=recv1.at[k],
            device_id={"ctx": to},
            device_id_type=MESH,
        )

    def second(k):
        to = lax.rem(me + k, count)
        return pltpu.make_async_remote_copy(
            src_ref=full.at[me],
            dst_ref=full.at[me],
            send_sem=send2.at[k],
            recv_sem=recv2.at[k],
            device_id={"ctx": to},
            device_id_type=MESH,
        )

    def each(action):
        def body(k, carry):
            action(k)
            return carry

        lax.fori_loop(1, count, body, 0)

    each(lambda k: first(k).start())
    to_after.start()
    to_before.start()
    got[me] = cand[me]
    ext_ref[pl.ds(MAXR, blocks)] = kv_ref[...]
    each(lambda k: first(k).wait())
    full[me] = got[place_ref[me // (count // G)]]
    each(lambda k: second(k).start())
    each(lambda k: second(k).wait())
    for g in range(G):
        for r in range(4):
            row = jnp.concatenate([full[(g * 4 + r) * 4 + c] for c in range(4)], axis=1)
            gkv_ref[g, r * 16 : r * 16 + 16, :] = row[:, :wide]
            gq_ref[g, r * 16 : r * 16 + 16, :] = row[:, wide:]
    to_after.wait()
    to_before.wait()


def edges(place, kv, q, count):
    blocks, rows, wide = kv.shape
    half = q.shape[2]
    part = (wide + half) // 4
    return pl.pallas_call(
        functools.partial(edges_kernel, count),
        name="edges",
        out_shape=(
            jax.ShapeDtypeStruct((blocks + 2 * MAXR, rows, wide), kv.dtype),
            jax.ShapeDtypeStruct((G, rows, wide), kv.dtype),
            jax.ShapeDtypeStruct((G, rows, half), kv.dtype),
        ),
        in_specs=[
            pl.BlockSpec(memory_space=SMEM),
            pl.BlockSpec(memory_space=VMEM),
            pl.BlockSpec(memory_space=VMEM),
        ],
        out_specs=(pl.BlockSpec(memory_space=VMEM),) * 3,
        scratch_shapes=[
            VMEM((count, 16, part), kv.dtype),
            VMEM((count, 16, part), kv.dtype),
            VMEM((count, 16, part), kv.dtype),
            pltpu.SemaphoreType.DMA((2,)),
            pltpu.SemaphoreType.DMA((2,)),
            pltpu.SemaphoreType.DMA((count,)),
            pltpu.SemaphoreType.DMA((count,)),
            pltpu.SemaphoreType.DMA((count,)),
            pltpu.SemaphoreType.DMA((count,)),
        ],
        compiler_params=pltpu.CompilerParams(
            collective_id=0, has_side_effects=True, vmem_limit_bytes=48 * 2**20
        ),
    )(place, kv, q)


def far_kernel(scale, head_count, gq_ref, kv_ref, out_ref):
    blocks, rows, wide = kv_ref.shape
    size = wide // (2 * head_count)
    for h in range(head_count):
        lanes = slice(h * size, (h + 1) * size)
        q = gq_ref[:, :, lanes].reshape(G * rows, size)
        k = kv_ref[:, :, lanes].reshape(blocks * rows, size)
        v = kv_ref[:, :, wide // 2 + h * size : wide // 2 + (h + 1) * size].reshape(
            blocks * rows, size
        )
        s = (
            lax.dot_general(q, k, (((1,), (1,)), ((), ())), preferred_element_type=jnp.float32)
            * scale
        )
        peak = jnp.max(s, axis=1, keepdims=True)
        p = jnp.exp(s - peak)
        total = jnp.sum(p, axis=1, keepdims=True)
        acc = jnp.dot(p.astype(jnp.bfloat16), v, preferred_element_type=jnp.float32)
        peak = jnp.broadcast_to(peak, acc.shape)
        total = jnp.broadcast_to(total, acc.shape)
        for r in range(8):
            cut = slice(r * 16, r * 16 + 16)
            out_ref[h * 8 + r, 0:16, :] = acc[cut]
            out_ref[h * 8 + r, 16:32, :] = peak[cut]
            out_ref[h * 8 + r, 32:48, :] = total[cut]


def far_partials(gq, kv, scale, head_count, count):
    size = gq.shape[2] // head_count
    return pl.pallas_call(
        functools.partial(far_kernel, scale, head_count),
        name="far_partials",
        out_shape=jax.ShapeDtypeStruct((count, 48, size), jnp.float32),
        in_specs=[pl.BlockSpec(memory_space=VMEM)] * 2,
        out_specs=pl.BlockSpec(memory_space=VMEM),
        compiler_params=pltpu.CompilerParams(vmem_limit_bytes=48 * 2**20),
    )(gq, kv)


def exchange_kernel(
    count,
    slots,
    source_ref,
    kv_ref,
    part_ref,
    random_ref,
    far_ref,
    stage,
    got,
    bulk_send,
    bulk_recv,
    send1,
    recv1,
    send2,
    recv2,
    own_sem,
):
    me = lax.axis_index("ctx")
    greet("ctx", count)

    def first(k):
        to = lax.rem(me + k, count)
        return pltpu.make_async_remote_copy(
            src_ref=part_ref.at[to],
            dst_ref=got.at[me],
            send_sem=send1.at[k],
            recv_sem=recv1.at[k],
            device_id={"ctx": to},
            device_id_type=MESH,
        )

    def second(k):
        to = lax.rem(me + k, count)
        return pltpu.make_async_remote_copy(
            src_ref=far_ref.at[me],
            dst_ref=far_ref.at[me],
            send_sem=send2.at[k],
            recv_sem=recv2.at[k],
            device_id={"ctx": to},
            device_id_type=MESH,
        )

    def bulk(k):
        to = lax.rem(me + k, count)
        return pltpu.make_async_remote_copy(
            src_ref=stage.at[pl.ds(to * slots, slots)],
            dst_ref=random_ref.at[pl.ds(me * slots, slots)],
            send_sem=bulk_send.at[k],
            recv_sem=bulk_recv.at[k],
            device_id={"ctx": to},
            device_id_type=MESH,
        )

    def each(action):
        def body(k, carry):
            action(k)
            return carry

        lax.fori_loop(1, count, body, 0)

    each(lambda k: first(k).start())
    got[me] = part_ref[me]

    def place(i, carry):
        stage[i] = kv_ref[source_ref[i]]
        return carry

    lax.fori_loop(0, count * slots, place, 0)
    each(lambda k: bulk(k).start())
    own = pltpu.make_async_copy(
        stage.at[pl.ds(me * slots, slots)], random_ref.at[pl.ds(me * slots, slots)], own_sem
    )
    own.start()
    each(lambda k: first(k).wait())

    def top(i, so_far):
        return jnp.maximum(so_far, got[i, 16:32, :])

    peak = lax.fori_loop(1, count, top, got[0, 16:32, :])

    def add(i, so_far):
        acc, total = so_far
        factor = jnp.exp(got[i, 16:32, :] - peak)
        return acc + got[i, 0:16, :] * factor, total + got[i, 32:48, :] * factor

    zero = jnp.zeros_like(peak)
    acc, total = lax.fori_loop(0, count, add, (zero, zero))
    far_ref[me] = (acc / total).astype(far_ref.dtype)
    each(lambda k: second(k).start())
    own.wait()
    each(lambda k: bulk(k).wait())
    each(lambda k: second(k).wait())


def exchange(source, kv, partials, count, slots):
    blocks, rows, wide = kv.shape
    size = partials.shape[2]
    dma = pltpu.SemaphoreType.DMA((count,))
    return pl.pallas_call(
        functools.partial(exchange_kernel, count, slots),
        name="exchange",
        out_shape=(
            jax.ShapeDtypeStruct((count * slots, rows, wide), kv.dtype),
            jax.ShapeDtypeStruct((count, 16, size), kv.dtype),
        ),
        in_specs=[
            pl.BlockSpec(memory_space=SMEM),
            pl.BlockSpec(memory_space=VMEM),
            pl.BlockSpec(memory_space=VMEM),
        ],
        out_specs=(pl.BlockSpec(memory_space=pl.ANY), pl.BlockSpec(memory_space=VMEM)),
        scratch_shapes=[
            VMEM((count * slots, rows, wide), kv.dtype),
            VMEM((count, 48, size), jnp.float32),
            dma,
            dma,
            dma,
            dma,
            dma,
            dma,
            pltpu.SemaphoreType.DMA,
        ],
        compiler_params=pltpu.CompilerParams(
            collective_id=1, has_side_effects=True, vmem_limit_bytes=56 * 2**20
        ),
    )(source, kv, partials)


def attention_kernel(
    scale,
    head_count,
    all_blocks,
    index_ref,
    info_ref,
    q_ref,
    ext_ref,
    gkv_ref,
    far_ref,
    rand0,
    rand1,
    rand2,
    out_ref,
):
    b = pl.program_id(0)
    rows = q_ref.shape[1]
    wide = gkv_ref.shape[2]
    half = wide // 2
    size = half // head_count
    me = lax.axis_index("ctx")
    block = me * pl.num_programs(0) + b
    replaced = info_ref[head_count + b]
    near = SPAN * rows
    spot = lax.broadcasted_iota(jnp.int32, (rows, near), 1) // rows - MAXR
    inside = (spot + block >= 0) & (spot + block < all_blocks)
    for h in range(head_count):
        kl = slice(h * size, (h + 1) * size)
        vl = slice(half + h * size, half + (h + 1) * size)
        reach = info_ref[h]
        q = q_ref[0, :, kl]

        def listed(lanes):
            return jnp.concatenate(
                [
                    gkv_ref[0, :, lanes],
                    gkv_ref[1, :, lanes],
                    rand0[0, :, lanes],
                    rand1[0, :, lanes],
                    rand2[0, :, lanes],
                ],
                axis=0,
            )

        def score(keys):
            return (
                lax.dot_general(
                    q, keys, (((1,), (1,)), ((), ())), preferred_element_type=jnp.float32
                )
                * scale
            )

        window_k = ext_ref[pl.ds(b, SPAN), :, kl].reshape(near, size)
        window_v = ext_ref[pl.ds(b, SPAN), :, vl].reshape(near, size)
        s1 = jnp.where(inside & (jnp.abs(spot) <= reach), score(window_k), -jnp.inf)
        s2 = score(listed(kl))
        peak = jnp.maximum(
            jnp.max(s1, axis=1, keepdims=True), jnp.max(s2, axis=1, keepdims=True)
        )
        p1 = jnp.exp(s1 - peak)
        p2 = jnp.exp(s2 - peak)
        total = jnp.sum(p1, axis=1, keepdims=True) + jnp.sum(p2, axis=1, keepdims=True)
        acc = jnp.dot(p1.astype(jnp.bfloat16), window_v, preferred_element_type=jnp.float32)
        acc = acc + jnp.dot(
            p2.astype(jnp.bfloat16), listed(vl), preferred_element_type=jnp.float32
        )
        out_ref[0, :, kl] = (acc / total).astype(out_ref.dtype)

    for g in range(G):

        @pl.when(replaced == g)
        def _():
            for h in range(head_count):
                for r in range(4):
                    out_ref[0, r * 16 : r * 16 + 16, h * size : (h + 1) * size] = far_ref[
                        h * 8 + g * 4 + r
                    ]


def attention(index, info, q, ext, gkv, far, random, scale, head_count, all_blocks):
    blocks, rows, half = q.shape
    wide = 2 * half

    def whole(x):
        return pl.BlockSpec(x.shape, lambda b, *_: (0,) * x.ndim)

    def pick(r):
        return pl.BlockSpec((1, rows, wide), lambda b, index, info: (index[b * R + r], 0, 0))

    one = pl.BlockSpec((1, rows, half), lambda b, *_: (b, 0, 0))
    return pl.pallas_call(
        functools.partial(attention_kernel, scale, head_count, all_blocks),
        name="attention",
        grid_spec=pltpu.PrefetchScalarGridSpec(
            num_scalar_prefetch=2,
            grid=(blocks,),
            in_specs=[one, whole(ext), whole(gkv), whole(far), pick(0), pick(1), pick(2)],
            out_specs=one,
        ),
        out_shape=jax.ShapeDtypeStruct(q.shape, q.dtype),
        compiler_params=pltpu.CompilerParams(vmem_limit_bytes=48 * 2**20),
    )(index, info, q, ext, gkv, far, random, random, random)


def project_kernel(
    ctx_count,
    tp_count,
    chunks,
    width,
    att_ref,
    residual_ref,
    gain_ref,
    bias_ref,
    w0,
    w1,
    w2,
    w3,
    cross_ref,
    encoded_ref,
    out_ref,
    w_all,
    cross,
    a1,
    a2,
    a3,
    mixed,
    stats,
    g0,
    g1,
    g2,
    g3,
    w_sem,
    cross_sem,
    send_sem,
    recv_sem,
):
    ctx = lax.axis_index("ctx")
    tp = lax.axis_index("tp")
    mate = tp + 1 - 2 * lax.rem(tp, 2)
    over = lax.rem(tp + 2, tp_count)
    cater = tp_count - 1 - tp
    beyond = lax.rem(ctx + ctx_count // 2, ctx_count)
    rows = att_ref.shape[0] // chunks
    cols = residual_ref.shape[1]

    for k, w in enumerate((w0, w1, w2, w3)):
        pltpu.make_async_copy(w, w_all.at[k], w_sem.at[k]).start()
    for k, block in enumerate((tp, mate, over, cater)):
        pltpu.make_async_copy(
            cross_ref.at[pl.ds(block * cols, cols)], cross.at[k], cross_sem.at[k]
        ).start()

    barrier = pltpu.get_barrier_semaphore()
    for other in (mate, over, cater):
        pl.semaphore_signal(barrier, inc=1, device_id={"tp": other}, device_id_type=MESH)
    pl.semaphore_signal(barrier, inc=1, device_id={"ctx": beyond}, device_id_type=MESH)
    pl.semaphore_wait(barrier, 4)

    def cut(c):
        return pl.ds(pl.multiple_of(c * rows, rows), rows)

    def hop(kind, c, src, dst, where):
        return pltpu.make_async_remote_copy(
            src_ref=src,
            dst_ref=dst,
            send_sem=send_sem.at[kind, c],
            recv_sem=recv_sem.at[kind, c],
            device_id=where,
            device_id_type=MESH,
        )

    def att_mate(c):
        return hop(0, c, att_ref.at[cut(c)], a1.at[cut(c)], {"tp": mate})

    def att_over(c):
        return hop(1, c, att_ref.at[cut(c)], a2.at[cut(c)], {"tp": over})

    def att_on(c):
        return hop(2, c, a2.at[cut(c)], a3.at[cut(c)], {"tp": mate})

    def stat(c, k):
        other = (mate, over, cater)[k - 1]
        return hop(2 + k, c, stats.at[c, 0], stats.at[c, k], {"tp": other})

    def roll(c):
        return hop(6, c, encoded_ref.at[cut(c)], g0.at[cut(c)], {"ctx": beyond})

    def enc_mate(c):
        return hop(7, c, g0.at[cut(c)], g1.at[cut(c)], {"tp": mate})

    def enc_over(c):
        return hop(8, c, g0.at[cut(c)], g2.at[cut(c)], {"tp": over})

    def enc_on(c):
        return hop(9, c, g2.at[cut(c)], g3.at[cut(c)], {"tp": mate})

    def begin(c, carry):
        att_over(c).start()
        att_mate(c).start()
        return carry

    lax.fori_loop(0, chunks, begin, 0)
    for k, w in enumerate((w0, w1, w2, w3)):
        pltpu.make_async_copy(w, w_all.at[k], w_sem.at[k]).wait()

    def step(t, carry):
        def at(delay, body):
            c = t - delay

            @pl.when((c >= 0) & (c < chunks))
            def _():
                body(c)

        def relay_att(c):
            att_over(c).wait_recv()
            att_on(c).start()

        def relay_enc(c):
            roll(c).wait_recv()
            enc_over(c).start()
            enc_mate(c).start()

        def relay_on(c):
            enc_over(c).wait_recv()
            enc_on(c).start()

        def normalize(c):
            for k in (1, 2, 3):
                stat(c, k).wait_recv()
            both = stats[c, 0] + stats[c, 1] + stats[c, 2] + stats[c, 3]
            total = jnp.transpose(jnp.broadcast_to(both[0:1], (rows, rows)))[:, 0:1]
            square = jnp.transpose(jnp.broadcast_to(both[8:9], (rows, rows)))[:, 0:1]
            mean = total / width
            variance = square / width - mean * mean
            scaled = (mixed[cut(c), :] - mean) * lax.rsqrt(variance + norm_eps)
            encoded_ref[cut(c), :] = (
                scaled * gain_ref[...].astype(jnp.float32) + bias_ref[...].astype(jnp.float32)
            ).astype(encoded_ref.dtype)

        def mix(c):
            att_mate(c).wait_recv()
            att_on(c).wait_recv()
            part = residual_ref[cut(c), :].astype(jnp.float32)
            for k, a in enumerate((att_ref, a1, a2, a3)):
                part = part + jnp.dot(
                    a[cut(c), :], w_all[k], preferred_element_type=jnp.float32
                )
            mixed[cut(c), :] = part
            lane = lax.broadcasted_iota(jnp.int32, (rows, rows), 1)
            total = jnp.sum(part, axis=1, keepdims=True)
            square = jnp.sum(part * part, axis=1, keepdims=True)
            turned = jnp.transpose(jnp.where(lane < rows // 2, total, square))
            stats[c, 0, 0:8, :] = turned[0:8]
            stats[c, 0, 8:16, :] = turned[rows // 2 : rows // 2 + 8]

        def cast(c):
            enc_mate(c).wait_recv()
            enc_on(c).wait_recv()
            acc = jnp.zeros((rows, out_ref.shape[1]), jnp.float32)
            for k, g in enumerate((g0, g1, g2, g3)):
                acc = acc + jnp.dot(g[cut(c), :], cross[k], preferred_element_type=jnp.float32)
            out_ref[cut(c), :] = acc.astype(out_ref.dtype)

        at(0, relay_att)
        at(ROLL, relay_enc)
        at(ROLL + 2, relay_on)
        at(2, normalize)
        at(1, mix)

        def send_rows(c):
            roll(c).start()

        def send_stats(c):
            for k in (1, 2, 3):
                stat(c, k).start()

        at(2, send_rows)
        at(1, send_stats)

        @pl.when(t == ROLL + 3)
        def _():
            for k in range(4):
                pltpu.make_async_copy(
                    cross_ref.at[pl.ds(0, cols)], cross.at[k], cross_sem.at[k]
                ).wait()

        at(ROLL + 3, cast)
        return carry

    lax.fori_loop(0, chunks + ROLL + 3, step, 0)

    def finish(c, carry):
        att_mate(c).wait_send()
        att_over(c).wait_send()
        att_on(c).wait_send()
        for k in (1, 2, 3):
            stat(c, k).wait_send()
        roll(c).wait_send()
        enc_mate(c).wait_send()
        enc_over(c).wait_send()
        enc_on(c).wait_send()
        return carry

    lax.fori_loop(0, chunks, finish, 0)


ROLL = 5
CHUNKS = 6


def project(att, residual, gain, bias, weights, cross_weight, ctx_count, tp_count):
    rows, depth = att.shape
    cols = residual.shape[1]
    wide = cross_weight.shape[1]
    vmem = pl.BlockSpec(memory_space=VMEM)
    hbm = pl.BlockSpec(memory_space=pl.ANY)
    kept = jnp.bfloat16
    return pl.pallas_call(
        functools.partial(project_kernel, ctx_count, tp_count, CHUNKS, cols * tp_count),
        name="project",
        out_shape=(
            jax.ShapeDtypeStruct((rows, cols), kept),
            jax.ShapeDtypeStruct((rows, wide), kept),
        ),
        in_specs=[vmem] * 4 + [hbm] * 5,
        out_specs=(vmem, vmem),
        scratch_shapes=[
            VMEM((4, depth, cols), kept),
            VMEM((4, cols, wide), kept),
            VMEM((rows, depth), kept),
            VMEM((rows, depth), kept),
            VMEM((rows, depth), kept),
            VMEM((rows, cols), jnp.float32),
            VMEM((CHUNKS, 4, 16, rows // CHUNKS), jnp.float32),
            VMEM((rows, cols), kept),
            VMEM((rows, cols), kept),
            VMEM((rows, cols), kept),
            VMEM((rows, cols), kept),
            pltpu.SemaphoreType.DMA((4,)),
            pltpu.SemaphoreType.DMA((4,)),
            pltpu.SemaphoreType.DMA((10, CHUNKS)),
            pltpu.SemaphoreType.DMA((10, CHUNKS)),
        ],
        compiler_params=pltpu.CompilerParams(
            collective_id=2, has_side_effects=True, vmem_limit_bytes=60 * 2**20
        ),
    )(att, residual, gain, bias, *weights, cross_weight)


def shards(
    queries,
    keyvals,
    residual,
    out_weight,
    norm_gain,
    norm_bias,
    cross_weight,
    window_reach,
    global_blocks,
    random_blocks,
):
    tok_rows, head_cols = queries.shape
    head_count = window_reach.shape[0]
    head_size = head_cols // head_count
    ctx_count = lax.axis_size("ctx")
    me = lax.axis_index("ctx")
    block_count = tok_rows // BLOCK
    all_blocks = block_count * ctx_count
    scale = 1.0 / math.sqrt(head_size)
    q = queries.reshape(block_count, BLOCK, head_cols)
    kv = keyvals.reshape(block_count, BLOCK, 2 * head_cols)

    req_count = block_count * R
    slots = 1 + (req_count + ctx_count - 2) // ctx_count
    requests = random_blocks.reshape(ctx_count, req_count)
    owners = requests // block_count
    local_ids = requests % block_count
    positions = jnp.arange(req_count, dtype=jnp.int32)
    earlier = positions[None, :] < positions[:, None]
    ranks = jnp.sum(
        ((owners[:, :, None] == owners[:, None, :]) & earlier[None, :, :]).astype(jnp.int32), axis=2
    )
    slot_ids = jnp.arange(slots, dtype=jnp.int32)
    matches = (owners[:, None, :] == me) & (ranks[:, None, :] == slot_ids[None, :, None])
    source_ids = jnp.sum(jnp.where(matches, local_ids[:, None, :], 0), axis=2).reshape(-1)
    my_index = lax.dynamic_index_in_dim(owners * slots + ranks, me, 0, keepdims=False)
    place = jnp.concatenate([global_blocks // block_count, global_blocks % block_count])
    own_ids = me * block_count + jnp.arange(block_count, dtype=jnp.int32)
    replaced = jnp.where(
        own_ids == global_blocks[0], 0, jnp.where(own_ids == global_blocks[1], 1, -1)
    )
    info = jnp.concatenate([window_reach, replaced])

    ext, gkv, gq = edges(place, kv, q, ctx_count)
    partials = far_partials(gq, kv, scale, head_count, ctx_count)
    random, far = exchange(source_ids, kv, partials, ctx_count, slots)
    attended = attention(my_index, info, q, ext, gkv, far, random, scale, head_count, all_blocks)
    attended = attended.reshape(tok_rows, head_cols)
    tp = lax.axis_index("tp")
    tp_count = lax.axis_size("tp")
    cols = residual.shape[1]
    mates = (tp, tp + 1 - 2 * lax.rem(tp, 2), lax.rem(tp + 2, tp_count), tp_count - 1 - tp)
    weights = []
    for k in range(tp_count):
        block = lax.dynamic_slice_in_dim(out_weight, mates[k] * cols, cols, axis=1)
        if k > 0:
            block = lax.ppermute(block, "tp", [(i, i ^ k) for i in range(tp_count)])
        weights.append(block)
    encoded, cross_kv = project(
        attended,
        residual,
        norm_gain.reshape(1, cols),
        norm_bias.reshape(1, cols),
        weights,
        cross_weight.reshape(D, 2 * head_cols),
        ctx_count,
        tp_count,
    )
    return (encoded, cross_kv.reshape(tok_rows, 2, head_cols))


def solution(mesh):
    placed = (
        P("ctx", "tp"),
        P("ctx", None, "tp"),
        P("ctx", "tp"),
        P("tp", None),
        P("tp"),
        P("tp"),
        P(None, None, "tp"),
        P("tp"),
        P(),
        P(),
    )
    return jax.shard_map(
        shards,
        mesh=mesh,
        in_specs=placed,
        out_specs=(P("ctx", "tp"), P("ctx", None, "tp")),
        check_vma=False,
    )
```

```python
import functools
import math

import jax
import jax.numpy as jnp
from jax import lax
from jax.experimental import pallas as pl
from jax.experimental.pallas import tpu as pltpu
from jax.sharding import PartitionSpec as P

D = 4096
BLOCK = 64
MAXR = 3
G = 2
R = 3
SPAN = 2 * MAXR + 1
MESH = pl.DeviceIdType.MESH
VMEM = pltpu.VMEM
SMEM = pltpu.SMEM

norm_eps = 1e-05


def greet(axis, count):
    me = lax.axis_index(axis)
    barrier = pltpu.get_barrier_semaphore()

    def signal(k, carry):
        pl.semaphore_signal(
            barrier, inc=1, device_id={axis: lax.rem(me + k, count)}, device_id_type=MESH
        )
        return carry

    lax.fori_loop(1, count, signal, 0)
    pl.semaphore_wait(barrier, count - 1)


def edges_kernel(
    count,
    place_ref,
    kv_ref,
    q_ref,
    ext_ref,
    gkv_ref,
    gq_ref,
    cand,
    got,
    full,
    halo_send,
    halo_recv,
    send1,
    recv1,
    send2,
    recv2,
):
    me = lax.axis_index("ctx")
    blocks = kv_ref.shape[0]
    wide = kv_ref.shape[2]
    half = q_ref.shape[2]
    part = (wide + half) // 4
    greet("ctx", count)
    after = lax.rem(me + 1, count)
    before = lax.rem(me + count - 1, count)
    to_after = pltpu.make_async_remote_copy(
        src_ref=kv_ref.at[pl.ds(blocks - MAXR, MAXR)],
        dst_ref=ext_ref.at[pl.ds(0, MAXR)],
        send_sem=halo_send.at[0],
        recv_sem=halo_recv.at[0],
        device_id={"ctx": after},
        device_id_type=MESH,
    )
    to_before = pltpu.make_async_remote_copy(
        src_ref=kv_ref.at[pl.ds(0, MAXR)],
        dst_ref=ext_ref.at[pl.ds(blocks + MAXR, MAXR)],
        send_sem=halo_send.at[1],
        recv_sem=halo_recv.at[1],
        device_id={"ctx": before},
        device_id_type=MESH,
    )
    for g in range(G):
        local = place_ref[G + g]
        row = jnp.concatenate([kv_ref[local], q_ref[local]], axis=1)
        for r in range(4):
            for c in range(4):
                cand[(g * 4 + r) * 4 + c] = row[r * 16 : r * 16 + 16, c * part : (c + 1) * part]

    def first(k):
        to = lax.rem(me + k, count)
        return pltpu.make_async_remote_copy(
            src_ref=cand.at[to],
            dst_ref=got.at[me],
            send_sem=send1.at[k],
            recv_sem=recv1.at[k],
            device_id={"ctx": to},
            device_id_type=MESH,
        )

    def second(k):
        to = lax.rem(me + k, count)
        return pltpu.make_async_remote_copy(
            src_ref=full.at[me],
            dst_ref=full.at[me],
            send_sem=send2.at[k],
            recv_sem=recv2.at[k],
            device_id={"ctx": to},
            device_id_type=MESH,
        )

    def each(action):
        def body(k, carry):
            action(k)
            return carry

        lax.fori_loop(1, count, body, 0)

    each(lambda k: first(k).start())
    to_after.start()
    to_before.start()
    got[me] = cand[me]
    ext_ref[pl.ds(MAXR, blocks)] = kv_ref[...]
    each(lambda k: first(k).wait())
    full[me] = got[place_ref[me // (count // G)]]
    each(lambda k: second(k).start())
    each(lambda k: second(k).wait())
    for g in range(G):
        for r in range(4):
            row = jnp.concatenate([full[(g * 4 + r) * 4 + c] for c in range(4)], axis=1)
            gkv_ref[g, r * 16 : r * 16 + 16, :] = row[:, :wide]
            gq_ref[g, r * 16 : r * 16 + 16, :] = row[:, wide:]
    to_after.wait()
    to_before.wait()


def edges(place, kv, q, count):
    blocks, rows, wide = kv.shape
    half = q.shape[2]
    part = (wide + half) // 4
    return pl.pallas_call(
        functools.partial(edges_kernel, count),
        name="edges",
        out_shape=(
            jax.ShapeDtypeStruct((blocks + 2 * MAXR, rows, wide), kv.dtype),
            jax.ShapeDtypeStruct((G, rows, wide), kv.dtype),
            jax.ShapeDtypeStruct((G, rows, half), kv.dtype),
        ),
        in_specs=[
            pl.BlockSpec(memory_space=SMEM),
            pl.BlockSpec(memory_space=VMEM),
            pl.BlockSpec(memory_space=VMEM),
        ],
        out_specs=(pl.BlockSpec(memory_space=VMEM),) * 3,
        scratch_shapes=[
            VMEM((count, 16, part), kv.dtype),
            VMEM((count, 16, part), kv.dtype),
            VMEM((count, 16, part), kv.dtype),
            pltpu.SemaphoreType.DMA((2,)),
            pltpu.SemaphoreType.DMA((2,)),
            pltpu.SemaphoreType.DMA((count,)),
            pltpu.SemaphoreType.DMA((count,)),
            pltpu.SemaphoreType.DMA((count,)),
            pltpu.SemaphoreType.DMA((count,)),
        ],
        compiler_params=pltpu.CompilerParams(
            collective_id=0, has_side_effects=True, vmem_limit_bytes=48 * 2**20
        ),
    )(place, kv, q)


def far_kernel(scale, head_count, gq_ref, kv_ref, out_ref):
    blocks, rows, wide = kv_ref.shape
    size = wide // (2 * head_count)
    for h in range(head_count):
        lanes = slice(h * size, (h + 1) * size)
        q = gq_ref[:, :, lanes].reshape(G * rows, size)
        k = kv_ref[:, :, lanes].reshape(blocks * rows, size)
        v = kv_ref[:, :, wide // 2 + h * size : wide // 2 + (h + 1) * size].reshape(
            blocks * rows, size
        )
        s = (
            lax.dot_general(q, k, (((1,), (1,)), ((), ())), preferred_element_type=jnp.float32)
            * scale
        )
        peak = jnp.max(s, axis=1, keepdims=True)
        p = jnp.exp(s - peak)
        total = jnp.sum(p, axis=1, keepdims=True)
        acc = jnp.dot(p.astype(jnp.bfloat16), v, preferred_element_type=jnp.float32)
        peak = jnp.broadcast_to(peak, acc.shape)
        total = jnp.broadcast_to(total, acc.shape)
        for r in range(8):
            cut = slice(r * 16, r * 16 + 16)
            out_ref[h * 8 + r, 0:16, :] = acc[cut]
            out_ref[h * 8 + r, 16:32, :] = peak[cut]
            out_ref[h * 8 + r, 32:48, :] = total[cut]


def far_partials(gq, kv, scale, head_count, count):
    size = gq.shape[2] // head_count
    return pl.pallas_call(
        functools.partial(far_kernel, scale, head_count),
        name="far_partials",
        out_shape=jax.ShapeDtypeStruct((count, 48, size), jnp.float32),
        in_specs=[pl.BlockSpec(memory_space=VMEM)] * 2,
        out_specs=pl.BlockSpec(memory_space=VMEM),
        compiler_params=pltpu.CompilerParams(vmem_limit_bytes=48 * 2**20),
    )(gq, kv)


def exchange_kernel(
    count,
    slots,
    source_ref,
    kv_ref,
    part_ref,
    random_ref,
    far_ref,
    stage,
    got,
    bulk_send,
    bulk_recv,
    send1,
    recv1,
    send2,
    recv2,
    own_sem,
):
    me = lax.axis_index("ctx")
    greet("ctx", count)

    def first(k):
        to = lax.rem(me + k, count)
        return pltpu.make_async_remote_copy(
            src_ref=part_ref.at[to],
            dst_ref=got.at[me],
            send_sem=send1.at[k],
            recv_sem=recv1.at[k],
            device_id={"ctx": to},
            device_id_type=MESH,
        )

    def second(k):
        to = lax.rem(me + k, count)
        return pltpu.make_async_remote_copy(
            src_ref=far_ref.at[me],
            dst_ref=far_ref.at[me],
            send_sem=send2.at[k],
            recv_sem=recv2.at[k],
            device_id={"ctx": to},
            device_id_type=MESH,
        )

    def bulk(k):
        to = lax.rem(me + k, count)
        return pltpu.make_async_remote_copy(
            src_ref=stage.at[pl.ds(to * slots, slots)],
            dst_ref=random_ref.at[pl.ds(me * slots, slots)],
            send_sem=bulk_send.at[k],
            recv_sem=bulk_recv.at[k],
            device_id={"ctx": to},
            device_id_type=MESH,
        )

    def each(action):
        def body(k, carry):
            action(k)
            return carry

        lax.fori_loop(1, count, body, 0)

    each(lambda k: first(k).start())
    got[me] = part_ref[me]

    def place(i, carry):
        stage[i] = kv_ref[source_ref[i]]
        return carry

    lax.fori_loop(0, count * slots, place, 0)
    each(lambda k: bulk(k).start())
    own = pltpu.make_async_copy(
        stage.at[pl.ds(me * slots, slots)], random_ref.at[pl.ds(me * slots, slots)], own_sem
    )
    own.start()
    each(lambda k: first(k).wait())

    def top(i, so_far):
        return jnp.maximum(so_far, got[i, 16:32, :])

    peak = lax.fori_loop(1, count, top, got[0, 16:32, :])

    def add(i, so_far):
        acc, total = so_far
        factor = jnp.exp(got[i, 16:32, :] - peak)
        return acc + got[i, 0:16, :] * factor, total + got[i, 32:48, :] * factor

    zero = jnp.zeros_like(peak)
    acc, total = lax.fori_loop(0, count, add, (zero, zero))
    far_ref[me] = (acc / total).astype(far_ref.dtype)
    each(lambda k: second(k).start())
    own.wait()
    each(lambda k: bulk(k).wait())
    each(lambda k: second(k).wait())


def exchange(source, kv, partials, count, slots):
    blocks, rows, wide = kv.shape
    size = partials.shape[2]
    dma = pltpu.SemaphoreType.DMA((count,))
    return pl.pallas_call(
        functools.partial(exchange_kernel, count, slots),
        name="exchange",
        out_shape=(
            jax.ShapeDtypeStruct((count * slots, rows, wide), kv.dtype),
            jax.ShapeDtypeStruct((count, 16, size), kv.dtype),
        ),
        in_specs=[
            pl.BlockSpec(memory_space=SMEM),
            pl.BlockSpec(memory_space=VMEM),
            pl.BlockSpec(memory_space=VMEM),
        ],
        out_specs=(pl.BlockSpec(memory_space=pl.ANY), pl.BlockSpec(memory_space=VMEM)),
        scratch_shapes=[
            VMEM((count * slots, rows, wide), kv.dtype),
            VMEM((count, 48, size), jnp.float32),
            dma,
            dma,
            dma,
            dma,
            dma,
            dma,
            pltpu.SemaphoreType.DMA,
        ],
        compiler_params=pltpu.CompilerParams(
            collective_id=1, has_side_effects=True, vmem_limit_bytes=56 * 2**20
        ),
    )(source, kv, partials)


def attention_kernel(
    scale,
    head_count,
    all_blocks,
    index_ref,
    info_ref,
    q_ref,
    ext_ref,
    gkv_ref,
    far_ref,
    rand0,
    rand1,
    rand2,
    out_ref,
):
    b = pl.program_id(0)
    rows = q_ref.shape[1]
    wide = gkv_ref.shape[2]
    half = wide // 2
    size = half // head_count
    me = lax.axis_index("ctx")
    block = me * pl.num_programs(0) + b
    replaced = info_ref[head_count + b]
    near = SPAN * rows
    spot = lax.broadcasted_iota(jnp.int32, (rows, near), 1) // rows - MAXR
    inside = (spot + block >= 0) & (spot + block < all_blocks)
    for h in range(head_count):
        kl = slice(h * size, (h + 1) * size)
        vl = slice(half + h * size, half + (h + 1) * size)
        reach = info_ref[h]
        q = q_ref[0, :, kl]

        def listed(lanes):
            return jnp.concatenate(
                [
                    gkv_ref[0, :, lanes],
                    gkv_ref[1, :, lanes],
                    rand0[0, :, lanes],
                    rand1[0, :, lanes],
                    rand2[0, :, lanes],
                ],
                axis=0,
            )

        def score(keys):
            return (
                lax.dot_general(
                    q, keys, (((1,), (1,)), ((), ())), preferred_element_type=jnp.float32
                )
                * scale
            )

        window_k = ext_ref[pl.ds(b, SPAN), :, kl].reshape(near, size)
        window_v = ext_ref[pl.ds(b, SPAN), :, vl].reshape(near, size)
        s1 = jnp.where(inside & (jnp.abs(spot) <= reach), score(window_k), -jnp.inf)
        s2 = score(listed(kl))
        peak = jnp.maximum(
            jnp.max(s1, axis=1, keepdims=True), jnp.max(s2, axis=1, keepdims=True)
        )
        p1 = jnp.exp(s1 - peak)
        p2 = jnp.exp(s2 - peak)
        total = jnp.sum(p1, axis=1, keepdims=True) + jnp.sum(p2, axis=1, keepdims=True)
        acc = jnp.dot(p1.astype(jnp.bfloat16), window_v, preferred_element_type=jnp.float32)
        acc = acc + jnp.dot(
            p2.astype(jnp.bfloat16), listed(vl), preferred_element_type=jnp.float32
        )
        out_ref[0, :, kl] = (acc / total).astype(out_ref.dtype)

    for g in range(G):

        @pl.when(replaced == g)
        def _():
            for h in range(head_count):
                for r in range(4):
                    out_ref[0, r * 16 : r * 16 + 16, h * size : (h + 1) * size] = far_ref[
                        h * 8 + g * 4 + r
                    ]


def attention(index, info, q, ext, gkv, far, random, scale, head_count, all_blocks):
    blocks, rows, half = q.shape
    wide = 2 * half

    def whole(x):
        return pl.BlockSpec(x.shape, lambda b, *_: (0,) * x.ndim)

    def pick(r):
        return pl.BlockSpec((1, rows, wide), lambda b, index, info: (index[b * R + r], 0, 0))

    one = pl.BlockSpec((1, rows, half), lambda b, *_: (b, 0, 0))
    return pl.pallas_call(
        functools.partial(attention_kernel, scale, head_count, all_blocks),
        name="attention",
        grid_spec=pltpu.PrefetchScalarGridSpec(
            num_scalar_prefetch=2,
            grid=(blocks,),
            in_specs=[one, whole(ext), whole(gkv), whole(far), pick(0), pick(1), pick(2)],
            out_specs=one,
        ),
        out_shape=jax.ShapeDtypeStruct(q.shape, q.dtype),
        compiler_params=pltpu.CompilerParams(vmem_limit_bytes=48 * 2**20),
    )(index, info, q, ext, gkv, far, random, random, random)


def project_kernel(
    ctx_count,
    tp_count,
    chunks,
    width,
    att_ref,
    residual_ref,
    gain_ref,
    bias_ref,
    w0,
    w1,
    w2,
    w3,
    cross_ref,
    encoded_ref,
    out_ref,
    w_all,
    cross,
    a1,
    a2,
    a3,
    mixed,
    stats,
    g0,
    g1,
    g2,
    g3,
    w_sem,
    cross_sem,
    send_sem,
    recv_sem,
):
    ctx = lax.axis_index("ctx")
    tp = lax.axis_index("tp")
    mate = tp + 1 - 2 * lax.rem(tp, 2)
    over = lax.rem(tp + 2, tp_count)
    cater = tp_count - 1 - tp
    beyond = lax.rem(ctx + ctx_count // 2, ctx_count)
    rows = att_ref.shape[0] // chunks
    cols = residual_ref.shape[1]

    own_cols = w0.at[:, pl.ds(pl.multiple_of(tp * residual_ref.shape[1], residual_ref.shape[1]), residual_ref.shape[1])]
    for k, w in enumerate((own_cols, w1, w2, w3)):
        pltpu.make_async_copy(w, w_all.at[k], w_sem.at[k]).start()
    for k, block in enumerate((tp, mate, over, cater)):
        pltpu.make_async_copy(
            cross_ref.at[pl.ds(block * cols, cols)], cross.at[k], cross_sem.at[k]
        ).start()

    barrier = pltpu.get_barrier_semaphore()
    for other in (mate, over, cater):
        pl.semaphore_signal(barrier, inc=1, device_id={"tp": other}, device_id_type=MESH)
    pl.semaphore_signal(barrier, inc=1, device_id={"ctx": beyond}, device_id_type=MESH)
    pl.semaphore_wait(barrier, 4)

    def cut(c):
        return pl.ds(pl.multiple_of(c * rows, rows), rows)

    def hop(kind, c, src, dst, where):
        return pltpu.make_async_remote_copy(
            src_ref=src,
            dst_ref=dst,
            send_sem=send_sem.at[kind, c],
            recv_sem=recv_sem.at[kind, c],
            device_id=where,
            device_id_type=MESH,
        )

    def att_mate(c):
        return hop(0, c, att_ref.at[cut(c)], a1.at[cut(c)], {"tp": mate})

    def att_over(c):
        return hop(1, c, att_ref.at[cut(c)], a2.at[cut(c)], {"tp": over})

    def att_on(c):
        return hop(2, c, a2.at[cut(c)], a3.at[cut(c)], {"tp": mate})

    def stat(c, k):
        other = (mate, over, cater)[k - 1]
        return hop(2 + k, c, stats.at[c, 0], stats.at[c, k], {"tp": other})

    def roll(c):
        return hop(6, c, encoded_ref.at[cut(c)], g0.at[cut(c)], {"ctx": beyond})

    def enc_mate(c):
        return hop(7, c, g0.at[cut(c)], g1.at[cut(c)], {"tp": mate})

    def enc_over(c):
        return hop(8, c, g0.at[cut(c)], g2.at[cut(c)], {"tp": over})

    def enc_on(c):
        return hop(9, c, g2.at[cut(c)], g3.at[cut(c)], {"tp": mate})

    def begin(c, carry):
        att_over(c).start()
        att_mate(c).start()
        return carry

    lax.fori_loop(0, chunks, begin, 0)
    for k, w in enumerate((own_cols, w1, w2, w3)):
        pltpu.make_async_copy(w, w_all.at[k], w_sem.at[k]).wait()

    def step(t, carry):
        def at(delay, body):
            c = t - delay

            @pl.when((c >= 0) & (c < chunks))
            def _():
                body(c)

        def relay_att(c):
            att_over(c).wait_recv()
            att_on(c).start()

        def relay_enc(c):
            roll(c).wait_recv()
            enc_over(c).start()
            enc_mate(c).start()

        def relay_on(c):
            enc_over(c).wait_recv()
            enc_on(c).start()

        def normalize(c):
            for k in (1, 2, 3):
                stat(c, k).wait_recv()
            both = stats[c, 0] + stats[c, 1] + stats[c, 2] + stats[c, 3]
            total = jnp.transpose(jnp.broadcast_to(both[0:1], (rows, rows)))[:, 0:1]
            square = jnp.transpose(jnp.broadcast_to(both[8:9], (rows, rows)))[:, 0:1]
            mean = total / width
            variance = square / width - mean * mean
            scaled = (mixed[cut(c), :] - mean) * lax.rsqrt(variance + norm_eps)
            encoded_ref[cut(c), :] = (
                scaled * gain_ref[...].astype(jnp.float32) + bias_ref[...].astype(jnp.float32)
            ).astype(encoded_ref.dtype)

        def mix(c):
            att_mate(c).wait_recv()
            att_on(c).wait_recv()
            part = residual_ref[cut(c), :].astype(jnp.float32)
            for k, a in enumerate((att_ref, a1, a2, a3)):
                part = part + jnp.dot(
                    a[cut(c), :], w_all[k], preferred_element_type=jnp.float32
                )
            mixed[cut(c), :] = part
            lane = lax.broadcasted_iota(jnp.int32, (rows, rows), 1)
            total = jnp.sum(part, axis=1, keepdims=True)
            square = jnp.sum(part * part, axis=1, keepdims=True)
            turned = jnp.transpose(jnp.where(lane < rows // 2, total, square))
            stats[c, 0, 0:8, :] = turned[0:8]
            stats[c, 0, 8:16, :] = turned[rows // 2 : rows // 2 + 8]

        def cast(c):
            enc_mate(c).wait_recv()
            enc_on(c).wait_recv()
            acc = jnp.zeros((rows, out_ref.shape[1]), jnp.float32)
            for k, g in enumerate((g0, g1, g2, g3)):
                acc = acc + jnp.dot(g[cut(c), :], cross[k], preferred_element_type=jnp.float32)
            out_ref[cut(c), :] = acc.astype(out_ref.dtype)

        at(0, relay_att)
        at(ROLL, relay_enc)
        at(ROLL + 2, relay_on)
        at(2, normalize)
        at(1, mix)

        def send_rows(c):
            roll(c).start()

        def send_stats(c):
            for k in (1, 2, 3):
                stat(c, k).start()

        at(2, send_rows)
        at(1, send_stats)

        @pl.when(t == ROLL + 3)
        def _():
            for k in range(4):
                pltpu.make_async_copy(
                    cross_ref.at[pl.ds(0, cols)], cross.at[k], cross_sem.at[k]
                ).wait()

        at(ROLL + 3, cast)
        return carry

    lax.fori_loop(0, chunks + ROLL + 3, step, 0)

    def finish(c, carry):
        att_mate(c).wait_send()
        att_over(c).wait_send()
        att_on(c).wait_send()
        for k in (1, 2, 3):
            stat(c, k).wait_send()
        roll(c).wait_send()
        enc_mate(c).wait_send()
        enc_over(c).wait_send()
        enc_on(c).wait_send()
        return carry

    lax.fori_loop(0, chunks, finish, 0)


ROLL = 5
CHUNKS = 6


def project(att, residual, gain, bias, out_weight, weights, cross_weight, ctx_count, tp_count):
    rows, depth = att.shape
    cols = residual.shape[1]
    wide = cross_weight.shape[1]
    vmem = pl.BlockSpec(memory_space=VMEM)
    hbm = pl.BlockSpec(memory_space=pl.ANY)
    kept = jnp.bfloat16
    return pl.pallas_call(
        functools.partial(project_kernel, ctx_count, tp_count, CHUNKS, cols * tp_count),
        name="project",
        out_shape=(
            jax.ShapeDtypeStruct((rows, cols), kept),
            jax.ShapeDtypeStruct((rows, wide), kept),
        ),
        in_specs=[vmem] * 4 + [hbm] * 5,
        out_specs=(vmem, vmem),
        scratch_shapes=[
            VMEM((4, depth, cols), kept),
            VMEM((4, cols, wide), kept),
            VMEM((rows, depth), kept),
            VMEM((rows, depth), kept),
            VMEM((rows, depth), kept),
            VMEM((rows, cols), jnp.float32),
            VMEM((CHUNKS, 4, 16, rows // CHUNKS), jnp.float32),
            VMEM((rows, cols), kept),
            VMEM((rows, cols), kept),
            VMEM((rows, cols), kept),
            VMEM((rows, cols), kept),
            pltpu.SemaphoreType.DMA((4,)),
            pltpu.SemaphoreType.DMA((4,)),
            pltpu.SemaphoreType.DMA((10, CHUNKS)),
            pltpu.SemaphoreType.DMA((10, CHUNKS)),
        ],
        compiler_params=pltpu.CompilerParams(
            collective_id=2, has_side_effects=True, vmem_limit_bytes=60 * 2**20
        ),
    )(att, residual, gain, bias, out_weight, *weights, cross_weight)


FIRST = 16
SECOND = 12
LINE = 4
HEAD_COLS = 128


def front_kernel(
    count,
    scale,
    list_ref,
    kv_ref,
    q_ref,
    weight_ref,
    out_ref,
    w1_ref,
    w2_ref,
    w3_ref,
    ext,
    cand,
    got,
    full,
    gkv,
    gq,
    part,
    far_got,
    far,
    pool0,
    pool1,
    pool2,
    pool3,
    hold0,
    hold1,
    hold2,
    hold3,
    last0,
    last1,
    last2,
    last3,
    stage1,
    stage2,
    pair_send,
    pair_recv,
    halo_send,
    halo_recv,
    weight_send,
    weight_recv,
    small_send,
    small_recv,
    bulk_send,
    bulk_recv,
):
    me = lax.axis_index("ctx")
    tp = lax.axis_index("tp")
    heads, blocks, rows, pair = kv_ref.shape
    size = pair // 2
    spot = (me // 8, lax.rem(me // 2, LINE))
    level = lax.rem(me, 2)
    twin = me + 1 - 2 * level
    mates = (tp + 1 - 2 * lax.rem(tp, 2), lax.rem(tp + 2, 4), 3 - tp)
    pools = (pool0, pool1, pool2, pool3)
    holds = (hold0, hold1, hold2, hold3)
    lasts = (last0, last1, last2, last3)
    wcols = w1_ref.shape[1]
    near = SPAN * rows

    barrier = pltpu.get_barrier_semaphore()

    def greeting(k, carry):
        pl.semaphore_signal(
            barrier, inc=1, device_id={"ctx": lax.rem(me + k, count)}, device_id_type=MESH
        )
        return carry

    lax.fori_loop(1, count, greeting, 0)
    for other in mates:
        pl.semaphore_signal(barrier, inc=1, device_id={"tp": other}, device_id_type=MESH)

    def base(c):
        return 20 + (c % 2) * (LINE * FIRST + LINE * SECOND + blocks * R)

    def along(c, stage, d):
        x, z = spot
        if (c + stage) % 2 == 0:
            x = lax.rem(x + d, LINE)
            return x, x * 8 + z * 2 + level
        z = lax.rem(z + d, LINE)
        return z, x * 8 + z * 2 + level

    def pair_copy(c):
        return pltpu.make_async_remote_copy(
            src_ref=kv_ref.at[c],
            dst_ref=pools[c].at[pl.ds(level * blocks, blocks)],
            send_sem=pair_send.at[c],
            recv_sem=pair_recv.at[c],
            device_id={"ctx": twin},
            device_id_type=MESH,
        )

    def halo_copy(k):
        src, dst, to = (
            (blocks - MAXR, 0, lax.rem(me + 1, count)),
            (0, blocks + MAXR, lax.rem(me + count - 1, count)),
        )[k]
        return pltpu.make_async_remote_copy(
            src_ref=kv_ref.at[:, pl.ds(src, MAXR)],
            dst_ref=ext.at[:, pl.ds(dst, MAXR)],
            send_sem=halo_send.at[k],
            recv_sem=halo_recv.at[k],
            device_id={"ctx": to},
            device_id_type=MESH,
        )

    def weight_copy(k):
        other = mates[k]
        return pltpu.make_async_remote_copy(
            src_ref=weight_ref.at[:, pl.ds(pl.multiple_of(other * wcols, wcols), wcols)],
            dst_ref=(w1_ref, w2_ref, w3_ref)[k],
            send_sem=weight_send.at[k],
            recv_sem=weight_recv.at[k],
            device_id={"tp": other},
            device_id_type=MESH,
        )

    def small(kind, k, scattered, src, dst):
        to = lax.rem(me + k, count)
        return pltpu.make_async_remote_copy(
            src_ref=src.at[to if scattered else me],
            dst_ref=dst.at[me],
            send_sem=small_send.at[kind, k],
            recv_sem=small_recv.at[kind, k],
            device_id={"ctx": to},
            device_id_type=MESH,
        )

    def bulk(c, stage, d):
        slots = (FIRST, SECOND)[stage]
        mine = spot[(c + stage) % 2]
        buffer = (stage1, stage2)[stage]
        return pltpu.make_async_remote_copy(
            src_ref=buffer.at[c, pl.ds((d - 1) * slots, slots)],
            dst_ref=(holds, lasts)[stage][c].at[pl.ds(mine * slots, slots)],
            send_sem=bulk_send.at[stage, c, d - 1],
            recv_sem=bulk_recv.at[stage, c, d - 1],
            device_id={"ctx": along(c, stage, d)[1]},
            device_id_type=MESH,
        )

    def each(action):
        def body(k, carry):
            action(k)
            return carry

        lax.fori_loop(1, count, body, 0)

    for g in range(G):
        local = list_ref[G + g]
        row = jnp.concatenate([kv_ref[c, local] for c in range(heads)] + [q_ref[local]], axis=1)
        cut = row.shape[1] // 4
        for r in range(4):
            for s in range(4):
                cand[(g * 4 + r) * 4 + s] = row[r * 16 : r * 16 + 16, s * cut : (s + 1) * cut]
    for c in range(heads):
        pools[c][pl.ds(level * blocks, blocks)] = kv_ref[c]
        ext[c, pl.ds(MAXR, blocks)] = kv_ref[c]
    pl.semaphore_wait(barrier, count - 1 + 3)

    each(lambda k: small(0, k, True, cand, got).start())
    for c in range(heads):
        pair_copy(c).start()
    for k in range(2):
        halo_copy(k).start()
    got[me] = cand[me]
    each(lambda k: small(0, k, True, cand, got).wait())
    full[me] = got[list_ref[me // (count // G)]]
    each(lambda k: small(1, k, False, full, full).start())

    for c in range(heads):
        pair_copy(c).wait()
        for d in range(1, LINE):
            target, _ = along(c, 0, d)

            def fill(j, carry):
                source = list_ref[base(c) + target * FIRST + j]
                stage1[c, (d - 1) * FIRST + j] = pools[c][source]
                return carry

            lax.fori_loop(0, FIRST, fill, 0)
        for d in (1, 3, 2):
            bulk(c, 0, d).start()

    each(lambda k: small(1, k, False, full, full).wait())
    for g in range(G):
        for r in range(4):
            row = jnp.concatenate([full[(g * 4 + r) * 4 + s] for s in range(4)], axis=1)
            gkv[g, r * 16 : r * 16 + 16, :] = row[:, : heads * pair]
            gq[g, r * 16 : r * 16 + 16, :] = row[:, heads * pair :]

    for h in range(heads):
        gq_h = gq[:, :, h * size : (h + 1) * size].reshape(G * rows, size)
        k_h = kv_ref[h, :, :, 0:size].reshape(blocks * rows, size)
        v_h = kv_ref[h, :, :, size:pair].reshape(blocks * rows, size)
        s = (
            lax.dot_general(gq_h, k_h, (((1,), (1,)), ((), ())), preferred_element_type=jnp.float32)
            * scale
        )
        peak = jnp.max(s, axis=1, keepdims=True)
        p = jnp.exp(s - peak)
        total = jnp.sum(p, axis=1, keepdims=True)
        acc = jnp.dot(p.astype(jnp.bfloat16), v_h, preferred_element_type=jnp.float32)
        peak = jnp.broadcast_to(peak, acc.shape)
        total = jnp.broadcast_to(total, acc.shape)
        for r in range(8):
            cut = slice(r * 16, r * 16 + 16)
            part[h * 8 + r, 0:16, :] = acc[cut]
            part[h * 8 + r, 16:32, :] = peak[cut]
            part[h * 8 + r, 32:48, :] = total[cut]
    far_got[me] = part[me]
    for k in range(3):
        weight_copy(k).start()
    each(lambda k: small(2, k, True, part, far_got).start())

    held = 2 * blocks
    ended = held + LINE * FIRST

    for c in range(heads):
        for d in range(1, LINE):
            bulk(c, 0, d).wait()
        for d in range(1, LINE):
            target, _ = along(c, 1, d)

            def fill(j, carry):
                source = list_ref[base(c) + LINE * FIRST + target * SECOND + j]
                stage2[c, (d - 1) * SECOND + j] = jnp.where(
                    source < held,
                    pools[c][jnp.minimum(source, held - 1)],
                    holds[c][jnp.maximum(source - held, 0)],
                )
                return carry

            lax.fori_loop(0, SECOND, fill, 0)
        for d in (1, 3, 2):
            bulk(c, 1, d).start()

    each(lambda k: small(2, k, True, part, far_got).wait())

    def top(i, so_far):
        return jnp.maximum(so_far, far_got[i, 16:32, :])

    far_peak = lax.fori_loop(1, count, top, far_got[0, 16:32, :])

    def add(i, so_far):
        acc, total = so_far
        factor = jnp.exp(far_got[i, 16:32, :] - far_peak)
        return acc + far_got[i, 0:16, :] * factor, total + far_got[i, 32:48, :] * factor

    zero = jnp.zeros_like(far_peak)
    far_acc, far_total = lax.fori_loop(0, count, add, (zero, zero))
    far[me] = (far_acc / far_total).astype(far.dtype)
    each(lambda k: small(3, k, False, far, far).start())

    for k in range(2):
        halo_copy(k).wait()

    place = lax.broadcasted_iota(jnp.int32, (rows, near), 1) // rows - MAXR
    for c in range(heads):
        for d in range(1, LINE):
            bulk(c, 1, d).wait()
        lanes = slice(c * size, (c + 1) * size)
        reach = list_ref[2 * G + c]
        allowed = jnp.abs(place) <= reach
        g_k = gkv[:, :, c * pair : c * pair + size].reshape(G * rows, size)
        g_v = gkv[:, :, c * pair + size : (c + 1) * pair].reshape(G * rows, size)

        def attend(b, carry):
            block = me * blocks + b
            inside = (place + block >= 0) & (place + block < count * blocks)
            q = q_ref[b, :, lanes]
            picked = []
            for r in range(R):
                at = list_ref[base(c) + LINE * (FIRST + SECOND) + b * R + r]
                picked.append(
                    jnp.where(
                        at < held,
                        pools[c][jnp.minimum(at, held - 1)],
                        jnp.where(
                            at < ended,
                            holds[c][jnp.clip(at - held, 0, LINE * FIRST - 1)],
                            lasts[c][jnp.maximum(at - ended, 0)],
                        ),
                    )
                )

            def score(keys):
                return (
                    lax.dot_general(
                        q, keys, (((1,), (1,)), ((), ())), preferred_element_type=jnp.float32
                    )
                    * scale
                )

            window = ext[c, pl.ds(b, SPAN)].reshape(near, pair)
            s1 = jnp.where(inside & allowed, score(window[:, :size]), -jnp.inf)
            s2 = score(jnp.concatenate([g_k] + [x[:, :size] for x in picked], axis=0))
            peak = jnp.maximum(
                jnp.max(s1, axis=1, keepdims=True), jnp.max(s2, axis=1, keepdims=True)
            )
            p1 = jnp.exp(s1 - peak)
            p2 = jnp.exp(s2 - peak)
            total = jnp.sum(p1, axis=1, keepdims=True) + jnp.sum(p2, axis=1, keepdims=True)
            acc = jnp.dot(
                p1.astype(jnp.bfloat16), window[:, size:], preferred_element_type=jnp.float32
            ) + jnp.dot(
                p2.astype(jnp.bfloat16),
                jnp.concatenate([g_v] + [x[:, size:] for x in picked], axis=0),
                preferred_element_type=jnp.float32,
            )
            out_ref[b, :, lanes] = (acc / total).astype(out_ref.dtype)
            return carry

        lax.fori_loop(0, blocks, attend, 0)

    each(lambda k: small(3, k, False, far, far).wait())
    swap = []
    for g in range(G):
        swap.append(
            jnp.concatenate(
                [
                    jnp.concatenate([far[h * 8 + g * 4 + r] for r in range(4)], axis=0)
                    for h in range(heads)
                ],
                axis=1,
            )
        )

    def replace(b, carry):
        which = list_ref[2 * G + heads + b]
        out_ref[b] = jnp.where(which == 0, swap[0], jnp.where(which == 1, swap[1], out_ref[b]))
        return carry

    lax.fori_loop(0, blocks, replace, 0)
    for k in range(3):
        weight_copy(k).wait()


def front(lists, kv, q, weight, scale, count, tp_count):
    heads, blocks, rows, pair = kv.shape
    size = pair // 2
    kept = kv.dtype
    vmem = pl.BlockSpec(memory_space=VMEM)
    hbm = pl.BlockSpec(memory_space=pl.ANY)
    cols = weight.shape[1] // tp_count
    moved = jax.ShapeDtypeStruct((weight.shape[0], cols), kept)
    cut = (heads * pair + heads * size) // 4
    dma = pltpu.SemaphoreType.DMA
    return pl.pallas_call(
        functools.partial(front_kernel, count, scale),
        name="front",
        out_shape=(jax.ShapeDtypeStruct(q.shape, kept), moved, moved, moved),
        in_specs=[pl.BlockSpec(memory_space=SMEM), vmem, vmem, hbm],
        out_specs=(vmem, hbm, hbm, hbm),
        scratch_shapes=[
            VMEM((heads, blocks + 2 * MAXR, rows, pair), kept),
            VMEM((count, 16, cut), kept),
            VMEM((count, 16, cut), kept),
            VMEM((count, 16, cut), kept),
            VMEM((G, rows, heads * pair), kept),
            VMEM((G, rows, heads * size), kept),
            VMEM((count, 48, size), jnp.float32),
            VMEM((count, 48, size), jnp.float32),
            VMEM((count, 16, size), kept),
        ]
        + [VMEM((2 * blocks, rows, pair), kept)] * heads
        + [VMEM((LINE * FIRST, rows, pair), kept)] * heads
        + [VMEM((LINE * SECOND, rows, pair), kept)] * heads
        + [
            VMEM((heads, (LINE - 1) * FIRST, rows, pair), kept),
            VMEM((heads, (LINE - 1) * SECOND, rows, pair), kept),
            dma((heads,)),
            dma((heads,)),
            dma((2,)),
            dma((2,)),
            dma((3,)),
            dma((3,)),
            dma((4, count)),
            dma((4, count)),
            dma((2, heads, LINE - 1)),
            dma((2, heads, LINE - 1)),
        ],
        compiler_params=pltpu.CompilerParams(
            collective_id=3, has_side_effects=True, vmem_limit_bytes=60 * 2**20
        ),
    )(lists, kv, q, weight)


def exclusive(flags):
    ones = flags.astype(jnp.int32)
    return jnp.cumsum(ones, axis=-1) - ones


def listing(flags, ranks, values, slots):
    wanted = jnp.arange(slots, dtype=jnp.int32)[:, None]
    hit = flags[..., None, :] & (ranks[..., None, :] == wanted)
    return jnp.sum(jnp.where(hit, values, 0), axis=-1)


def route(asked, first, second, entries):
    many = asked.shape[-1]
    ids = jnp.arange(many, dtype=jnp.int32)
    line = jnp.arange(LINE, dtype=jnp.int32)
    need = jnp.any(asked, axis=1)
    rank = exclusive(need)
    mine = need[:, first, second]
    list1 = listing(mine, rank[:, first, second], ids, FIRST)
    held = many + line[:, None, None] * FIRST + jnp.minimum(rank[first], FIRST - 1)
    where = jnp.where(line[:, None, None] == first, ids, held)
    here = asked[first]
    wanted = here[:, :, second].reshape(LINE, LINE * many)
    list2 = listing(wanted, exclusive(wanted), where[:, second].reshape(-1), SECOND)
    own = jnp.swapaxes(here[second], 0, 1).reshape(LINE, LINE * many)
    ended = (
        many
        + LINE * FIRST
        + line[:, None] * SECOND
        + jnp.minimum(exclusive(own), SECOND - 1)
    )
    ended = jnp.swapaxes(ended.reshape(LINE, LINE, many), 0, 1)
    final = jnp.where(line[None, :, None] == second, where, ended)
    return list1.reshape(-1), list2.reshape(-1), final


def plan(random_blocks, block_count, ctx_count, me):
    req_count = block_count * R
    all_blocks = block_count * ctx_count
    requests = random_blocks.reshape(ctx_count, req_count)
    asked = jnp.any(
        requests[:, :, None] == jnp.arange(all_blocks, dtype=jnp.int32)[None, None, :], axis=1
    )
    asked = asked.reshape(LINE, LINE, 2, LINE, LINE, 2 * block_count)
    line = jnp.arange(LINE, dtype=jnp.int32)
    apart = line[:, None] != line[None, :]
    ones = asked.astype(jnp.int32)

    def most(counts, mask):
        return jnp.max(jnp.where(mask, counts, 0))

    first_x = most(jnp.sum(jnp.max(ones, axis=1), axis=-1), apart[:, None, :, None])
    first_z = most(jnp.sum(jnp.max(ones, axis=0), axis=-1), apart[:, None, None, :])
    second_z = most(jnp.sum(ones, axis=(3, 5)), apart[None, :, None, :])
    second_x = most(jnp.sum(ones, axis=(4, 5)), apart[:, None, None, :])
    fits = (jnp.maximum(first_x, first_z) <= FIRST) & (jnp.maximum(second_x, second_z) <= SECOND)
    x, z, level = me // 8, me // 2 % LINE, me % 2
    flat = asked[:, :, level]
    mine = requests[me]
    picked = mine[:, None] == jnp.arange(all_blocks, dtype=jnp.int32)[None, :]
    lists = []
    for turned in (False, True):
        if turned:
            a, b, final = route(jnp.transpose(flat, (1, 0, 3, 2, 4)), z, x, mine)
            final = jnp.swapaxes(final, 0, 1)
        else:
            a, b, final = route(flat, x, z, mine)
        lists += [a, b, jnp.sum(jnp.where(picked, final.reshape(-1)[None, :], 0), axis=1)]
    return fits, lists


def direct(place, info, source_ids, my_index, kv_heads, q, out_weight, scale, count, slots):
    heads, block_count, rows, pair = kv_heads.shape
    kv = jnp.transpose(
        kv_heads.reshape(heads, block_count, rows, 2, pair // 2), (1, 2, 3, 0, 4)
    ).reshape(block_count, rows, heads * pair)
    ext, gkv, gq = edges(place, kv, q, count)
    partials = far_partials(gq, kv, scale, heads, count)
    random, far = exchange(source_ids, kv, partials, count, slots)
    attended = attention(
        my_index, info, q, ext, gkv, far, random, scale, heads, count * block_count
    )
    tp = lax.axis_index("tp")
    tp_count = lax.axis_size("tp")
    cols = out_weight.shape[1] // tp_count
    mates = (tp, tp + 1 - 2 * lax.rem(tp, 2), lax.rem(tp + 2, tp_count), tp_count - 1 - tp)
    weights = []
    for k in range(1, tp_count):
        block = lax.dynamic_slice_in_dim(out_weight, mates[k] * cols, cols, axis=1)
        weights.append(lax.ppermute(block, "tp", [(i, i ^ k) for i in range(tp_count)]))
    return (attended, *weights)


def shards(
    queries,
    keyvals,
    residual,
    out_weight,
    norm_gain,
    norm_bias,
    cross_weight,
    window_reach,
    global_blocks,
    random_blocks,
):
    tok_rows, head_cols = queries.shape
    head_count = window_reach.shape[0]
    head_size = head_cols // head_count
    ctx_count = lax.axis_size("ctx")
    tp_count = lax.axis_size("tp")
    me = lax.axis_index("ctx")
    block_count = tok_rows // BLOCK
    scale = 1.0 / math.sqrt(head_size)
    q = queries.reshape(block_count, BLOCK, head_cols)
    kv_heads = jnp.transpose(
        keyvals.reshape(block_count, BLOCK, 2, head_count, head_size), (3, 0, 1, 2, 4)
    ).reshape(head_count, block_count, BLOCK, 2 * head_size)

    place = jnp.concatenate([global_blocks // block_count, global_blocks % block_count])
    own_ids = me * block_count + jnp.arange(block_count, dtype=jnp.int32)
    replaced = jnp.where(
        own_ids == global_blocks[0], 0, jnp.where(own_ids == global_blocks[1], 1, -1)
    )
    info = jnp.concatenate([window_reach, replaced])
    fits, lists = plan(random_blocks, block_count, ctx_count, me)
    lists = jnp.concatenate([place, info] + lists)

    def staged(kv_heads, q, out_weight):
        return tuple(front(lists, kv_heads, q, out_weight, scale, ctx_count, tp_count))

    def plain(kv_heads, q, out_weight):
        req_count = block_count * R
        slots = 1 + (req_count + ctx_count - 2) // ctx_count
        requests = random_blocks.reshape(ctx_count, req_count)
        owners = requests // block_count
        local_ids = requests % block_count
        positions = jnp.arange(req_count, dtype=jnp.int32)
        earlier = positions[None, :] < positions[:, None]
        ranks = jnp.sum(
            ((owners[:, :, None] == owners[:, None, :]) & earlier[None, :, :]).astype(jnp.int32),
            axis=2,
        )
        slot_ids = jnp.arange(slots, dtype=jnp.int32)
        matches = (owners[:, None, :] == me) & (ranks[:, None, :] == slot_ids[None, :, None])
        source_ids = jnp.sum(jnp.where(matches, local_ids[:, None, :], 0), axis=2).reshape(-1)
        my_index = lax.dynamic_index_in_dim(owners * slots + ranks, me, 0, keepdims=False)
        return direct(
            place, info, source_ids, my_index, kv_heads, q, out_weight, scale, ctx_count, slots
        )

    attended, *weights = lax.cond(fits, staged, plain, kv_heads, q, out_weight)
    attended = attended.reshape(tok_rows, head_cols)
    cols = residual.shape[1]
    encoded, cross_kv = project(
        attended,
        residual,
        norm_gain.reshape(1, cols),
        norm_bias.reshape(1, cols),
        out_weight,
        weights,
        cross_weight.reshape(D, 2 * head_cols),
        ctx_count,
        tp_count,
    )
    return (encoded, cross_kv.reshape(tok_rows, 2, head_cols))


def solution(mesh):
    placed = (
        P("ctx", "tp"),
        P("ctx", None, "tp"),
        P("ctx", "tp"),
        P("tp", None),
        P("tp"),
        P("tp"),
        P(None, None, "tp"),
        P("tp"),
        P(),
        P(),
    )
    return jax.shard_map(
        shards,
        mesh=mesh,
        in_specs=placed,
        out_specs=(P("ctx", "tp"), P("ctx", None, "tp")),
        check_vma=False,
    )
```

```python
import functools
import math

import jax
import jax.numpy as jnp
import numpy as np
from jax import lax
from jax.experimental import pallas as pl
from jax.experimental.pallas import tpu as pltpu
from jax.sharding import PartitionSpec as P

D = 4096
BLOCK = 64
MAXR = 3
G = 2
R = 3
SPAN = 2 * MAXR + 1
MESH = pl.DeviceIdType.MESH
VMEM = pltpu.VMEM
SMEM = pltpu.SMEM

norm_eps = 1e-05


def greet(axis, count):
    me = lax.axis_index(axis)
    barrier = pltpu.get_barrier_semaphore()

    def signal(k, carry):
        pl.semaphore_signal(
            barrier, inc=1, device_id={axis: lax.rem(me + k, count)}, device_id_type=MESH
        )
        return carry

    lax.fori_loop(1, count, signal, 0)
    pl.semaphore_wait(barrier, count - 1)


def edges_kernel(
    count,
    place_ref,
    kv_ref,
    q_ref,
    ext_ref,
    gkv_ref,
    gq_ref,
    cand,
    got,
    full,
    halo_send,
    halo_recv,
    send1,
    recv1,
    send2,
    recv2,
):
    me = lax.axis_index("ctx")
    blocks = kv_ref.shape[0]
    wide = kv_ref.shape[2]
    half = q_ref.shape[2]
    part = (wide + half) // 4
    greet("ctx", count)
    after = lax.rem(me + 1, count)
    before = lax.rem(me + count - 1, count)
    to_after = pltpu.make_async_remote_copy(
        src_ref=kv_ref.at[pl.ds(blocks - MAXR, MAXR)],
        dst_ref=ext_ref.at[pl.ds(0, MAXR)],
        send_sem=halo_send.at[0],
        recv_sem=halo_recv.at[0],
        device_id={"ctx": after},
        device_id_type=MESH,
    )
    to_before = pltpu.make_async_remote_copy(
        src_ref=kv_ref.at[pl.ds(0, MAXR)],
        dst_ref=ext_ref.at[pl.ds(blocks + MAXR, MAXR)],
        send_sem=halo_send.at[1],
        recv_sem=halo_recv.at[1],
        device_id={"ctx": before},
        device_id_type=MESH,
    )
    for g in range(G):
        local = place_ref[G + g]
        row = jnp.concatenate([kv_ref[local], q_ref[local]], axis=1)
        for r in range(4):
            for c in range(4):
                cand[(g * 4 + r) * 4 + c] = row[r * 16 : r * 16 + 16, c * part : (c + 1) * part]

    def first(k):
        to = lax.rem(me + k, count)
        return pltpu.make_async_remote_copy(
            src_ref=cand.at[to],
            dst_ref=got.at[me],
            send_sem=send1.at[k],
            recv_sem=recv1.at[k],
            device_id={"ctx": to},
            device_id_type=MESH,
        )

    def second(k):
        to = lax.rem(me + k, count)
        return pltpu.make_async_remote_copy(
            src_ref=full.at[me],
            dst_ref=full.at[me],
            send_sem=send2.at[k],
            recv_sem=recv2.at[k],
            device_id={"ctx": to},
            device_id_type=MESH,
        )

    def each(action):
        def body(k, carry):
            action(k)
            return carry

        lax.fori_loop(1, count, body, 0)

    each(lambda k: first(k).start())
    to_after.start()
    to_before.start()
    got[me] = cand[me]
    ext_ref[pl.ds(MAXR, blocks)] = kv_ref[...]
    each(lambda k: first(k).wait())
    full[me] = got[place_ref[me // (count // G)]]
    each(lambda k: second(k).start())
    each(lambda k: second(k).wait())
    for g in range(G):
        for r in range(4):
            row = jnp.concatenate([full[(g * 4 + r) * 4 + c] for c in range(4)], axis=1)
            gkv_ref[g, r * 16 : r * 16 + 16, :] = row[:, :wide]
            gq_ref[g, r * 16 : r * 16 + 16, :] = row[:, wide:]
    to_after.wait()
    to_before.wait()


def edges(place, kv, q, count):
    blocks, rows, wide = kv.shape
    half = q.shape[2]
    part = (wide + half) // 4
    return pl.pallas_call(
        functools.partial(edges_kernel, count),
        name="edges",
        out_shape=(
            jax.ShapeDtypeStruct((blocks + 2 * MAXR, rows, wide), kv.dtype),
            jax.ShapeDtypeStruct((G, rows, wide), kv.dtype),
            jax.ShapeDtypeStruct((G, rows, half), kv.dtype),
        ),
        in_specs=[
            pl.BlockSpec(memory_space=SMEM),
            pl.BlockSpec(memory_space=VMEM),
            pl.BlockSpec(memory_space=VMEM),
        ],
        out_specs=(pl.BlockSpec(memory_space=VMEM),) * 3,
        scratch_shapes=[
            VMEM((count, 16, part), kv.dtype),
            VMEM((count, 16, part), kv.dtype),
            VMEM((count, 16, part), kv.dtype),
            pltpu.SemaphoreType.DMA((2,)),
            pltpu.SemaphoreType.DMA((2,)),
            pltpu.SemaphoreType.DMA((count,)),
            pltpu.SemaphoreType.DMA((count,)),
            pltpu.SemaphoreType.DMA((count,)),
            pltpu.SemaphoreType.DMA((count,)),
        ],
        compiler_params=pltpu.CompilerParams(
            collective_id=0, has_side_effects=True, vmem_limit_bytes=48 * 2**20
        ),
    )(place, kv, q)


def far_kernel(scale, head_count, gq_ref, kv_ref, out_ref):
    blocks, rows, wide = kv_ref.shape
    size = wide // (2 * head_count)
    for h in range(head_count):
        lanes = slice(h * size, (h + 1) * size)
        q = gq_ref[:, :, lanes].reshape(G * rows, size)
        k = kv_ref[:, :, lanes].reshape(blocks * rows, size)
        v = kv_ref[:, :, wide // 2 + h * size : wide // 2 + (h + 1) * size].reshape(
            blocks * rows, size
        )
        s = (
            lax.dot_general(q, k, (((1,), (1,)), ((), ())), preferred_element_type=jnp.float32)
            * scale
        )
        peak = jnp.max(s, axis=1, keepdims=True)
        p = jnp.exp(s - peak)
        total = jnp.sum(p, axis=1, keepdims=True)
        acc = jnp.dot(p.astype(jnp.bfloat16), v, preferred_element_type=jnp.float32)
        peak = jnp.broadcast_to(peak, acc.shape)
        total = jnp.broadcast_to(total, acc.shape)
        for r in range(8):
            cut = slice(r * 16, r * 16 + 16)
            out_ref[h * 8 + r, 0:16, :] = acc[cut]
            out_ref[h * 8 + r, 16:32, :] = peak[cut]
            out_ref[h * 8 + r, 32:48, :] = total[cut]


def far_partials(gq, kv, scale, head_count, count):
    size = gq.shape[2] // head_count
    return pl.pallas_call(
        functools.partial(far_kernel, scale, head_count),
        name="far_partials",
        out_shape=jax.ShapeDtypeStruct((count, 48, size), jnp.float32),
        in_specs=[pl.BlockSpec(memory_space=VMEM)] * 2,
        out_specs=pl.BlockSpec(memory_space=VMEM),
        compiler_params=pltpu.CompilerParams(vmem_limit_bytes=48 * 2**20),
    )(gq, kv)


def exchange_kernel(
    count,
    slots,
    source_ref,
    kv_ref,
    part_ref,
    random_ref,
    far_ref,
    stage,
    got,
    bulk_send,
    bulk_recv,
    send1,
    recv1,
    send2,
    recv2,
    own_sem,
):
    me = lax.axis_index("ctx")
    greet("ctx", count)

    def first(k):
        to = lax.rem(me + k, count)
        return pltpu.make_async_remote_copy(
            src_ref=part_ref.at[to],
            dst_ref=got.at[me],
            send_sem=send1.at[k],
            recv_sem=recv1.at[k],
            device_id={"ctx": to},
            device_id_type=MESH,
        )

    def second(k):
        to = lax.rem(me + k, count)
        return pltpu.make_async_remote_copy(
            src_ref=far_ref.at[me],
            dst_ref=far_ref.at[me],
            send_sem=send2.at[k],
            recv_sem=recv2.at[k],
            device_id={"ctx": to},
            device_id_type=MESH,
        )

    def bulk(k):
        to = lax.rem(me + k, count)
        return pltpu.make_async_remote_copy(
            src_ref=stage.at[pl.ds(to * slots, slots)],
            dst_ref=random_ref.at[pl.ds(me * slots, slots)],
            send_sem=bulk_send.at[k],
            recv_sem=bulk_recv.at[k],
            device_id={"ctx": to},
            device_id_type=MESH,
        )

    def each(action):
        def body(k, carry):
            action(k)
            return carry

        lax.fori_loop(1, count, body, 0)

    each(lambda k: first(k).start())
    got[me] = part_ref[me]

    def place(i, carry):
        stage[i] = kv_ref[source_ref[i]]
        return carry

    lax.fori_loop(0, count * slots, place, 0)
    each(lambda k: bulk(k).start())
    own = pltpu.make_async_copy(
        stage.at[pl.ds(me * slots, slots)], random_ref.at[pl.ds(me * slots, slots)], own_sem
    )
    own.start()
    each(lambda k: first(k).wait())

    def top(i, so_far):
        return jnp.maximum(so_far, got[i, 16:32, :])

    peak = lax.fori_loop(1, count, top, got[0, 16:32, :])

    def add(i, so_far):
        acc, total = so_far
        factor = jnp.exp(got[i, 16:32, :] - peak)
        return acc + got[i, 0:16, :] * factor, total + got[i, 32:48, :] * factor

    zero = jnp.zeros_like(peak)
    acc, total = lax.fori_loop(0, count, add, (zero, zero))
    far_ref[me] = (acc / total).astype(far_ref.dtype)
    each(lambda k: second(k).start())
    own.wait()
    each(lambda k: bulk(k).wait())
    each(lambda k: second(k).wait())


def exchange(source, kv, partials, count, slots):
    blocks, rows, wide = kv.shape
    size = partials.shape[2]
    dma = pltpu.SemaphoreType.DMA((count,))
    return pl.pallas_call(
        functools.partial(exchange_kernel, count, slots),
        name="exchange",
        out_shape=(
            jax.ShapeDtypeStruct((count * slots, rows, wide), kv.dtype),
            jax.ShapeDtypeStruct((count, 16, size), kv.dtype),
        ),
        in_specs=[
            pl.BlockSpec(memory_space=SMEM),
            pl.BlockSpec(memory_space=VMEM),
            pl.BlockSpec(memory_space=VMEM),
        ],
        out_specs=(pl.BlockSpec(memory_space=pl.ANY), pl.BlockSpec(memory_space=VMEM)),
        scratch_shapes=[
            VMEM((count * slots, rows, wide), kv.dtype),
            VMEM((count, 48, size), jnp.float32),
            dma,
            dma,
            dma,
            dma,
            dma,
            dma,
            pltpu.SemaphoreType.DMA,
        ],
        compiler_params=pltpu.CompilerParams(
            collective_id=1, has_side_effects=True, vmem_limit_bytes=56 * 2**20
        ),
    )(source, kv, partials)


def attention_kernel(
    scale,
    head_count,
    all_blocks,
    index_ref,
    info_ref,
    q_ref,
    ext_ref,
    gkv_ref,
    far_ref,
    rand0,
    rand1,
    rand2,
    out_ref,
):
    b = pl.program_id(0)
    rows = q_ref.shape[1]
    wide = gkv_ref.shape[2]
    half = wide // 2
    size = half // head_count
    me = lax.axis_index("ctx")
    block = me * pl.num_programs(0) + b
    replaced = info_ref[head_count + b]
    near = SPAN * rows
    spot = lax.broadcasted_iota(jnp.int32, (rows, near), 1) // rows - MAXR
    inside = (spot + block >= 0) & (spot + block < all_blocks)
    for h in range(head_count):
        kl = slice(h * size, (h + 1) * size)
        vl = slice(half + h * size, half + (h + 1) * size)
        reach = info_ref[h]
        q = q_ref[0, :, kl]

        def listed(lanes):
            return jnp.concatenate(
                [
                    gkv_ref[0, :, lanes],
                    gkv_ref[1, :, lanes],
                    rand0[0, :, lanes],
                    rand1[0, :, lanes],
                    rand2[0, :, lanes],
                ],
                axis=0,
            )

        def score(keys):
            return (
                lax.dot_general(
                    q, keys, (((1,), (1,)), ((), ())), preferred_element_type=jnp.float32
                )
                * scale
            )

        window_k = ext_ref[pl.ds(b, SPAN), :, kl].reshape(near, size)
        window_v = ext_ref[pl.ds(b, SPAN), :, vl].reshape(near, size)
        s1 = jnp.where(inside & (jnp.abs(spot) <= reach), score(window_k), -jnp.inf)
        s2 = score(listed(kl))
        peak = jnp.maximum(
            jnp.max(s1, axis=1, keepdims=True), jnp.max(s2, axis=1, keepdims=True)
        )
        p1 = jnp.exp(s1 - peak)
        p2 = jnp.exp(s2 - peak)
        total = jnp.sum(p1, axis=1, keepdims=True) + jnp.sum(p2, axis=1, keepdims=True)
        acc = jnp.dot(p1.astype(jnp.bfloat16), window_v, preferred_element_type=jnp.float32)
        acc = acc + jnp.dot(
            p2.astype(jnp.bfloat16), listed(vl), preferred_element_type=jnp.float32
        )
        out_ref[0, :, kl] = (acc / total).astype(out_ref.dtype)

    for g in range(G):

        @pl.when(replaced == g)
        def _():
            for h in range(head_count):
                for r in range(4):
                    out_ref[0, r * 16 : r * 16 + 16, h * size : (h + 1) * size] = far_ref[
                        h * 8 + g * 4 + r
                    ]


def attention(index, info, q, ext, gkv, far, random, scale, head_count, all_blocks):
    blocks, rows, half = q.shape
    wide = 2 * half

    def whole(x):
        return pl.BlockSpec(x.shape, lambda b, *_: (0,) * x.ndim)

    def pick(r):
        return pl.BlockSpec((1, rows, wide), lambda b, index, info: (index[b * R + r], 0, 0))

    one = pl.BlockSpec((1, rows, half), lambda b, *_: (b, 0, 0))
    return pl.pallas_call(
        functools.partial(attention_kernel, scale, head_count, all_blocks),
        name="attention",
        grid_spec=pltpu.PrefetchScalarGridSpec(
            num_scalar_prefetch=2,
            grid=(blocks,),
            in_specs=[one, whole(ext), whole(gkv), whole(far), pick(0), pick(1), pick(2)],
            out_specs=one,
        ),
        out_shape=jax.ShapeDtypeStruct(q.shape, q.dtype),
        compiler_params=pltpu.CompilerParams(vmem_limit_bytes=48 * 2**20),
    )(index, info, q, ext, gkv, far, random, random, random)


def project_kernel(
    ctx_count,
    tp_count,
    chunks,
    width,
    att_ref,
    a1,
    a2,
    a3,
    residual_ref,
    gain_ref,
    bias_ref,
    w0,
    w1,
    w2,
    w3,
    cross_ref,
    encoded_ref,
    out_ref,
    w_all,
    cross,
    mixed,
    stats,
    g0,
    g1,
    g2,
    g3,
    w_sem,
    cross_sem,
    send_sem,
    recv_sem,
):
    ctx = lax.axis_index("ctx")
    tp = lax.axis_index("tp")
    mate = tp + 1 - 2 * lax.rem(tp, 2)
    over = lax.rem(tp + 2, tp_count)
    cater = tp_count - 1 - tp
    beyond = lax.rem(ctx + ctx_count // 2, ctx_count)
    rows = att_ref.shape[0] // chunks
    cols = residual_ref.shape[1]

    own_cols = w0.at[:, pl.ds(pl.multiple_of(tp * residual_ref.shape[1], residual_ref.shape[1]), residual_ref.shape[1])]
    for k, w in enumerate((own_cols, w1, w2, w3)):
        pltpu.make_async_copy(w, w_all.at[k], w_sem.at[k]).start()
    for k, block in enumerate((tp, mate, over, cater)):
        pltpu.make_async_copy(
            cross_ref.at[pl.ds(block * cols, cols)], cross.at[k], cross_sem.at[k]
        ).start()

    barrier = pltpu.get_barrier_semaphore()
    for other in (mate, over, cater):
        pl.semaphore_signal(barrier, inc=1, device_id={"tp": other}, device_id_type=MESH)
    pl.semaphore_signal(barrier, inc=1, device_id={"ctx": beyond}, device_id_type=MESH)
    pl.semaphore_wait(barrier, 4)

    def cut(c):
        return pl.ds(pl.multiple_of(c * rows, rows), rows)

    def hop(kind, c, src, dst, where):
        return pltpu.make_async_remote_copy(
            src_ref=src,
            dst_ref=dst,
            send_sem=send_sem.at[kind, c],
            recv_sem=recv_sem.at[kind, c],
            device_id=where,
            device_id_type=MESH,
        )

    def stat(c, k):
        other = (mate, over, cater)[k - 1]
        return hop(2 + k, c, stats.at[c, 0], stats.at[c, k], {"tp": other})

    def roll(c):
        return hop(6, c, encoded_ref.at[cut(c)], g0.at[cut(c)], {"ctx": beyond})

    def enc_mate(c):
        return hop(7, c, g0.at[cut(c)], g1.at[cut(c)], {"tp": mate})

    def enc_over(c):
        return hop(8, c, g0.at[cut(c)], g2.at[cut(c)], {"tp": over})

    def enc_on(c):
        return hop(9, c, g2.at[cut(c)], g3.at[cut(c)], {"tp": mate})

    for k, w in enumerate((own_cols, w1, w2, w3)):
        pltpu.make_async_copy(w, w_all.at[k], w_sem.at[k]).wait()

    def step(t, carry):
        def at(delay, body):
            c = t - delay

            @pl.when((c >= 0) & (c < chunks))
            def _():
                body(c)

        def relay_enc(c):
            roll(c).wait_recv()
            enc_over(c).start()
            enc_mate(c).start()

        def relay_on(c):
            enc_over(c).wait_recv()
            enc_on(c).start()

        def normalize(c):
            for k in (1, 2, 3):
                stat(c, k).wait_recv()
            both = stats[c, 0] + stats[c, 1] + stats[c, 2] + stats[c, 3]
            total = jnp.transpose(jnp.broadcast_to(both[0:1], (rows, rows)))[:, 0:1]
            square = jnp.transpose(jnp.broadcast_to(both[8:9], (rows, rows)))[:, 0:1]
            mean = total / width
            variance = square / width - mean * mean
            scaled = (mixed[cut(c), :] - mean) * lax.rsqrt(variance + norm_eps)
            encoded_ref[cut(c), :] = (
                scaled * gain_ref[...].astype(jnp.float32) + bias_ref[...].astype(jnp.float32)
            ).astype(encoded_ref.dtype)

        def mix(c):
            part = residual_ref[cut(c), :].astype(jnp.float32)
            for k, a in enumerate((att_ref, a1, a2, a3)):
                part = part + jnp.dot(
                    a[cut(c), :], w_all[k], preferred_element_type=jnp.float32
                )
            mixed[cut(c), :] = part
            lane = lax.broadcasted_iota(jnp.int32, (rows, rows), 1)
            total = jnp.sum(part, axis=1, keepdims=True)
            square = jnp.sum(part * part, axis=1, keepdims=True)
            turned = jnp.transpose(jnp.where(lane < rows // 2, total, square))
            stats[c, 0, 0:8, :] = turned[0:8]
            stats[c, 0, 8:16, :] = turned[rows // 2 : rows // 2 + 8]

        def cast(c):
            enc_mate(c).wait_recv()
            enc_on(c).wait_recv()
            acc = jnp.zeros((rows, out_ref.shape[1]), jnp.float32)
            for k, g in enumerate((g0, g1, g2, g3)):
                acc = acc + jnp.dot(g[cut(c), :], cross[k], preferred_element_type=jnp.float32)
            out_ref[cut(c), :] = acc.astype(out_ref.dtype)

        at(ROLL, relay_enc)
        at(ROLL + 1, relay_on)
        at(1, normalize)
        at(0, mix)

        def send_rows(c):
            roll(c).start()

        def send_stats(c):
            for k in (1, 2, 3):
                stat(c, k).start()

        at(1, send_rows)
        at(0, send_stats)

        @pl.when(t == ROLL + 2)
        def _():
            for k in range(4):
                pltpu.make_async_copy(
                    cross_ref.at[pl.ds(0, cols)], cross.at[k], cross_sem.at[k]
                ).wait()

        at(ROLL + 2, cast)
        return carry

    lax.fori_loop(0, chunks + ROLL + 2, step, 0)

    def finish(c, carry):
        for k in (1, 2, 3):
            stat(c, k).wait_send()
        roll(c).wait_send()
        enc_mate(c).wait_send()
        enc_over(c).wait_send()
        enc_on(c).wait_send()
        return carry

    lax.fori_loop(0, chunks, finish, 0)


ROLL = 3
CHUNKS = 6


def project(att, residual, gain, bias, out_weight, weights, cross_weight, ctx_count, tp_count):
    rows, depth = att[0].shape
    cols = residual.shape[1]
    wide = cross_weight.shape[1]
    vmem = pl.BlockSpec(memory_space=VMEM)
    hbm = pl.BlockSpec(memory_space=pl.ANY)
    kept = jnp.bfloat16
    return pl.pallas_call(
        functools.partial(project_kernel, ctx_count, tp_count, CHUNKS, cols * tp_count),
        name="project",
        out_shape=(
            jax.ShapeDtypeStruct((rows, cols), kept),
            jax.ShapeDtypeStruct((rows, wide), kept),
        ),
        in_specs=[vmem] * 7 + [hbm] * 5,
        out_specs=(vmem, vmem),
        scratch_shapes=[
            VMEM((4, depth, cols), kept),
            VMEM((4, cols, wide), kept),
            VMEM((rows, cols), jnp.float32),
            VMEM((CHUNKS, 4, 16, rows // CHUNKS), jnp.float32),
            VMEM((rows, cols), kept),
            VMEM((rows, cols), kept),
            VMEM((rows, cols), kept),
            VMEM((rows, cols), kept),
            pltpu.SemaphoreType.DMA((4,)),
            pltpu.SemaphoreType.DMA((4,)),
            pltpu.SemaphoreType.DMA((10, CHUNKS)),
            pltpu.SemaphoreType.DMA((10, CHUNKS)),
        ],
        compiler_params=pltpu.CompilerParams(
            collective_id=2, has_side_effects=True, vmem_limit_bytes=60 * 2**20
        ),
    )(*att, residual, gain, bias, out_weight, *weights, cross_weight)


FIRST = 14
SECOND = 12
LINE = 4
HEAD_COLS = 128


def front_kernel(
    count,
    scale,
    list_ref,
    kv_ref,
    q_ref,
    weight_ref,
    out_ref,
    w1_ref,
    w2_ref,
    w3_ref,
    a1_ref,
    a2_ref,
    a3_ref,
    ext,
    cand,
    got,
    full,
    gkv,
    gq,
    part,
    far_got,
    far,
    pool0,
    pool1,
    pool2,
    pool3,
    hold0,
    hold1,
    hold2,
    hold3,
    last0,
    last1,
    last2,
    last3,
    stage1,
    stage2,
    sums,
    stats,
    att_send,
    att_recv,
    pair_send,
    pair_recv,
    halo_send,
    halo_recv,
    weight_send,
    weight_recv,
    small_send,
    small_recv,
    bulk_send,
    bulk_recv,
):
    me = lax.axis_index("ctx")
    tp = lax.axis_index("tp")
    heads, blocks = ext.shape[0], kv_ref.shape[0]
    rows, pair = ext.shape[2:]
    size = pair // 2
    spot = (me // 8, lax.rem(me // 2, LINE))
    level = lax.rem(me, 2)
    twin = me + 1 - 2 * level
    mates = (tp + 1 - 2 * lax.rem(tp, 2), lax.rem(tp + 2, 4), 3 - tp)
    pools = (pool0, pool1, pool2, pool3)
    holds = (hold0, hold1, hold2, hold3)
    lasts = (last0, last1, last2, last3)
    wcols = w1_ref.shape[1]
    near = SPAN * rows

    barrier = pltpu.get_barrier_semaphore()

    def greeting(k, carry):
        pl.semaphore_signal(
            barrier, inc=1, device_id={"ctx": lax.rem(me + k, count)}, device_id_type=MESH
        )
        return carry

    lax.fori_loop(1, count, greeting, 0)
    for other in mates[:2]:
        pl.semaphore_signal(barrier, inc=1, device_id={"tp": other}, device_id_type=MESH)
    pl.semaphore_signal(
        barrier, inc=1, device_id={"ctx": twin, "tp": mates[2]}, device_id_type=MESH
    )

    def base(c):
        return HEADER + (c % 2) * ROUTE

    def along(c, stage, d):
        x, z = spot
        if (c + stage) % 2 == 0:
            x = lax.rem(x + d, LINE)
            return x, x * 8 + z * 2 + level
        z = lax.rem(z + d, LINE)
        return z, x * 8 + z * 2 + level

    def pair_copy(c):
        return pltpu.make_async_remote_copy(
            src_ref=ext.at[c, pl.ds(MAXR, blocks)],
            dst_ref=pools[c].at[pl.ds(level * blocks, blocks)],
            send_sem=pair_send.at[c],
            recv_sem=pair_recv.at[c],
            device_id={"ctx": twin},
            device_id_type=MESH,
        )

    def halo_copy(c):
        return pltpu.make_async_remote_copy(
            src_ref=pools[c].at[pl.ds((2 * blocks - MAXR) * (1 - level), MAXR)],
            dst_ref=ext.at[c, pl.ds((blocks + MAXR) * level, MAXR)],
            send_sem=halo_send.at[c],
            recv_sem=halo_recv.at[c],
            device_id={"ctx": lax.rem(me + 2 - 4 * level + count, count)},
            device_id_type=MESH,
        )

    def weight_copy(k):
        other = mates[k]
        return pltpu.make_async_remote_copy(
            src_ref=weight_ref.at[:, pl.ds(pl.multiple_of(other * wcols, wcols), wcols)],
            dst_ref=(w1_ref, w2_ref, w3_ref)[k],
            send_sem=weight_send.at[k],
            recv_sem=weight_recv.at[k],
            device_id={"tp": other} if k < 2 else {"ctx": twin, "tp": other},
            device_id_type=MESH,
        )

    def small(kind, k, scattered, src, dst):
        to = lax.rem(me + k, count)
        return pltpu.make_async_remote_copy(
            src_ref=src.at[to if scattered else me],
            dst_ref=dst.at[me],
            send_sem=small_send.at[kind, k],
            recv_sem=small_recv.at[kind, k],
            device_id={"ctx": to},
            device_id_type=MESH,
        )

    def bulk(c, stage, d):
        slots = (FIRST, SECOND)[stage]
        mine = spot[(c + stage) % 2]
        buffer = (stage1, stage2)[stage]
        return pltpu.make_async_remote_copy(
            src_ref=buffer.at[c, pl.ds((d - 1) * slots, slots)],
            dst_ref=(holds, lasts)[stage][c].at[pl.ds(mine * slots, slots)],
            send_sem=bulk_send.at[stage, c, d - 1],
            recv_sem=bulk_recv.at[stage, c, d - 1],
            device_id={"ctx": along(c, stage, d)[1]},
            device_id_type=MESH,
        )

    def each(action):
        def body(k, carry):
            action(k)
            return carry

        lax.fori_loop(1, count, body, 0)

    for g in range(G):
        local = list_ref[G + g]
        row = jnp.concatenate([kv_ref[local], q_ref[local]], axis=1)
        cut = row.shape[1] // 4
        for r in range(4):
            for s in range(4):
                cand[(g * 4 + r) * 4 + s] = row[r * 16 : r * 16 + 16, s * cut : (s + 1) * cut]
    for c in range(heads):
        for half in range(2):
            lanes = slice(half * size, (half + 1) * size)
            begin = half * heads * size + c * size
            own = kv_ref[:, :, begin : begin + size]
            pools[c][pl.ds(level * blocks, blocks), :, lanes] = own
            ext[c, pl.ds(MAXR, blocks), :, lanes] = own
    pl.semaphore_wait(barrier, count - 1 + 3)

    def scatter(c):
        pair_copy(c).wait()
        halo_copy(c).start()
        ext[c, pl.ds((blocks + MAXR) * (1 - level), MAXR)] = pools[c][
            pl.ds(blocks - MAXR * level, MAXR)
        ]
        for d in range(1, LINE):
            target, _ = along(c, 0, d)

            def fill(j, carry):
                source = list_ref[base(c) + target * STRIDE + j]
                stage1[c, (d - 1) * FIRST + j] = pools[c][source]
                return carry

            lax.fori_loop(0, FIRST, fill, 0, unroll=2)
        for d in (1, 3, 2):
            bulk(c, 0, d).start()

    def forward(c):
        for d in range(1, LINE):
            bulk(c, 0, d).wait()
        for d in range(1, LINE):
            target, _ = along(c, 1, d)

            def fill(j, carry):
                source = list_ref[base(c) + (LINE + target) * STRIDE + j]
                stage2[c, (d - 1) * SECOND + j] = jnp.where(
                    source < held,
                    pools[c][jnp.minimum(source, held - 1)],
                    holds[c][jnp.maximum(source - held, 0)],
                )
                return carry

            lax.fori_loop(0, SECOND, fill, 0, unroll=2)
        for d in (1, 3, 2):
            bulk(c, 1, d).start()

    held = 2 * blocks
    ended = held + LINE * FIRST

    place = lax.broadcasted_iota(jnp.int32, (rows, near), 1) // rows - MAXR
    left = lax.broadcasted_iota(jnp.int32, (rows, size), 1) < size // 2

    def score(q, keys):
        return (
            lax.dot_general(q, keys, (((1,), (1,)), ((), ())), preferred_element_type=jnp.float32)
            * scale
        )

    def nearby(c):
        halo_copy(c).wait()
        lanes = slice(c * size, (c + 1) * size)
        allowed = jnp.abs(place) <= list_ref[2 * G + c]
        g_k = gkv[:, :, c * size : (c + 1) * size].reshape(G * rows, size)
        g_v = gkv[:, :, (heads + c) * size : (heads + c + 1) * size].reshape(G * rows, size)

        def attend(b, carry):
            block = me * blocks + b
            inside = (place + block >= 0) & (place + block < count * blocks)
            q = q_ref[b, :, lanes]
            window = ext[c, pl.ds(b, SPAN)].reshape(near, pair)
            s1 = jnp.where(inside & allowed, score(q, window[:, :size]), -jnp.inf)
            s2 = score(q, g_k)
            peak = jnp.maximum(
                jnp.max(s1, axis=1, keepdims=True), jnp.max(s2, axis=1, keepdims=True)
            )
            p1 = jnp.exp(s1 - peak)
            p2 = jnp.exp(s2 - peak)
            total = jnp.sum(p1, axis=1, keepdims=True) + jnp.sum(p2, axis=1, keepdims=True)
            sums[c, b] = jnp.dot(
                p1.astype(jnp.bfloat16), window[:, size:], preferred_element_type=jnp.float32
            ) + jnp.dot(p2.astype(jnp.bfloat16), g_v, preferred_element_type=jnp.float32)
            stats[c, b] = jnp.where(left, peak, total)
            return carry

        lax.fori_loop(0, blocks, attend, 0)

    def distant(c):
        for d in range(1, LINE):
            bulk(c, 1, d).wait()
        lanes = slice(c * size, (c + 1) * size)
        swap = [
            jnp.concatenate([far[c * 8 + g * 4 + r] for r in range(4)], axis=0) for g in range(G)
        ]

        def attend(b, carry):
            q = q_ref[b, :, lanes]
            picked = []
            for r in range(R):
                at = list_ref[base(c) + 2 * LINE * STRIDE + b * R + r]
                picked.append(
                    jnp.where(
                        at < held,
                        pools[c][jnp.minimum(at, held - 1)],
                        jnp.where(
                            at < ended,
                            holds[c][jnp.clip(at - held, 0, LINE * FIRST - 1)],
                            lasts[c][jnp.maximum(at - ended, 0)],
                        ),
                    )
                )
            extra = jnp.concatenate(picked, axis=0)
            s2 = score(q, extra[:, :size])
            first_peak = stats[c, b, :, 0:1]
            peak = jnp.maximum(first_peak, jnp.max(s2, axis=1, keepdims=True))
            factor = jnp.exp(first_peak - peak)
            p2 = jnp.exp(s2 - peak)
            total = stats[c, b, :, size // 2 : size // 2 + 1] * factor + jnp.sum(
                p2, axis=1, keepdims=True
            )
            acc = sums[c, b] * factor + jnp.dot(
                p2.astype(jnp.bfloat16), extra[:, size:], preferred_element_type=jnp.float32
            )
            which = list_ref[2 * G + heads + b]
            result = (acc / total).astype(out_ref.dtype)
            out_ref[b, :, lanes] = jnp.where(
                which == 0, swap[0], jnp.where(which == 1, swap[1], result)
            )
            return carry

        lax.fori_loop(0, blocks, attend, 0)

    def att_copy(kind, c, src, dst, other):
        lanes = pl.ds(c * size, size)
        return pltpu.make_async_remote_copy(
            src_ref=src.at[:, :, lanes],
            dst_ref=dst.at[:, :, lanes],
            send_sem=att_send.at[kind, c],
            recv_sem=att_recv.at[kind, c],
            device_id={"tp": other},
            device_id_type=MESH,
        )

    def att_mate(c):
        return att_copy(0, c, out_ref, a1_ref, mates[0])

    def att_over(c):
        return att_copy(1, c, out_ref, a2_ref, mates[1])

    def att_on(c):
        return att_copy(2, c, a2_ref, a3_ref, mates[0])

    each(lambda k: small(0, k, True, cand, got).start())
    for c in range(heads):
        pair_copy(c).start()
    got[me] = cand[me]
    each(lambda k: small(0, k, True, cand, got).wait())
    full[me] = got[list_ref[me // (count // G)]]
    each(lambda k: small(1, k, False, full, full).start())
    scatter(0)
    scatter(1)

    each(lambda k: small(1, k, False, full, full).wait())
    for g in range(G):
        for r in range(4):
            row = jnp.concatenate([full[(g * 4 + r) * 4 + s] for s in range(4)], axis=1)
            gkv[g, r * 16 : r * 16 + 16, :] = row[:, : heads * pair]
            gq[g, r * 16 : r * 16 + 16, :] = row[:, heads * pair :]

    half_lane = lax.broadcasted_iota(jnp.int32, (G * rows, size), 1) < size // 2
    for h in range(heads):
        gq_h = gq[:, :, h * size : (h + 1) * size].reshape(G * rows, size)
        k_h = kv_ref[:, :, h * size : (h + 1) * size].reshape(blocks * rows, size)
        v_h = kv_ref[:, :, (heads + h) * size : (heads + h + 1) * size].reshape(
            blocks * rows, size
        )
        s = (
            lax.dot_general(gq_h, k_h, (((1,), (1,)), ((), ())), preferred_element_type=jnp.float32)
            * scale
        )
        peak = jnp.max(s, axis=1, keepdims=True)
        p = jnp.exp(s - peak)
        total = jnp.sum(p, axis=1, keepdims=True)
        acc = jnp.dot(p.astype(jnp.bfloat16), v_h, preferred_element_type=jnp.float32)
        both = jnp.where(half_lane, peak, total)
        for r in range(8):
            cut = slice(r * 16, r * 16 + 16)
            part[h * 8 + r, 0:16, :] = acc[cut]
            part[h * 8 + r, 16:32, :] = both[cut]
    far_got[me] = part[me]
    each(lambda k: small(2, k, True, part, far_got).start())
    scatter(2)
    scatter(3)
    for k in range(3):
        weight_copy(k).start()
    forward(0)
    nearby(0)
    forward(1)
    nearby(1)

    each(lambda k: small(2, k, True, part, far_got).wait())

    def top(i, so_far):
        return jnp.maximum(so_far, far_got[i, 16:32, 0:1])

    far_peak = lax.fori_loop(1, count, top, far_got[0, 16:32, 0:1], unroll=4)

    def add(i, so_far):
        acc, total = so_far
        factor = jnp.exp(far_got[i, 16:32, 0:1] - far_peak)
        return (
            acc + far_got[i, 0:16, :] * factor,
            total + far_got[i, 16:32, size // 2 : size // 2 + 1] * factor,
        )

    far_acc, far_total = lax.fori_loop(
        0, count, add, (jnp.zeros((16, size), jnp.float32), jnp.zeros((16, 1), jnp.float32)), unroll=4
    )
    far[me] = (far_acc / far_total).astype(far.dtype)
    each(lambda k: small(3, k, False, far, far).start())
    forward(2)
    forward(3)

    nearby(2)
    nearby(3)

    each(lambda k: small(3, k, False, far, far).wait())
    for c in range(heads):
        distant(c)
        if c > 0:
            att_over(c - 1).wait_recv()
            att_on(c - 1).start()
        att_over(c).start()
        att_mate(c).start()
    att_over(heads - 1).wait_recv()
    att_on(heads - 1).start()
    for c in range(heads):
        att_over(c).wait_send()
        att_mate(c).wait()
        att_on(c).wait()
    for k in range(3):
        weight_copy(k).wait()


def front(lists, kv, q, heads, weight, scale, count, tp_count):
    blocks, rows, wide = kv.shape
    pair = wide // heads
    size = pair // 2
    kept = kv.dtype
    vmem = pl.BlockSpec(memory_space=VMEM)
    hbm = pl.BlockSpec(memory_space=pl.ANY)
    cols = weight.shape[1] // tp_count
    moved = jax.ShapeDtypeStruct((weight.shape[0], cols), kept)
    same = jax.ShapeDtypeStruct(q.shape, kept)
    cut = (heads * pair + heads * size) // 4
    dma = pltpu.SemaphoreType.DMA
    return pl.pallas_call(
        functools.partial(front_kernel, count, scale),
        name="front",
        out_shape=(jax.ShapeDtypeStruct(q.shape, kept),) + (moved,) * 3 + (same,) * 3,
        in_specs=[pl.BlockSpec(memory_space=SMEM), vmem, vmem, hbm],
        out_specs=(vmem,) + (hbm,) * 6,
        scratch_shapes=[
            VMEM((heads, blocks + 2 * MAXR, rows, pair), kept),
            VMEM((count, 16, cut), kept),
            VMEM((count, 16, cut), kept),
            VMEM((count, 16, cut), kept),
            VMEM((G, rows, heads * pair), kept),
            VMEM((G, rows, heads * size), kept),
            VMEM((count, 32, size), jnp.float32),
            VMEM((count, 32, size), jnp.float32),
            VMEM((count, 16, size), kept),
        ]
        + [VMEM((2 * blocks, rows, pair), kept)] * heads
        + [VMEM((LINE * FIRST, rows, pair), kept)] * heads
        + [VMEM((LINE * SECOND, rows, pair), kept)] * heads
        + [
            VMEM((heads, (LINE - 1) * FIRST, rows, pair), kept),
            VMEM((heads, (LINE - 1) * SECOND, rows, pair), kept),
            VMEM((heads, blocks, rows, size), jnp.float32),
            VMEM((heads, blocks, rows, size), jnp.float32),
            dma((3, heads)),
            dma((3, heads)),
            dma((heads,)),
            dma((heads,)),
            dma((heads,)),
            dma((heads,)),
            dma((3,)),
            dma((3,)),
            dma((4, count)),
            dma((4, count)),
            dma((2, heads, LINE - 1)),
            dma((2, heads, LINE - 1)),
        ],
        compiler_params=pltpu.CompilerParams(
            collective_id=3, has_side_effects=True, vmem_limit_bytes=60 * 2**20
        ),
    )(lists, kv, q, weight)


STRIDE = 16
HEADER = 24
ROUTE = 2 * LINE * STRIDE + 40


def plan_kernel(count, blocks, row_ref, col_ref, req_ref, reqt_ref, reach_ref, gb_ref, out_ref):
    me = lax.axis_index("ctx")
    x, z, level = me // 8, lax.rem(me // 2, LINE), lax.rem(me, 2)
    many = 2 * blocks
    total = count * blocks
    low = jnp.bfloat16

    def iota(shape, dim):
        return lax.broadcasted_iota(jnp.int32, shape, dim)

    def product(a, b):
        return jnp.dot(a.astype(low), b.astype(low), preferred_element_type=jnp.float32)

    def flag(condition):
        return jnp.where(condition, 1.0, 0.0)

    ids = iota((count, total), 1)
    asked = jnp.zeros((count, total), jnp.float32)
    for e in range(blocks * R):
        asked = jnp.where(req_ref[:, e : e + 1] == ids, 1.0, asked)

    place = {"x": row_ref[0:1, :], "z": row_ref[1:2, :]}
    inner = row_ref[2:3, :].astype(jnp.float32)
    group = row_ref[3:4, :]
    place_col = {"x": col_ref[:, 0:1], "z": col_ref[:, 1:2]}
    group_col = col_ref[:, 3:4]
    before = iota((total, total), 0) < iota((total, total), 1)

    r8, s8 = iota((8, count), 0), iota((8, count), 1)
    where_of = {"x": s8 >> 3, "z": (s8 >> 1) & 3}
    lane = iota((8, 128), 1)
    line8 = iota((8, 128), 0) >> 1
    lane32 = iota((count, 128), 1)
    row32 = iota((count, 128), 0)
    own32 = {"x": row32 >> 3, "z": (row32 >> 1) & 3}
    pair_of = {"x": lane >> 2, "z": lane & 3}
    seats = flag(group_col == iota((total, 128), 1))
    longest = []
    for first, second in (("x", "z"), ("z", "x")):
        same = (where_of[first] == r8 >> 1) & ((s8 & 1) == (r8 & 1))
        need = flag(product(flag(same), asked) > 0)
        counts = product(need, seats)
        apart = (lane < LINE * LINE) & (pair_of[first] != line8)
        longest.append(jnp.max(jnp.where(apart, counts - FIRST, -1.0)))
        counts = product(asked, flag(place_col[second] == iota((total, 128), 1)))
        apart = (lane32 < LINE) & (lane32 != own32[second])
        longest.append(jnp.max(jnp.where(apart, counts - SECOND, -1.0)))
    over = jnp.maximum(
        jnp.maximum(longest[0], longest[1]), jnp.maximum(longest[2], longest[3])
    )

    head = iota((HEADER, 128), 0)
    top = jnp.where(head == 20, jnp.where(over > 0, 0, 1), 0)
    entries = []
    for g in range(G):
        entries.append((g, gb_ref[g] // blocks))
        entries.append((G + g, lax.rem(gb_ref[g], blocks)))
    for h in range(4):
        entries.append((2 * G + h, reach_ref[h]))
    for b in range(blocks):
        block = me * blocks + b
        which = jnp.where(block == gb_ref[0], 0, jnp.where(block == gb_ref[1], 1, -1))
        entries.append((2 * G + 4 + b, which))
    for k, value in entries:
        top = jnp.where(head == k, value, top)
    out_ref[0:HEADER, :] = top

    spots = {"x": x, "z": z}
    mine = (place["x"] == x) & (place["z"] == z)
    turn = iota((8, total), 0)
    asked_col = jnp.sum(
        jnp.where(iota(reqt_ref.shape, 1) == me, reqt_ref[...], 0), axis=1, keepdims=True
    )

    def store(offset, column):
        out_ref[offset : offset + column.shape[0], :] = jnp.broadcast_to(
            column.astype(jnp.int32), (column.shape[0], 128)
        )

    for o, (first, second) in enumerate((("x", "z"), ("z", "x"))):
        start = HEADER + o * ROUTE
        line_first = place[first].astype(jnp.float32)
        line_second = place[second].astype(jnp.float32)
        same = (where_of[first] == r8) & ((s8 & 1) == level)
        need = flag(product(flag(same), asked) > 0)
        rank = product(need, flag(before & (group_col == group)))
        slot = iota((STRIDE, total), 0).astype(jnp.float32)
        for t in range(LINE):
            hit = (need[t : t + 1] > 0) & mine & (rank[t : t + 1] == slot)
            column = jnp.sum(jnp.where(hit, inner, 0.0), axis=1, keepdims=True)
            store(start + t * STRIDE, column)
        my_rank = jnp.sum(jnp.where(turn == spots[first], rank, 0.0), axis=0, keepdims=True)
        found = jnp.where(
            place[first] == spots[first],
            inner,
            many + line_first * FIRST + jnp.minimum(my_rank, FIRST - 1),
        )
        line = (where_of[first] == spots[first]) & (where_of[second] == r8)
        here = product(flag(line & ((s8 & 1) == level)), asked)
        wanted = flag((here > 0) & (place[second] == spots[second]))
        rank = product(wanted, flag(before))
        for t in range(LINE):
            hit = (wanted[t : t + 1] > 0) & (rank[t : t + 1] == slot)
            column = jnp.sum(jnp.where(hit, found, 0.0), axis=1, keepdims=True)
            store(start + (LINE + t) * STRIDE, column)
        own = jnp.sum(jnp.where(turn == spots[second], here, 0.0), axis=0, keepdims=True)
        rank = product(
            jnp.broadcast_to(own, (8, total)),
            flag(before & (place_col[second] == place[second])),
        )[0:1]
        final = jnp.where(
            place[second] == spots[second],
            found,
            many + LINE * FIRST + line_second * SECOND + jnp.minimum(rank, SECOND - 1),
        )
        hit = asked_col == iota((reqt_ref.shape[0], total), 1)
        column = jnp.sum(jnp.where(hit, final, 0.0), axis=1, keepdims=True)
        store(start + 2 * LINE * STRIDE, column)


def plan(random_blocks, global_blocks, window_reach, blocks, count):
    requests = random_blocks.reshape(count, blocks * R)
    total = count * blocks
    ids = np.arange(total)
    table = np.zeros((8, total), np.int32)
    table[0] = ids // (LINE * 2 * blocks)
    table[1] = ids // (2 * blocks) % LINE
    table[2] = ids % (2 * blocks)
    table[3] = ids // (2 * blocks)
    turned = jnp.pad(requests.T, ((0, 40 - blocks * R), (0, 0)), constant_values=-1)
    vmem = pl.BlockSpec(memory_space=VMEM)
    smem = pl.BlockSpec(memory_space=SMEM)
    out = pl.pallas_call(
        functools.partial(plan_kernel, count, blocks),
        name="plan",
        out_shape=jax.ShapeDtypeStruct((HEADER + 2 * ROUTE, 128), jnp.int32),
        in_specs=[vmem] * 4 + [smem] * 2,
        out_specs=vmem,
        compiler_params=pltpu.CompilerParams(vmem_limit_bytes=48 * 2**20),
    )(table, np.ascontiguousarray(table.T), requests, turned, window_reach, global_blocks)
    return out[:, 0]


def direct(place, info, source_ids, my_index, kv, q, out_weight, scale, count, slots):
    block_count = q.shape[0]
    heads = info.shape[0] - block_count
    ext, gkv, gq = edges(place, kv, q, count)
    partials = far_partials(gq, kv, scale, heads, count)
    random, far = exchange(source_ids, kv, partials, count, slots)
    attended = attention(
        my_index, info, q, ext, gkv, far, random, scale, heads, count * block_count
    )
    tp = lax.axis_index("tp")
    tp_count = lax.axis_size("tp")
    cols = out_weight.shape[1] // tp_count
    mates = (tp, tp + 1 - 2 * lax.rem(tp, 2), lax.rem(tp + 2, tp_count), tp_count - 1 - tp)
    weights = []
    for k in range(1, tp_count):
        block = lax.dynamic_slice_in_dim(out_weight, mates[k] * cols, cols, axis=1)
        weights.append(lax.ppermute(block, "tp", [(i, i ^ k) for i in range(tp_count)]))
    for k in range(1, tp_count):
        weights.append(lax.ppermute(attended, "tp", [(i, i ^ k) for i in range(tp_count)]))
    return (attended, *weights)


def shards(
    queries,
    keyvals,
    residual,
    out_weight,
    norm_gain,
    norm_bias,
    cross_weight,
    window_reach,
    global_blocks,
    random_blocks,
):
    tok_rows, head_cols = queries.shape
    head_count = window_reach.shape[0]
    head_size = head_cols // head_count
    ctx_count = lax.axis_size("ctx")
    tp_count = lax.axis_size("tp")
    me = lax.axis_index("ctx")
    block_count = tok_rows // BLOCK
    scale = 1.0 / math.sqrt(head_size)
    q = queries.reshape(block_count, BLOCK, head_cols)
    kv = keyvals.reshape(block_count, BLOCK, 2 * head_cols)
    lists = plan(random_blocks, global_blocks, window_reach, block_count, ctx_count)
    fits = lists[20] > 0

    def staged(kv, q, out_weight):
        return tuple(front(lists, kv, q, head_count, out_weight, scale, ctx_count, tp_count))

    def plain(kv, q, out_weight):
        req_count = block_count * R
        slots = 1 + (req_count + ctx_count - 2) // ctx_count
        requests = random_blocks.reshape(ctx_count, req_count)
        owners = requests // block_count
        local_ids = requests % block_count
        positions = jnp.arange(req_count, dtype=jnp.int32)
        earlier = positions[None, :] < positions[:, None]
        ranks = jnp.sum(
            ((owners[:, :, None] == owners[:, None, :]) & earlier[None, :, :]).astype(jnp.int32),
            axis=2,
        )
        slot_ids = jnp.arange(slots, dtype=jnp.int32)
        matches = (owners[:, None, :] == me) & (ranks[:, None, :] == slot_ids[None, :, None])
        source_ids = jnp.sum(jnp.where(matches, local_ids[:, None, :], 0), axis=2).reshape(-1)
        my_index = lax.dynamic_index_in_dim(owners * slots + ranks, me, 0, keepdims=False)
        place = lists[: 2 * G]
        info = lists[2 * G : 2 * G + head_count + block_count]
        return direct(
            place, info, source_ids, my_index, kv, q, out_weight, scale, ctx_count, slots
        )

    attended, *rest = lax.cond(fits, staged, plain, kv, q, out_weight)
    weights = rest[: tp_count - 1]
    gathered = [x.reshape(tok_rows, head_cols) for x in [attended] + rest[tp_count - 1 :]]
    cols = residual.shape[1]
    encoded, cross_kv = project(
        gathered,
        residual,
        norm_gain.reshape(1, cols),
        norm_bias.reshape(1, cols),
        out_weight,
        weights,
        cross_weight.reshape(D, 2 * head_cols),
        ctx_count,
        tp_count,
    )
    return (encoded, cross_kv.reshape(tok_rows, 2, head_cols))


def solution(mesh):
    placed = (
        P("ctx", "tp"),
        P("ctx", None, "tp"),
        P("ctx", "tp"),
        P("tp", None),
        P("tp"),
        P("tp"),
        P(None, None, "tp"),
        P("tp"),
        P(),
        P(),
    )
    return jax.shard_map(
        shards,
        mesh=mesh,
        in_specs=placed,
        out_specs=(P("ctx", "tp"), P("ctx", None, "tp")),
        check_vma=False,
    )
```

```python
import functools
import math

import jax
import jax.numpy as jnp
import numpy as np
from jax import lax
from jax.experimental import pallas as pl
from jax.experimental.pallas import tpu as pltpu
from jax.sharding import PartitionSpec as P

D = 4096
BLOCK = 64
MAXR = 3
G = 2
R = 3
SPAN = 2 * MAXR + 1
MESH = pl.DeviceIdType.MESH
VMEM = pltpu.VMEM
SMEM = pltpu.SMEM

norm_eps = 1e-05


def greet(axis, count):
    me = lax.axis_index(axis)
    barrier = pltpu.get_barrier_semaphore()

    def signal(k, carry):
        pl.semaphore_signal(
            barrier, inc=1, device_id={axis: lax.rem(me + k, count)}, device_id_type=MESH
        )
        return carry

    lax.fori_loop(1, count, signal, 0)
    pl.semaphore_wait(barrier, count - 1)


def edges_kernel(
    count,
    place_ref,
    kv_ref,
    q_ref,
    ext_ref,
    gkv_ref,
    gq_ref,
    cand,
    got,
    full,
    halo_send,
    halo_recv,
    send1,
    recv1,
    send2,
    recv2,
):
    me = lax.axis_index("ctx")
    blocks = kv_ref.shape[0]
    wide = kv_ref.shape[2]
    half = q_ref.shape[2]
    part = (wide + half) // 4
    greet("ctx", count)
    after = lax.rem(me + 1, count)
    before = lax.rem(me + count - 1, count)
    to_after = pltpu.make_async_remote_copy(
        src_ref=kv_ref.at[pl.ds(blocks - MAXR, MAXR)],
        dst_ref=ext_ref.at[pl.ds(0, MAXR)],
        send_sem=halo_send.at[0],
        recv_sem=halo_recv.at[0],
        device_id={"ctx": after},
        device_id_type=MESH,
    )
    to_before = pltpu.make_async_remote_copy(
        src_ref=kv_ref.at[pl.ds(0, MAXR)],
        dst_ref=ext_ref.at[pl.ds(blocks + MAXR, MAXR)],
        send_sem=halo_send.at[1],
        recv_sem=halo_recv.at[1],
        device_id={"ctx": before},
        device_id_type=MESH,
    )
    for g in range(G):
        local = place_ref[G + g]
        row = jnp.concatenate([kv_ref[local], q_ref[local]], axis=1)
        for r in range(4):
            for c in range(4):
                cand[(g * 4 + r) * 4 + c] = row[r * 16 : r * 16 + 16, c * part : (c + 1) * part]

    def first(k):
        to = lax.rem(me + k, count)
        return pltpu.make_async_remote_copy(
            src_ref=cand.at[to],
            dst_ref=got.at[me],
            send_sem=send1.at[k],
            recv_sem=recv1.at[k],
            device_id={"ctx": to},
            device_id_type=MESH,
        )

    def second(k):
        to = lax.rem(me + k, count)
        return pltpu.make_async_remote_copy(
            src_ref=full.at[me],
            dst_ref=full.at[me],
            send_sem=send2.at[k],
            recv_sem=recv2.at[k],
            device_id={"ctx": to},
            device_id_type=MESH,
        )

    def each(action):
        def body(k, carry):
            action(k)
            return carry

        lax.fori_loop(1, count, body, 0)

    each(lambda k: first(k).start())
    to_after.start()
    to_before.start()
    got[me] = cand[me]
    ext_ref[pl.ds(MAXR, blocks)] = kv_ref[...]
    each(lambda k: first(k).wait())
    full[me] = got[place_ref[me // (count // G)]]
    each(lambda k: second(k).start())
    each(lambda k: second(k).wait())
    for g in range(G):
        for r in range(4):
            row = jnp.concatenate([full[(g * 4 + r) * 4 + c] for c in range(4)], axis=1)
            gkv_ref[g, r * 16 : r * 16 + 16, :] = row[:, :wide]
            gq_ref[g, r * 16 : r * 16 + 16, :] = row[:, wide:]
    to_after.wait()
    to_before.wait()


def edges(place, kv, q, count):
    blocks, rows, wide = kv.shape
    half = q.shape[2]
    part = (wide + half) // 4
    return pl.pallas_call(
        functools.partial(edges_kernel, count),
        name="edges",
        out_shape=(
            jax.ShapeDtypeStruct((blocks + 2 * MAXR, rows, wide), kv.dtype),
            jax.ShapeDtypeStruct((G, rows, wide), kv.dtype),
            jax.ShapeDtypeStruct((G, rows, half), kv.dtype),
        ),
        in_specs=[
            pl.BlockSpec(memory_space=SMEM),
            pl.BlockSpec(memory_space=VMEM),
            pl.BlockSpec(memory_space=VMEM),
        ],
        out_specs=(pl.BlockSpec(memory_space=VMEM),) * 3,
        scratch_shapes=[
            VMEM((count, 16, part), kv.dtype),
            VMEM((count, 16, part), kv.dtype),
            VMEM((count, 16, part), kv.dtype),
            pltpu.SemaphoreType.DMA((2,)),
            pltpu.SemaphoreType.DMA((2,)),
            pltpu.SemaphoreType.DMA((count,)),
            pltpu.SemaphoreType.DMA((count,)),
            pltpu.SemaphoreType.DMA((count,)),
            pltpu.SemaphoreType.DMA((count,)),
        ],
        compiler_params=pltpu.CompilerParams(
            collective_id=0, has_side_effects=True, vmem_limit_bytes=48 * 2**20
        ),
    )(place, kv, q)


def far_kernel(scale, head_count, gq_ref, kv_ref, out_ref):
    blocks, rows, wide = kv_ref.shape
    size = wide // (2 * head_count)
    for h in range(head_count):
        lanes = slice(h * size, (h + 1) * size)
        q = gq_ref[:, :, lanes].reshape(G * rows, size)
        k = kv_ref[:, :, lanes].reshape(blocks * rows, size)
        v = kv_ref[:, :, wide // 2 + h * size : wide // 2 + (h + 1) * size].reshape(
            blocks * rows, size
        )
        s = (
            lax.dot_general(q, k, (((1,), (1,)), ((), ())), preferred_element_type=jnp.float32)
            * scale
        )
        peak = jnp.max(s, axis=1, keepdims=True)
        p = jnp.exp(s - peak)
        total = jnp.sum(p, axis=1, keepdims=True)
        acc = jnp.dot(p.astype(jnp.bfloat16), v, preferred_element_type=jnp.float32)
        peak = jnp.broadcast_to(peak, acc.shape)
        total = jnp.broadcast_to(total, acc.shape)
        for r in range(8):
            cut = slice(r * 16, r * 16 + 16)
            out_ref[h * 8 + r, 0:16, :] = acc[cut]
            out_ref[h * 8 + r, 16:32, :] = peak[cut]
            out_ref[h * 8 + r, 32:48, :] = total[cut]


def far_partials(gq, kv, scale, head_count, count):
    size = gq.shape[2] // head_count
    return pl.pallas_call(
        functools.partial(far_kernel, scale, head_count),
        name="far_partials",
        out_shape=jax.ShapeDtypeStruct((count, 48, size), jnp.float32),
        in_specs=[pl.BlockSpec(memory_space=VMEM)] * 2,
        out_specs=pl.BlockSpec(memory_space=VMEM),
        compiler_params=pltpu.CompilerParams(vmem_limit_bytes=48 * 2**20),
    )(gq, kv)


def exchange_kernel(
    count,
    slots,
    source_ref,
    kv_ref,
    part_ref,
    random_ref,
    far_ref,
    stage,
    got,
    bulk_send,
    bulk_recv,
    send1,
    recv1,
    send2,
    recv2,
    own_sem,
):
    me = lax.axis_index("ctx")
    greet("ctx", count)

    def first(k):
        to = lax.rem(me + k, count)
        return pltpu.make_async_remote_copy(
            src_ref=part_ref.at[to],
            dst_ref=got.at[me],
            send_sem=send1.at[k],
            recv_sem=recv1.at[k],
            device_id={"ctx": to},
            device_id_type=MESH,
        )

    def second(k):
        to = lax.rem(me + k, count)
        return pltpu.make_async_remote_copy(
            src_ref=far_ref.at[me],
            dst_ref=far_ref.at[me],
            send_sem=send2.at[k],
            recv_sem=recv2.at[k],
            device_id={"ctx": to},
            device_id_type=MESH,
        )

    def bulk(k):
        to = lax.rem(me + k, count)
        return pltpu.make_async_remote_copy(
            src_ref=stage.at[pl.ds(to * slots, slots)],
            dst_ref=random_ref.at[pl.ds(me * slots, slots)],
            send_sem=bulk_send.at[k],
            recv_sem=bulk_recv.at[k],
            device_id={"ctx": to},
            device_id_type=MESH,
        )

    def each(action):
        def body(k, carry):
            action(k)
            return carry

        lax.fori_loop(1, count, body, 0)

    each(lambda k: first(k).start())
    got[me] = part_ref[me]

    def place(i, carry):
        stage[i] = kv_ref[source_ref[i]]
        return carry

    lax.fori_loop(0, count * slots, place, 0)
    each(lambda k: bulk(k).start())
    own = pltpu.make_async_copy(
        stage.at[pl.ds(me * slots, slots)], random_ref.at[pl.ds(me * slots, slots)], own_sem
    )
    own.start()
    each(lambda k: first(k).wait())

    def top(i, so_far):
        return jnp.maximum(so_far, got[i, 16:32, :])

    peak = lax.fori_loop(1, count, top, got[0, 16:32, :])

    def add(i, so_far):
        acc, total = so_far
        factor = jnp.exp(got[i, 16:32, :] - peak)
        return acc + got[i, 0:16, :] * factor, total + got[i, 32:48, :] * factor

    zero = jnp.zeros_like(peak)
    acc, total = lax.fori_loop(0, count, add, (zero, zero))
    far_ref[me] = (acc / total).astype(far_ref.dtype)
    each(lambda k: second(k).start())
    own.wait()
    each(lambda k: bulk(k).wait())
    each(lambda k: second(k).wait())


def exchange(source, kv, partials, count, slots):
    blocks, rows, wide = kv.shape
    size = partials.shape[2]
    dma = pltpu.SemaphoreType.DMA((count,))
    return pl.pallas_call(
        functools.partial(exchange_kernel, count, slots),
        name="exchange",
        out_shape=(
            jax.ShapeDtypeStruct((count * slots, rows, wide), kv.dtype),
            jax.ShapeDtypeStruct((count, 16, size), kv.dtype),
        ),
        in_specs=[
            pl.BlockSpec(memory_space=SMEM),
            pl.BlockSpec(memory_space=VMEM),
            pl.BlockSpec(memory_space=VMEM),
        ],
        out_specs=(pl.BlockSpec(memory_space=pl.ANY), pl.BlockSpec(memory_space=VMEM)),
        scratch_shapes=[
            VMEM((count * slots, rows, wide), kv.dtype),
            VMEM((count, 48, size), jnp.float32),
            dma,
            dma,
            dma,
            dma,
            dma,
            dma,
            pltpu.SemaphoreType.DMA,
        ],
        compiler_params=pltpu.CompilerParams(
            collective_id=1, has_side_effects=True, vmem_limit_bytes=56 * 2**20
        ),
    )(source, kv, partials)


def attention_kernel(
    scale,
    head_count,
    all_blocks,
    index_ref,
    info_ref,
    q_ref,
    ext_ref,
    gkv_ref,
    far_ref,
    rand0,
    rand1,
    rand2,
    out_ref,
):
    b = pl.program_id(0)
    rows = q_ref.shape[1]
    wide = gkv_ref.shape[2]
    half = wide // 2
    size = half // head_count
    me = lax.axis_index("ctx")
    block = me * pl.num_programs(0) + b
    replaced = info_ref[head_count + b]
    near = SPAN * rows
    spot = lax.broadcasted_iota(jnp.int32, (rows, near), 1) // rows - MAXR
    inside = (spot + block >= 0) & (spot + block < all_blocks)
    for h in range(head_count):
        kl = slice(h * size, (h + 1) * size)
        vl = slice(half + h * size, half + (h + 1) * size)
        reach = info_ref[h]
        q = q_ref[0, :, kl]

        def listed(lanes):
            return jnp.concatenate(
                [
                    gkv_ref[0, :, lanes],
                    gkv_ref[1, :, lanes],
                    rand0[0, :, lanes],
                    rand1[0, :, lanes],
                    rand2[0, :, lanes],
                ],
                axis=0,
            )

        def score(keys):
            return (
                lax.dot_general(
                    q, keys, (((1,), (1,)), ((), ())), preferred_element_type=jnp.float32
                )
                * scale
            )

        window_k = ext_ref[pl.ds(b, SPAN), :, kl].reshape(near, size)
        window_v = ext_ref[pl.ds(b, SPAN), :, vl].reshape(near, size)
        s1 = jnp.where(inside & (jnp.abs(spot) <= reach), score(window_k), -jnp.inf)
        s2 = score(listed(kl))
        peak = jnp.maximum(
            jnp.max(s1, axis=1, keepdims=True), jnp.max(s2, axis=1, keepdims=True)
        )
        p1 = jnp.exp(s1 - peak)
        p2 = jnp.exp(s2 - peak)
        total = jnp.sum(p1, axis=1, keepdims=True) + jnp.sum(p2, axis=1, keepdims=True)
        acc = jnp.dot(p1.astype(jnp.bfloat16), window_v, preferred_element_type=jnp.float32)
        acc = acc + jnp.dot(
            p2.astype(jnp.bfloat16), listed(vl), preferred_element_type=jnp.float32
        )
        out_ref[0, :, kl] = (acc / total).astype(out_ref.dtype)

    for g in range(G):

        @pl.when(replaced == g)
        def _():
            for h in range(head_count):
                for r in range(4):
                    out_ref[0, r * 16 : r * 16 + 16, h * size : (h + 1) * size] = far_ref[
                        h * 8 + g * 4 + r
                    ]


def attention(index, info, q, ext, gkv, far, random, scale, head_count, all_blocks):
    blocks, rows, half = q.shape
    wide = 2 * half

    def whole(x):
        return pl.BlockSpec(x.shape, lambda b, *_: (0,) * x.ndim)

    def pick(r):
        return pl.BlockSpec((1, rows, wide), lambda b, index, info: (index[b * R + r], 0, 0))

    one = pl.BlockSpec((1, rows, half), lambda b, *_: (b, 0, 0))
    return pl.pallas_call(
        functools.partial(attention_kernel, scale, head_count, all_blocks),
        name="attention",
        grid_spec=pltpu.PrefetchScalarGridSpec(
            num_scalar_prefetch=2,
            grid=(blocks,),
            in_specs=[one, whole(ext), whole(gkv), whole(far), pick(0), pick(1), pick(2)],
            out_specs=one,
        ),
        out_shape=jax.ShapeDtypeStruct(q.shape, q.dtype),
        compiler_params=pltpu.CompilerParams(vmem_limit_bytes=48 * 2**20),
    )(index, info, q, ext, gkv, far, random, random, random)


def project_kernel(
    ctx_count,
    tp_count,
    chunks,
    width,
    att_ref,
    a1,
    a2,
    a3,
    residual_ref,
    gain_ref,
    bias_ref,
    w0,
    w1,
    w2,
    w3,
    cross_ref,
    encoded_ref,
    out_ref,
    w_all,
    cross,
    mixed,
    stats,
    g0,
    g1,
    g2,
    g3,
    w_sem,
    cross_sem,
    send_sem,
    recv_sem,
):
    ctx = lax.axis_index("ctx")
    tp = lax.axis_index("tp")
    mate = tp + 1 - 2 * lax.rem(tp, 2)
    over = lax.rem(tp + 2, tp_count)
    cater = tp_count - 1 - tp
    beyond = lax.rem(ctx + ctx_count // 2, ctx_count)
    rows = att_ref.shape[0] // chunks
    cols = residual_ref.shape[1]

    own_cols = w0.at[:, pl.ds(pl.multiple_of(tp * residual_ref.shape[1], residual_ref.shape[1]), residual_ref.shape[1])]
    for k, w in enumerate((own_cols, w1, w2, w3)):
        pltpu.make_async_copy(w, w_all.at[k], w_sem.at[k]).start()
    for k, block in enumerate((tp, mate, over, cater)):
        pltpu.make_async_copy(
            cross_ref.at[pl.ds(block * cols, cols)], cross.at[k], cross_sem.at[k]
        ).start()

    barrier = pltpu.get_barrier_semaphore()
    for other in (mate, over, cater):
        pl.semaphore_signal(barrier, inc=1, device_id={"tp": other}, device_id_type=MESH)
    pl.semaphore_signal(barrier, inc=1, device_id={"ctx": beyond}, device_id_type=MESH)
    pl.semaphore_wait(barrier, 4)

    def cut(c):
        return pl.ds(pl.multiple_of(c * rows, rows), rows)

    def hop(kind, c, src, dst, where):
        return pltpu.make_async_remote_copy(
            src_ref=src,
            dst_ref=dst,
            send_sem=send_sem.at[kind, c],
            recv_sem=recv_sem.at[kind, c],
            device_id=where,
            device_id_type=MESH,
        )

    def stat(c, k):
        other = (mate, over, cater)[k - 1]
        return hop(2 + k, c, stats.at[c, 0], stats.at[c, k], {"tp": other})

    def roll(c):
        return hop(6, c, encoded_ref.at[cut(c)], g0.at[cut(c)], {"ctx": beyond})

    def enc_mate(c):
        return hop(7, c, g0.at[cut(c)], g1.at[cut(c)], {"tp": mate})

    def enc_over(c):
        return hop(8, c, g0.at[cut(c)], g2.at[cut(c)], {"tp": over})

    def enc_on(c):
        return hop(9, c, g2.at[cut(c)], g3.at[cut(c)], {"tp": mate})

    for k, w in enumerate((own_cols, w1, w2, w3)):
        pltpu.make_async_copy(w, w_all.at[k], w_sem.at[k]).wait()

    def step(t, carry):
        def at(delay, body):
            c = t - delay

            @pl.when((c >= 0) & (c < chunks))
            def _():
                body(c)

        def relay_enc(c):
            roll(c).wait_recv()
            enc_over(c).start()
            enc_mate(c).start()

        def relay_on(c):
            enc_over(c).wait_recv()
            enc_on(c).start()

        def normalize(c):
            for k in (1, 2, 3):
                stat(c, k).wait_recv()
            both = stats[c, 0] + stats[c, 1] + stats[c, 2] + stats[c, 3]
            total = jnp.transpose(jnp.broadcast_to(both[0:1], (rows, rows)))[:, 0:1]
            square = jnp.transpose(jnp.broadcast_to(both[8:9], (rows, rows)))[:, 0:1]
            mean = total / width
            variance = square / width - mean * mean
            scaled = (mixed[cut(c), :] - mean) * lax.rsqrt(variance + norm_eps)
            encoded_ref[cut(c), :] = (
                scaled * gain_ref[...].astype(jnp.float32) + bias_ref[...].astype(jnp.float32)
            ).astype(encoded_ref.dtype)

        def mix(c):
            part = residual_ref[cut(c), :].astype(jnp.float32)
            for k, a in enumerate((att_ref, a1, a2, a3)):
                part = part + jnp.dot(
                    a[cut(c), :], w_all[k], preferred_element_type=jnp.float32
                )
            mixed[cut(c), :] = part
            lane = lax.broadcasted_iota(jnp.int32, (rows, rows), 1)
            total = jnp.sum(part, axis=1, keepdims=True)
            square = jnp.sum(part * part, axis=1, keepdims=True)
            turned = jnp.transpose(jnp.where(lane < rows // 2, total, square))
            stats[c, 0, 0:8, :] = turned[0:8]
            stats[c, 0, 8:16, :] = turned[rows // 2 : rows // 2 + 8]

        def cast(c):
            enc_mate(c).wait_recv()
            enc_on(c).wait_recv()
            acc = jnp.zeros((rows, out_ref.shape[1]), jnp.float32)
            for k, g in enumerate((g0, g1, g2, g3)):
                acc = acc + jnp.dot(g[cut(c), :], cross[k], preferred_element_type=jnp.float32)
            out_ref[cut(c), :] = acc.astype(out_ref.dtype)

        at(ROLL, relay_enc)
        at(ROLL + 1, relay_on)
        at(1, normalize)
        at(0, mix)

        def send_rows(c):
            roll(c).start()

        def send_stats(c):
            for k in (1, 2, 3):
                stat(c, k).start()

        at(1, send_rows)
        at(0, send_stats)

        @pl.when(t == ROLL + 2)
        def _():
            for k in range(4):
                pltpu.make_async_copy(
                    cross_ref.at[pl.ds(0, cols)], cross.at[k], cross_sem.at[k]
                ).wait()

        at(ROLL + 2, cast)
        return carry

    lax.fori_loop(0, chunks + ROLL + 2, step, 0)

    def finish(c, carry):
        for k in (1, 2, 3):
            stat(c, k).wait_send()
        roll(c).wait_send()
        enc_mate(c).wait_send()
        enc_over(c).wait_send()
        enc_on(c).wait_send()
        return carry

    lax.fori_loop(0, chunks, finish, 0)


ROLL = 3
CHUNKS = 6


def project(att, residual, gain, bias, out_weight, weights, cross_weight, ctx_count, tp_count):
    rows, depth = att[0].shape
    cols = residual.shape[1]
    wide = cross_weight.shape[1]
    vmem = pl.BlockSpec(memory_space=VMEM)
    hbm = pl.BlockSpec(memory_space=pl.ANY)
    kept = jnp.bfloat16
    return pl.pallas_call(
        functools.partial(project_kernel, ctx_count, tp_count, CHUNKS, cols * tp_count),
        name="project",
        out_shape=(
            jax.ShapeDtypeStruct((rows, cols), kept),
            jax.ShapeDtypeStruct((rows, wide), kept),
        ),
        in_specs=[vmem] * 7 + [hbm] * 5,
        out_specs=(vmem, vmem),
        scratch_shapes=[
            VMEM((4, depth, cols), kept),
            VMEM((4, cols, wide), kept),
            VMEM((rows, cols), jnp.float32),
            VMEM((CHUNKS, 4, 16, rows // CHUNKS), jnp.float32),
            VMEM((rows, cols), kept),
            VMEM((rows, cols), kept),
            VMEM((rows, cols), kept),
            VMEM((rows, cols), kept),
            pltpu.SemaphoreType.DMA((4,)),
            pltpu.SemaphoreType.DMA((4,)),
            pltpu.SemaphoreType.DMA((10, CHUNKS)),
            pltpu.SemaphoreType.DMA((10, CHUNKS)),
        ],
        compiler_params=pltpu.CompilerParams(
            collective_id=2, has_side_effects=True, vmem_limit_bytes=60 * 2**20
        ),
    )(*att, residual, gain, bias, out_weight, *weights, cross_weight)


FIRST = 14
SECOND = 12
LINE = 4
HEAD_COLS = 128


def front_kernel(
    count,
    scale,
    list_ref,
    kv_ref,
    q_ref,
    weight_ref,
    out_ref,
    w1_ref,
    w2_ref,
    w3_ref,
    a1_ref,
    a2_ref,
    a3_ref,
    ext,
    cand,
    got,
    full,
    gkv,
    gq,
    part,
    far_got,
    far,
    pool0,
    pool1,
    pool2,
    pool3,
    pool4,
    pool5,
    pool6,
    pool7,
    hold0,
    hold1,
    hold2,
    hold3,
    hold4,
    hold5,
    hold6,
    hold7,
    last0,
    last1,
    last2,
    last3,
    last4,
    last5,
    last6,
    last7,
    stage1,
    stage2,
    sums,
    stats,
    att_send,
    att_recv,
    pair_send,
    pair_recv,
    halo_send,
    halo_recv,
    weight_send,
    weight_recv,
    small_send,
    small_recv,
    bulk_send,
    bulk_recv,
):
    me = lax.axis_index("ctx")
    tp = lax.axis_index("tp")
    units, blocks = ext.shape[0], kv_ref.shape[0]
    rows, size = ext.shape[2:]
    heads, pair = units // 2, 2 * size
    spot = (me // 8, lax.rem(me // 2, LINE))
    level = lax.rem(me, 2)
    twin = me + 1 - 2 * level
    mates = (tp + 1 - 2 * lax.rem(tp, 2), lax.rem(tp + 2, 4), 3 - tp)
    pools = (pool0, pool1, pool2, pool3, pool4, pool5, pool6, pool7)
    holds = (hold0, hold1, hold2, hold3, hold4, hold5, hold6, hold7)
    lasts = (last0, last1, last2, last3, last4, last5, last6, last7)
    wcols = w1_ref.shape[1]
    near = SPAN * rows

    barrier = pltpu.get_barrier_semaphore()

    def greeting(k, carry):
        pl.semaphore_signal(
            barrier, inc=1, device_id={"ctx": lax.rem(me + k, count)}, device_id_type=MESH
        )
        return carry

    lax.fori_loop(1, count, greeting, 0)
    for other in mates[:2]:
        pl.semaphore_signal(barrier, inc=1, device_id={"tp": other}, device_id_type=MESH)
    pl.semaphore_signal(
        barrier, inc=1, device_id={"ctx": twin, "tp": mates[2]}, device_id_type=MESH
    )

    def base(c):
        return HEADER + (c % 2) * ROUTE

    def along(c, stage, d):
        x, z = spot
        if (c + stage) % 2 == 0:
            x = lax.rem(x + d, LINE)
            return x, x * 8 + z * 2 + level
        z = lax.rem(z + d, LINE)
        return z, x * 8 + z * 2 + level

    def pair_copy(c):
        return pltpu.make_async_remote_copy(
            src_ref=ext.at[c, pl.ds(MAXR, blocks)],
            dst_ref=pools[c].at[pl.ds(level * blocks, blocks)],
            send_sem=pair_send.at[c],
            recv_sem=pair_recv.at[c],
            device_id={"ctx": twin},
            device_id_type=MESH,
        )

    def halo_copy(c):
        return pltpu.make_async_remote_copy(
            src_ref=pools[c].at[pl.ds((2 * blocks - MAXR) * (1 - level), MAXR)],
            dst_ref=ext.at[c, pl.ds((blocks + MAXR) * level, MAXR)],
            send_sem=halo_send.at[c],
            recv_sem=halo_recv.at[c],
            device_id={"ctx": lax.rem(me + 2 - 4 * level + count, count)},
            device_id_type=MESH,
        )

    def weight_copy(k):
        other = mates[k]
        return pltpu.make_async_remote_copy(
            src_ref=weight_ref.at[:, pl.ds(pl.multiple_of(other * wcols, wcols), wcols)],
            dst_ref=(w1_ref, w2_ref, w3_ref)[k],
            send_sem=weight_send.at[k],
            recv_sem=weight_recv.at[k],
            device_id={"tp": other} if k < 2 else {"ctx": twin, "tp": other},
            device_id_type=MESH,
        )

    def small(kind, k, scattered, src, dst):
        to = lax.rem(me + k, count)
        return pltpu.make_async_remote_copy(
            src_ref=src.at[to if scattered else me],
            dst_ref=dst.at[me],
            send_sem=small_send.at[kind, k],
            recv_sem=small_recv.at[kind, k],
            device_id={"ctx": to},
            device_id_type=MESH,
        )

    def bulk(c, stage, d):
        slots = (FIRST, SECOND)[stage]
        mine = spot[(c + stage) % 2]
        buffer = (stage1, stage2)[stage]
        return pltpu.make_async_remote_copy(
            src_ref=buffer.at[c, pl.ds((d - 1) * slots, slots)],
            dst_ref=(holds, lasts)[stage][c].at[pl.ds(mine * slots, slots)],
            send_sem=bulk_send.at[stage, c, d - 1],
            recv_sem=bulk_recv.at[stage, c, d - 1],
            device_id={"ctx": along(c, stage, d)[1]},
            device_id_type=MESH,
        )

    def each(action):
        def body(k, carry):
            action(k)
            return carry

        lax.fori_loop(1, count, body, 0)

    for g in range(G):
        local = list_ref[G + g]
        row = jnp.concatenate([kv_ref[local], q_ref[local]], axis=1)
        cut = row.shape[1] // 4
        for r in range(4):
            for s in range(4):
                cand[(g * 4 + r) * 4 + s] = row[r * 16 : r * 16 + 16, s * cut : (s + 1) * cut]
    for c in range(units):
        begin = (c % 2 * heads + c // 2) * size
        own = kv_ref[:, :, begin : begin + size]
        pools[c][pl.ds(level * blocks, blocks)] = own
        ext[c, pl.ds(MAXR, blocks)] = own
    pl.semaphore_wait(barrier, count - 1 + 3)

    def scatter(c):
        if c + 3 < units:
            pair_copy(c + 3).start()
        pair_copy(c).wait()
        halo_copy(c).start()
        ext[c, pl.ds((blocks + MAXR) * (1 - level), MAXR)] = pools[c][
            pl.ds(blocks - MAXR * level, MAXR)
        ]
        for d in range(1, LINE):
            target, _ = along(c, 0, d)

            def fill(j, carry):
                source = list_ref[base(c) + target * STRIDE + j]
                stage1[c, (d - 1) * FIRST + j] = pools[c][source]
                return carry

            lax.fori_loop(0, FIRST, fill, 0, unroll=2)
        for d in (1, 3, 2):
            bulk(c, 0, d).start()

    def forward(c):
        for d in range(1, LINE):
            bulk(c, 0, d).wait()
        for d in range(1, LINE):
            target, _ = along(c, 1, d)

            def fill(j, carry):
                source = list_ref[base(c) + (LINE + target) * STRIDE + j]
                stage2[c, (d - 1) * SECOND + j] = jnp.where(
                    source < held,
                    pools[c][jnp.minimum(source, held - 1)],
                    holds[c][jnp.maximum(source - held, 0)],
                )
                return carry

            lax.fori_loop(0, SECOND, fill, 0, unroll=2)
        for d in (1, 3, 2):
            bulk(c, 1, d).start()

    held = 2 * blocks
    ended = held + LINE * FIRST

    place = lax.broadcasted_iota(jnp.int32, (rows, near), 1) // rows - MAXR
    left = lax.broadcasted_iota(jnp.int32, (rows, size), 1) < size // 2

    def score(q, keys):
        return (
            lax.dot_general(q, keys, (((1,), (1,)), ((), ())), preferred_element_type=jnp.float32)
            * scale
        )

    def nearby(c):
        halo_copy(2 * c).wait()
        halo_copy(2 * c + 1).wait()
        lanes = slice(c * size, (c + 1) * size)
        allowed = jnp.abs(place) <= list_ref[2 * G + c]
        g_k = gkv[:, :, c * size : (c + 1) * size].reshape(G * rows, size)
        g_v = gkv[:, :, (heads + c) * size : (heads + c + 1) * size].reshape(G * rows, size)

        def attend(b, carry):
            block = me * blocks + b
            inside = (place + block >= 0) & (place + block < count * blocks)
            q = q_ref[b, :, lanes]
            window_k = ext[2 * c, pl.ds(b, SPAN)].reshape(near, size)
            window_v = ext[2 * c + 1, pl.ds(b, SPAN)].reshape(near, size)
            s1 = jnp.where(inside & allowed, score(q, window_k), -jnp.inf)
            s2 = score(q, g_k)
            peak = jnp.maximum(
                jnp.max(s1, axis=1, keepdims=True), jnp.max(s2, axis=1, keepdims=True)
            )
            p1 = jnp.exp(s1 - peak)
            p2 = jnp.exp(s2 - peak)
            total = jnp.sum(p1, axis=1, keepdims=True) + jnp.sum(p2, axis=1, keepdims=True)
            sums[c, b] = jnp.dot(
                p1.astype(jnp.bfloat16), window_v, preferred_element_type=jnp.float32
            ) + jnp.dot(p2.astype(jnp.bfloat16), g_v, preferred_element_type=jnp.float32)
            stats[c, b] = jnp.where(left, peak, total)
            return carry

        lax.fori_loop(0, blocks, attend, 0)

    def distant(c):
        for d in range(1, LINE):
            bulk(2 * c, 1, d).wait()
            bulk(2 * c + 1, 1, d).wait()
        lanes = slice(c * size, (c + 1) * size)
        swap = [
            jnp.concatenate([far[c * 8 + g * 4 + r] for r in range(4)], axis=0) for g in range(G)
        ]

        def collect(u, b):
            picked = []
            for r in range(R):
                at = list_ref[base(u) + 2 * LINE * STRIDE + b * R + r]
                picked.append(
                    jnp.where(
                        at < held,
                        pools[u][jnp.minimum(at, held - 1)],
                        jnp.where(
                            at < ended,
                            holds[u][jnp.clip(at - held, 0, LINE * FIRST - 1)],
                            lasts[u][jnp.maximum(at - ended, 0)],
                        ),
                    )
                )
            return jnp.concatenate(picked, axis=0)

        def attend(b, carry):
            q = q_ref[b, :, lanes]
            extra_v = collect(2 * c + 1, b)
            s2 = score(q, collect(2 * c, b))
            first_peak = stats[c, b, :, 0:1]
            peak = jnp.maximum(first_peak, jnp.max(s2, axis=1, keepdims=True))
            factor = jnp.exp(first_peak - peak)
            p2 = jnp.exp(s2 - peak)
            total = stats[c, b, :, size // 2 : size // 2 + 1] * factor + jnp.sum(
                p2, axis=1, keepdims=True
            )
            acc = sums[c, b] * factor + jnp.dot(
                p2.astype(jnp.bfloat16), extra_v, preferred_element_type=jnp.float32
            )
            which = list_ref[2 * G + heads + b]
            result = (acc / total).astype(out_ref.dtype)
            out_ref[b, :, lanes] = jnp.where(
                which == 0, swap[0], jnp.where(which == 1, swap[1], result)
            )
            return carry

        lax.fori_loop(0, blocks, attend, 0)

    def att_copy(kind, c, src, dst, other):
        lanes = pl.ds(c * size, size)
        return pltpu.make_async_remote_copy(
            src_ref=src.at[:, :, lanes],
            dst_ref=dst.at[:, :, lanes],
            send_sem=att_send.at[kind, c],
            recv_sem=att_recv.at[kind, c],
            device_id={"tp": other},
            device_id_type=MESH,
        )

    def att_mate(c):
        return att_copy(0, c, out_ref, a1_ref, mates[0])

    def att_over(c):
        return att_copy(1, c, out_ref, a2_ref, mates[1])

    def att_on(c):
        return att_copy(2, c, a2_ref, a3_ref, mates[0])

    each(lambda k: small(0, k, True, cand, got).start())
    for c in range(3):
        pair_copy(c).start()
    got[me] = cand[me]
    each(lambda k: small(0, k, True, cand, got).wait())
    full[me] = got[list_ref[me // (count // G)]]
    each(lambda k: small(1, k, False, full, full).start())
    for c in range(3):
        scatter(c)

    each(lambda k: small(1, k, False, full, full).wait())
    for g in range(G):
        for r in range(4):
            row = jnp.concatenate([full[(g * 4 + r) * 4 + s] for s in range(4)], axis=1)
            gkv[g, r * 16 : r * 16 + 16, :] = row[:, : heads * pair]
            gq[g, r * 16 : r * 16 + 16, :] = row[:, heads * pair :]

    half_lane = lax.broadcasted_iota(jnp.int32, (G * rows, size), 1) < size // 2
    for h in range(heads):
        gq_h = gq[:, :, h * size : (h + 1) * size].reshape(G * rows, size)
        k_h = kv_ref[:, :, h * size : (h + 1) * size].reshape(blocks * rows, size)
        v_h = kv_ref[:, :, (heads + h) * size : (heads + h + 1) * size].reshape(
            blocks * rows, size
        )
        s = (
            lax.dot_general(gq_h, k_h, (((1,), (1,)), ((), ())), preferred_element_type=jnp.float32)
            * scale
        )
        peak = jnp.max(s, axis=1, keepdims=True)
        p = jnp.exp(s - peak)
        total = jnp.sum(p, axis=1, keepdims=True)
        acc = jnp.dot(p.astype(jnp.bfloat16), v_h, preferred_element_type=jnp.float32)
        both = jnp.where(half_lane, peak, total)
        for r in range(8):
            cut = slice(r * 16, r * 16 + 16)
            part[h * 8 + r, 0:16, :] = acc[cut]
            part[h * 8 + r, 16:32, :] = both[cut]
    far_got[me] = part[me]
    each(lambda k: small(2, k, True, part, far_got).start())
    for c in range(3, units):
        scatter(c)
    for k in range(3):
        weight_copy(k).start()
    forward(0)
    forward(1)
    nearby(0)
    forward(2)
    forward(3)
    nearby(1)

    each(lambda k: small(2, k, True, part, far_got).wait())

    def top(i, so_far):
        return jnp.maximum(so_far, far_got[i, 16:32, 0:1])

    far_peak = lax.fori_loop(1, count, top, far_got[0, 16:32, 0:1], unroll=4)

    def add(i, so_far):
        acc, total = so_far
        factor = jnp.exp(far_got[i, 16:32, 0:1] - far_peak)
        return (
            acc + far_got[i, 0:16, :] * factor,
            total + far_got[i, 16:32, size // 2 : size // 2 + 1] * factor,
        )

    far_acc, far_total = lax.fori_loop(
        0, count, add, (jnp.zeros((16, size), jnp.float32), jnp.zeros((16, 1), jnp.float32)), unroll=4
    )
    far[me] = (far_acc / far_total).astype(far.dtype)
    each(lambda k: small(3, k, False, far, far).start())
    for c in range(heads, units):
        forward(c)

    nearby(2)
    nearby(3)

    each(lambda k: small(3, k, False, far, far).wait())
    for c in range(heads):
        distant(c)
        if c > 0:
            att_over(c - 1).wait_recv()
            att_on(c - 1).start()
        att_over(c).start()
        att_mate(c).start()
    att_over(heads - 1).wait_recv()
    att_on(heads - 1).start()
    for c in range(heads):
        att_over(c).wait_send()
        att_mate(c).wait()
        att_on(c).wait()
    for k in range(3):
        weight_copy(k).wait()


def front(lists, kv, q, heads, weight, scale, count, tp_count):
    blocks, rows, wide = kv.shape
    pair = wide // heads
    size = pair // 2
    kept = kv.dtype
    vmem = pl.BlockSpec(memory_space=VMEM)
    hbm = pl.BlockSpec(memory_space=pl.ANY)
    cols = weight.shape[1] // tp_count
    moved = jax.ShapeDtypeStruct((weight.shape[0], cols), kept)
    same = jax.ShapeDtypeStruct(q.shape, kept)
    cut = (heads * pair + heads * size) // 4
    dma = pltpu.SemaphoreType.DMA
    return pl.pallas_call(
        functools.partial(front_kernel, count, scale),
        name="front",
        out_shape=(jax.ShapeDtypeStruct(q.shape, kept),) + (moved,) * 3 + (same,) * 3,
        in_specs=[pl.BlockSpec(memory_space=SMEM), vmem, vmem, hbm],
        out_specs=(vmem,) + (hbm,) * 6,
        scratch_shapes=[
            VMEM((2 * heads, blocks + 2 * MAXR, rows, size), kept),
            VMEM((count, 16, cut), kept),
            VMEM((count, 16, cut), kept),
            VMEM((count, 16, cut), kept),
            VMEM((G, rows, heads * pair), kept),
            VMEM((G, rows, heads * size), kept),
            VMEM((count, 32, size), jnp.float32),
            VMEM((count, 32, size), jnp.float32),
            VMEM((count, 16, size), kept),
        ]
        + [VMEM((2 * blocks, rows, size), kept)] * (2 * heads)
        + [VMEM((LINE * FIRST, rows, size), kept)] * (2 * heads)
        + [VMEM((LINE * SECOND, rows, size), kept)] * (2 * heads)
        + [
            VMEM((2 * heads, (LINE - 1) * FIRST, rows, size), kept),
            VMEM((2 * heads, (LINE - 1) * SECOND, rows, size), kept),
            VMEM((heads, blocks, rows, size), jnp.float32),
            VMEM((heads, blocks, rows, size), jnp.float32),
            dma((3, heads)),
            dma((3, heads)),
            dma((2 * heads,)),
            dma((2 * heads,)),
            dma((2 * heads,)),
            dma((2 * heads,)),
            dma((3,)),
            dma((3,)),
            dma((4, count)),
            dma((4, count)),
            dma((2, 2 * heads, LINE - 1)),
            dma((2, 2 * heads, LINE - 1)),
        ],
        compiler_params=pltpu.CompilerParams(
            collective_id=3, has_side_effects=True, vmem_limit_bytes=60 * 2**20
        ),
    )(lists, kv, q, weight)


STRIDE = 16
HEADER = 24
ROUTE = 2 * LINE * STRIDE + 40


def plan_kernel(count, blocks, row_ref, col_ref, req_ref, reqt_ref, reach_ref, gb_ref, out_ref):
    me = lax.axis_index("ctx")
    x, z, level = me // 8, lax.rem(me // 2, LINE), lax.rem(me, 2)
    many = 2 * blocks
    total = count * blocks
    low = jnp.bfloat16

    def iota(shape, dim):
        return lax.broadcasted_iota(jnp.int32, shape, dim)

    def product(a, b):
        return jnp.dot(a.astype(low), b.astype(low), preferred_element_type=jnp.float32)

    def flag(condition):
        return jnp.where(condition, 1.0, 0.0)

    ids = iota((count, total), 1)
    asked = jnp.zeros((count, total), jnp.float32)
    for e in range(blocks * R):
        asked = jnp.where(req_ref[:, e : e + 1] == ids, 1.0, asked)

    place = {"x": row_ref[0:1, :], "z": row_ref[1:2, :]}
    inner = row_ref[2:3, :].astype(jnp.float32)
    group = row_ref[3:4, :]
    place_col = {"x": col_ref[:, 0:1], "z": col_ref[:, 1:2]}
    group_col = col_ref[:, 3:4]
    before = iota((total, total), 0) < iota((total, total), 1)

    r8, s8 = iota((8, count), 0), iota((8, count), 1)
    where_of = {"x": s8 >> 3, "z": (s8 >> 1) & 3}
    lane = iota((8, 128), 1)
    line8 = iota((8, 128), 0) >> 1
    lane32 = iota((count, 128), 1)
    row32 = iota((count, 128), 0)
    own32 = {"x": row32 >> 3, "z": (row32 >> 1) & 3}
    pair_of = {"x": lane >> 2, "z": lane & 3}
    seats = flag(group_col == iota((total, 128), 1))
    longest = []
    for first, second in (("x", "z"), ("z", "x")):
        same = (where_of[first] == r8 >> 1) & ((s8 & 1) == (r8 & 1))
        need = flag(product(flag(same), asked) > 0)
        counts = product(need, seats)
        apart = (lane < LINE * LINE) & (pair_of[first] != line8)
        longest.append(jnp.max(jnp.where(apart, counts - FIRST, -1.0)))
        counts = product(asked, flag(place_col[second] == iota((total, 128), 1)))
        apart = (lane32 < LINE) & (lane32 != own32[second])
        longest.append(jnp.max(jnp.where(apart, counts - SECOND, -1.0)))
    over = jnp.maximum(
        jnp.maximum(longest[0], longest[1]), jnp.maximum(longest[2], longest[3])
    )

    head = iota((HEADER, 128), 0)
    top = jnp.where(head == 20, jnp.where(over > 0, 0, 1), 0)
    entries = []
    for g in range(G):
        entries.append((g, gb_ref[g] // blocks))
        entries.append((G + g, lax.rem(gb_ref[g], blocks)))
    for h in range(4):
        entries.append((2 * G + h, reach_ref[h]))
    for b in range(blocks):
        block = me * blocks + b
        which = jnp.where(block == gb_ref[0], 0, jnp.where(block == gb_ref[1], 1, -1))
        entries.append((2 * G + 4 + b, which))
    for k, value in entries:
        top = jnp.where(head == k, value, top)
    out_ref[0:HEADER, :] = top

    spots = {"x": x, "z": z}
    mine = (place["x"] == x) & (place["z"] == z)
    turn = iota((8, total), 0)
    asked_col = jnp.sum(
        jnp.where(iota(reqt_ref.shape, 1) == me, reqt_ref[...], 0), axis=1, keepdims=True
    )

    def store(offset, column):
        out_ref[offset : offset + column.shape[0], :] = jnp.broadcast_to(
            column.astype(jnp.int32), (column.shape[0], 128)
        )

    for o, (first, second) in enumerate((("x", "z"), ("z", "x"))):
        start = HEADER + o * ROUTE
        line_first = place[first].astype(jnp.float32)
        line_second = place[second].astype(jnp.float32)
        same = (where_of[first] == r8) & ((s8 & 1) == level)
        need = flag(product(flag(same), asked) > 0)
        rank = product(need, flag(before & (group_col == group)))
        slot = iota((STRIDE, total), 0).astype(jnp.float32)
        for t in range(LINE):
            hit = (need[t : t + 1] > 0) & mine & (rank[t : t + 1] == slot)
            column = jnp.sum(jnp.where(hit, inner, 0.0), axis=1, keepdims=True)
            store(start + t * STRIDE, column)
        my_rank = jnp.sum(jnp.where(turn == spots[first], rank, 0.0), axis=0, keepdims=True)
        found = jnp.where(
            place[first] == spots[first],
            inner,
            many + line_first * FIRST + jnp.minimum(my_rank, FIRST - 1),
        )
        line = (where_of[first] == spots[first]) & (where_of[second] == r8)
        here = product(flag(line & ((s8 & 1) == level)), asked)
        wanted = flag((here > 0) & (place[second] == spots[second]))
        rank = product(wanted, flag(before))
        for t in range(LINE):
            hit = (wanted[t : t + 1] > 0) & (rank[t : t + 1] == slot)
            column = jnp.sum(jnp.where(hit, found, 0.0), axis=1, keepdims=True)
            store(start + (LINE + t) * STRIDE, column)
        own = jnp.sum(jnp.where(turn == spots[second], here, 0.0), axis=0, keepdims=True)
        rank = product(
            jnp.broadcast_to(own, (8, total)),
            flag(before & (place_col[second] == place[second])),
        )[0:1]
        final = jnp.where(
            place[second] == spots[second],
            found,
            many + LINE * FIRST + line_second * SECOND + jnp.minimum(rank, SECOND - 1),
        )
        hit = asked_col == iota((reqt_ref.shape[0], total), 1)
        column = jnp.sum(jnp.where(hit, final, 0.0), axis=1, keepdims=True)
        store(start + 2 * LINE * STRIDE, column)


def plan(random_blocks, global_blocks, window_reach, blocks, count):
    requests = random_blocks.reshape(count, blocks * R)
    total = count * blocks
    ids = np.arange(total)
    table = np.zeros((8, total), np.int32)
    table[0] = ids // (LINE * 2 * blocks)
    table[1] = ids // (2 * blocks) % LINE
    table[2] = ids % (2 * blocks)
    table[3] = ids // (2 * blocks)
    turned = jnp.pad(requests.T, ((0, 40 - blocks * R), (0, 0)), constant_values=-1)
    vmem = pl.BlockSpec(memory_space=VMEM)
    smem = pl.BlockSpec(memory_space=SMEM)
    out = pl.pallas_call(
        functools.partial(plan_kernel, count, blocks),
        name="plan",
        out_shape=jax.ShapeDtypeStruct((HEADER + 2 * ROUTE, 128), jnp.int32),
        in_specs=[vmem] * 4 + [smem] * 2,
        out_specs=vmem,
        compiler_params=pltpu.CompilerParams(vmem_limit_bytes=48 * 2**20),
    )(table, np.ascontiguousarray(table.T), requests, turned, window_reach, global_blocks)
    return out[:, 0]


def direct(place, info, source_ids, my_index, kv, q, out_weight, scale, count, slots):
    block_count = q.shape[0]
    heads = info.shape[0] - block_count
    ext, gkv, gq = edges(place, kv, q, count)
    partials = far_partials(gq, kv, scale, heads, count)
    random, far = exchange(source_ids, kv, partials, count, slots)
    attended = attention(
        my_index, info, q, ext, gkv, far, random, scale, heads, count * block_count
    )
    tp = lax.axis_index("tp")
    tp_count = lax.axis_size("tp")
    cols = out_weight.shape[1] // tp_count
    mates = (tp, tp + 1 - 2 * lax.rem(tp, 2), lax.rem(tp + 2, tp_count), tp_count - 1 - tp)
    weights = []
    for k in range(1, tp_count):
        block = lax.dynamic_slice_in_dim(out_weight, mates[k] * cols, cols, axis=1)
        weights.append(lax.ppermute(block, "tp", [(i, i ^ k) for i in range(tp_count)]))
    for k in range(1, tp_count):
        weights.append(lax.ppermute(attended, "tp", [(i, i ^ k) for i in range(tp_count)]))
    return (attended, *weights)


def shards(
    queries,
    keyvals,
    residual,
    out_weight,
    norm_gain,
    norm_bias,
    cross_weight,
    window_reach,
    global_blocks,
    random_blocks,
):
    tok_rows, head_cols = queries.shape
    head_count = window_reach.shape[0]
    head_size = head_cols // head_count
    ctx_count = lax.axis_size("ctx")
    tp_count = lax.axis_size("tp")
    me = lax.axis_index("ctx")
    block_count = tok_rows // BLOCK
    scale = 1.0 / math.sqrt(head_size)
    q = queries.reshape(block_count, BLOCK, head_cols)
    kv = keyvals.reshape(block_count, BLOCK, 2 * head_cols)
    lists = plan(random_blocks, global_blocks, window_reach, block_count, ctx_count)
    fits = lists[20] > 0

    def staged(kv, q, out_weight):
        return tuple(front(lists, kv, q, head_count, out_weight, scale, ctx_count, tp_count))

    def plain(kv, q, out_weight):
        req_count = block_count * R
        slots = 1 + (req_count + ctx_count - 2) // ctx_count
        requests = random_blocks.reshape(ctx_count, req_count)
        owners = requests // block_count
        local_ids = requests % block_count
        positions = jnp.arange(req_count, dtype=jnp.int32)
        earlier = positions[None, :] < positions[:, None]
        ranks = jnp.sum(
            ((owners[:, :, None] == owners[:, None, :]) & earlier[None, :, :]).astype(jnp.int32),
            axis=2,
        )
        slot_ids = jnp.arange(slots, dtype=jnp.int32)
        matches = (owners[:, None, :] == me) & (ranks[:, None, :] == slot_ids[None, :, None])
        source_ids = jnp.sum(jnp.where(matches, local_ids[:, None, :], 0), axis=2).reshape(-1)
        my_index = lax.dynamic_index_in_dim(owners * slots + ranks, me, 0, keepdims=False)
        place = lists[: 2 * G]
        info = lists[2 * G : 2 * G + head_count + block_count]
        return direct(
            place, info, source_ids, my_index, kv, q, out_weight, scale, ctx_count, slots
        )

    attended, *rest = lax.cond(fits, staged, plain, kv, q, out_weight)
    weights = rest[: tp_count - 1]
    gathered = [x.reshape(tok_rows, head_cols) for x in [attended] + rest[tp_count - 1 :]]
    cols = residual.shape[1]
    encoded, cross_kv = project(
        gathered,
        residual,
        norm_gain.reshape(1, cols),
        norm_bias.reshape(1, cols),
        out_weight,
        weights,
        cross_weight.reshape(D, 2 * head_cols),
        ctx_count,
        tp_count,
    )
    return (encoded, cross_kv.reshape(tok_rows, 2, head_cols))


def solution(mesh):
    placed = (
        P("ctx", "tp"),
        P("ctx", None, "tp"),
        P("ctx", "tp"),
        P("tp", None),
        P("tp"),
        P("tp"),
        P(None, None, "tp"),
        P("tp"),
        P(),
        P(),
    )
    return jax.shard_map(
        shards,
        mesh=mesh,
        in_specs=placed,
        out_specs=(P("ctx", "tp"), P("ctx", None, "tp")),
        check_vma=False,
    )
```

```python
import functools
import math

import jax
import jax.numpy as jnp
import numpy as np
from jax import lax
from jax.experimental import pallas as pl
from jax.experimental.pallas import tpu as pltpu
from jax.sharding import PartitionSpec as P

D = 4096
BLOCK = 64
MAXR = 3
G = 2
R = 3
SPAN = 2 * MAXR + 1
MESH = pl.DeviceIdType.MESH
VMEM = pltpu.VMEM
SMEM = pltpu.SMEM

norm_eps = 1e-05


def greet(axis, count):
    me = lax.axis_index(axis)
    barrier = pltpu.get_barrier_semaphore()

    def signal(k, carry):
        pl.semaphore_signal(
            barrier, inc=1, device_id={axis: lax.rem(me + k, count)}, device_id_type=MESH
        )
        return carry

    lax.fori_loop(1, count, signal, 0)
    pl.semaphore_wait(barrier, count - 1)


def edges_kernel(
    count,
    place_ref,
    kv_ref,
    q_ref,
    ext_ref,
    gkv_ref,
    gq_ref,
    cand,
    got,
    full,
    halo_send,
    halo_recv,
    send1,
    recv1,
    send2,
    recv2,
):
    me = lax.axis_index("ctx")
    blocks = kv_ref.shape[0]
    wide = kv_ref.shape[2]
    half = q_ref.shape[2]
    part = (wide + half) // 4
    greet("ctx", count)
    after = lax.rem(me + 1, count)
    before = lax.rem(me + count - 1, count)
    to_after = pltpu.make_async_remote_copy(
        src_ref=kv_ref.at[pl.ds(blocks - MAXR, MAXR)],
        dst_ref=ext_ref.at[pl.ds(0, MAXR)],
        send_sem=halo_send.at[0],
        recv_sem=halo_recv.at[0],
        device_id={"ctx": after},
        device_id_type=MESH,
    )
    to_before = pltpu.make_async_remote_copy(
        src_ref=kv_ref.at[pl.ds(0, MAXR)],
        dst_ref=ext_ref.at[pl.ds(blocks + MAXR, MAXR)],
        send_sem=halo_send.at[1],
        recv_sem=halo_recv.at[1],
        device_id={"ctx": before},
        device_id_type=MESH,
    )
    for g in range(G):
        local = place_ref[G + g]
        row = jnp.concatenate([kv_ref[local], q_ref[local]], axis=1)
        for r in range(4):
            for c in range(4):
                cand[(g * 4 + r) * 4 + c] = row[r * 16 : r * 16 + 16, c * part : (c + 1) * part]

    def first(k):
        to = lax.rem(me + k, count)
        return pltpu.make_async_remote_copy(
            src_ref=cand.at[to],
            dst_ref=got.at[me],
            send_sem=send1.at[k],
            recv_sem=recv1.at[k],
            device_id={"ctx": to},
            device_id_type=MESH,
        )

    def second(k):
        to = lax.rem(me + k, count)
        return pltpu.make_async_remote_copy(
            src_ref=full.at[me],
            dst_ref=full.at[me],
            send_sem=send2.at[k],
            recv_sem=recv2.at[k],
            device_id={"ctx": to},
            device_id_type=MESH,
        )

    def each(action):
        def body(k, carry):
            action(k)
            return carry

        lax.fori_loop(1, count, body, 0)

    each(lambda k: first(k).start())
    to_after.start()
    to_before.start()
    got[me] = cand[me]
    ext_ref[pl.ds(MAXR, blocks)] = kv_ref[...]
    each(lambda k: first(k).wait())
    full[me] = got[place_ref[me // (count // G)]]
    each(lambda k: second(k).start())
    each(lambda k: second(k).wait())
    for g in range(G):
        for r in range(4):
            row = jnp.concatenate([full[(g * 4 + r) * 4 + c] for c in range(4)], axis=1)
            gkv_ref[g, r * 16 : r * 16 + 16, :] = row[:, :wide]
            gq_ref[g, r * 16 : r * 16 + 16, :] = row[:, wide:]
    to_after.wait()
    to_before.wait()


def edges(place, kv, q, count):
    blocks, rows, wide = kv.shape
    half = q.shape[2]
    part = (wide + half) // 4
    return pl.pallas_call(
        functools.partial(edges_kernel, count),
        name="edges",
        out_shape=(
            jax.ShapeDtypeStruct((blocks + 2 * MAXR, rows, wide), kv.dtype),
            jax.ShapeDtypeStruct((G, rows, wide), kv.dtype),
            jax.ShapeDtypeStruct((G, rows, half), kv.dtype),
        ),
        in_specs=[
            pl.BlockSpec(memory_space=SMEM),
            pl.BlockSpec(memory_space=VMEM),
            pl.BlockSpec(memory_space=VMEM),
        ],
        out_specs=(pl.BlockSpec(memory_space=VMEM),) * 3,
        scratch_shapes=[
            VMEM((count, 16, part), kv.dtype),
            VMEM((count, 16, part), kv.dtype),
            VMEM((count, 16, part), kv.dtype),
            pltpu.SemaphoreType.DMA((2,)),
            pltpu.SemaphoreType.DMA((2,)),
            pltpu.SemaphoreType.DMA((count,)),
            pltpu.SemaphoreType.DMA((count,)),
            pltpu.SemaphoreType.DMA((count,)),
            pltpu.SemaphoreType.DMA((count,)),
        ],
        compiler_params=pltpu.CompilerParams(
            collective_id=0, has_side_effects=True, vmem_limit_bytes=48 * 2**20
        ),
    )(place, kv, q)


def far_kernel(scale, head_count, gq_ref, kv_ref, out_ref):
    blocks, rows, wide = kv_ref.shape
    size = wide // (2 * head_count)
    for h in range(head_count):
        lanes = slice(h * size, (h + 1) * size)
        q = gq_ref[:, :, lanes].reshape(G * rows, size)
        k = kv_ref[:, :, lanes].reshape(blocks * rows, size)
        v = kv_ref[:, :, wide // 2 + h * size : wide // 2 + (h + 1) * size].reshape(
            blocks * rows, size
        )
        s = (
            lax.dot_general(q, k, (((1,), (1,)), ((), ())), preferred_element_type=jnp.float32)
            * scale
        )
        peak = jnp.max(s, axis=1, keepdims=True)
        p = jnp.exp(s - peak)
        total = jnp.sum(p, axis=1, keepdims=True)
        acc = jnp.dot(p.astype(jnp.bfloat16), v, preferred_element_type=jnp.float32)
        peak = jnp.broadcast_to(peak, acc.shape)
        total = jnp.broadcast_to(total, acc.shape)
        for r in range(8):
            cut = slice(r * 16, r * 16 + 16)
            out_ref[h * 8 + r, 0:16, :] = acc[cut]
            out_ref[h * 8 + r, 16:32, :] = peak[cut]
            out_ref[h * 8 + r, 32:48, :] = total[cut]


def far_partials(gq, kv, scale, head_count, count):
    size = gq.shape[2] // head_count
    return pl.pallas_call(
        functools.partial(far_kernel, scale, head_count),
        name="far_partials",
        out_shape=jax.ShapeDtypeStruct((count, 48, size), jnp.float32),
        in_specs=[pl.BlockSpec(memory_space=VMEM)] * 2,
        out_specs=pl.BlockSpec(memory_space=VMEM),
        compiler_params=pltpu.CompilerParams(vmem_limit_bytes=48 * 2**20),
    )(gq, kv)


def exchange_kernel(
    count,
    slots,
    source_ref,
    kv_ref,
    part_ref,
    random_ref,
    far_ref,
    stage,
    got,
    bulk_send,
    bulk_recv,
    send1,
    recv1,
    send2,
    recv2,
    own_sem,
):
    me = lax.axis_index("ctx")
    greet("ctx", count)

    def first(k):
        to = lax.rem(me + k, count)
        return pltpu.make_async_remote_copy(
            src_ref=part_ref.at[to],
            dst_ref=got.at[me],
            send_sem=send1.at[k],
            recv_sem=recv1.at[k],
            device_id={"ctx": to},
            device_id_type=MESH,
        )

    def second(k):
        to = lax.rem(me + k, count)
        return pltpu.make_async_remote_copy(
            src_ref=far_ref.at[me],
            dst_ref=far_ref.at[me],
            send_sem=send2.at[k],
            recv_sem=recv2.at[k],
            device_id={"ctx": to},
            device_id_type=MESH,
        )

    def bulk(k):
        to = lax.rem(me + k, count)
        return pltpu.make_async_remote_copy(
            src_ref=stage.at[pl.ds(to * slots, slots)],
            dst_ref=random_ref.at[pl.ds(me * slots, slots)],
            send_sem=bulk_send.at[k],
            recv_sem=bulk_recv.at[k],
            device_id={"ctx": to},
            device_id_type=MESH,
        )

    def each(action):
        def body(k, carry):
            action(k)
            return carry

        lax.fori_loop(1, count, body, 0)

    each(lambda k: first(k).start())
    got[me] = part_ref[me]

    def place(i, carry):
        stage[i] = kv_ref[source_ref[i]]
        return carry

    lax.fori_loop(0, count * slots, place, 0)
    each(lambda k: bulk(k).start())
    own = pltpu.make_async_copy(
        stage.at[pl.ds(me * slots, slots)], random_ref.at[pl.ds(me * slots, slots)], own_sem
    )
    own.start()
    each(lambda k: first(k).wait())

    def top(i, so_far):
        return jnp.maximum(so_far, got[i, 16:32, :])

    peak = lax.fori_loop(1, count, top, got[0, 16:32, :])

    def add(i, so_far):
        acc, total = so_far
        factor = jnp.exp(got[i, 16:32, :] - peak)
        return acc + got[i, 0:16, :] * factor, total + got[i, 32:48, :] * factor

    zero = jnp.zeros_like(peak)
    acc, total = lax.fori_loop(0, count, add, (zero, zero))
    far_ref[me] = (acc / total).astype(far_ref.dtype)
    each(lambda k: second(k).start())
    own.wait()
    each(lambda k: bulk(k).wait())
    each(lambda k: second(k).wait())


def exchange(source, kv, partials, count, slots):
    blocks, rows, wide = kv.shape
    size = partials.shape[2]
    dma = pltpu.SemaphoreType.DMA((count,))
    return pl.pallas_call(
        functools.partial(exchange_kernel, count, slots),
        name="exchange",
        out_shape=(
            jax.ShapeDtypeStruct((count * slots, rows, wide), kv.dtype),
            jax.ShapeDtypeStruct((count, 16, size), kv.dtype),
        ),
        in_specs=[
            pl.BlockSpec(memory_space=SMEM),
            pl.BlockSpec(memory_space=VMEM),
            pl.BlockSpec(memory_space=VMEM),
        ],
        out_specs=(pl.BlockSpec(memory_space=pl.ANY), pl.BlockSpec(memory_space=VMEM)),
        scratch_shapes=[
            VMEM((count * slots, rows, wide), kv.dtype),
            VMEM((count, 48, size), jnp.float32),
            dma,
            dma,
            dma,
            dma,
            dma,
            dma,
            pltpu.SemaphoreType.DMA,
        ],
        compiler_params=pltpu.CompilerParams(
            collective_id=1, has_side_effects=True, vmem_limit_bytes=56 * 2**20
        ),
    )(source, kv, partials)


def attention_kernel(
    scale,
    head_count,
    all_blocks,
    index_ref,
    info_ref,
    q_ref,
    ext_ref,
    gkv_ref,
    far_ref,
    rand0,
    rand1,
    rand2,
    out_ref,
):
    b = pl.program_id(0)
    rows = q_ref.shape[1]
    wide = gkv_ref.shape[2]
    half = wide // 2
    size = half // head_count
    me = lax.axis_index("ctx")
    block = me * pl.num_programs(0) + b
    replaced = info_ref[head_count + b]
    near = SPAN * rows
    spot = lax.broadcasted_iota(jnp.int32, (rows, near), 1) // rows - MAXR
    inside = (spot + block >= 0) & (spot + block < all_blocks)
    for h in range(head_count):
        kl = slice(h * size, (h + 1) * size)
        vl = slice(half + h * size, half + (h + 1) * size)
        reach = info_ref[h]
        q = q_ref[0, :, kl]

        def listed(lanes):
            return jnp.concatenate(
                [
                    gkv_ref[0, :, lanes],
                    gkv_ref[1, :, lanes],
                    rand0[0, :, lanes],
                    rand1[0, :, lanes],
                    rand2[0, :, lanes],
                ],
                axis=0,
            )

        def score(keys):
            return (
                lax.dot_general(
                    q, keys, (((1,), (1,)), ((), ())), preferred_element_type=jnp.float32
                )
                * scale
            )

        window_k = ext_ref[pl.ds(b, SPAN), :, kl].reshape(near, size)
        window_v = ext_ref[pl.ds(b, SPAN), :, vl].reshape(near, size)
        s1 = jnp.where(inside & (jnp.abs(spot) <= reach), score(window_k), -jnp.inf)
        s2 = score(listed(kl))
        peak = jnp.maximum(
            jnp.max(s1, axis=1, keepdims=True), jnp.max(s2, axis=1, keepdims=True)
        )
        p1 = jnp.exp(s1 - peak)
        p2 = jnp.exp(s2 - peak)
        total = jnp.sum(p1, axis=1, keepdims=True) + jnp.sum(p2, axis=1, keepdims=True)
        acc = jnp.dot(p1.astype(jnp.bfloat16), window_v, preferred_element_type=jnp.float32)
        acc = acc + jnp.dot(
            p2.astype(jnp.bfloat16), listed(vl), preferred_element_type=jnp.float32
        )
        out_ref[0, :, kl] = (acc / total).astype(out_ref.dtype)

    for g in range(G):

        @pl.when(replaced == g)
        def _():
            for h in range(head_count):
                for r in range(4):
                    out_ref[0, r * 16 : r * 16 + 16, h * size : (h + 1) * size] = far_ref[
                        h * 8 + g * 4 + r
                    ]


def attention(index, info, q, ext, gkv, far, random, scale, head_count, all_blocks):
    blocks, rows, half = q.shape
    wide = 2 * half

    def whole(x):
        return pl.BlockSpec(x.shape, lambda b, *_: (0,) * x.ndim)

    def pick(r):
        return pl.BlockSpec((1, rows, wide), lambda b, index, info: (index[b * R + r], 0, 0))

    one = pl.BlockSpec((1, rows, half), lambda b, *_: (b, 0, 0))
    return pl.pallas_call(
        functools.partial(attention_kernel, scale, head_count, all_blocks),
        name="attention",
        grid_spec=pltpu.PrefetchScalarGridSpec(
            num_scalar_prefetch=2,
            grid=(blocks,),
            in_specs=[one, whole(ext), whole(gkv), whole(far), pick(0), pick(1), pick(2)],
            out_specs=one,
        ),
        out_shape=jax.ShapeDtypeStruct(q.shape, q.dtype),
        compiler_params=pltpu.CompilerParams(vmem_limit_bytes=48 * 2**20),
    )(index, info, q, ext, gkv, far, random, random, random)


def project_kernel(
    ctx_count,
    tp_count,
    chunks,
    width,
    att_ref,
    a1,
    a2,
    a3,
    residual_ref,
    gain_ref,
    bias_ref,
    w0,
    w1,
    w2,
    w3,
    cross_ref,
    encoded_ref,
    out_ref,
    w_all,
    raw,
    cross,
    mixed,
    stats,
    g0,
    g1,
    g2,
    g3,
    w_sem,
    cross_sem,
    send_sem,
    recv_sem,
):
    ctx = lax.axis_index("ctx")
    tp = lax.axis_index("tp")
    mate = tp + 1 - 2 * lax.rem(tp, 2)
    over = lax.rem(tp + 2, tp_count)
    cater = tp_count - 1 - tp
    beyond = lax.rem(ctx + ctx_count // 2, ctx_count)
    rows = att_ref.shape[0] // chunks
    cols = residual_ref.shape[1]

    own_cols = w0.at[:, pl.ds(pl.multiple_of(tp * residual_ref.shape[1], residual_ref.shape[1]), residual_ref.shape[1])]
    for k, w in enumerate((own_cols, w1, w2, w3)):
        pltpu.make_async_copy(w, w_all.at[k], w_sem.at[k]).start()
    for k, block in enumerate((tp, mate, over, cater)):
        pltpu.make_async_copy(
            cross_ref.at[pl.ds(block * cols, cols)], raw.at[k], cross_sem.at[k]
        ).start()

    barrier = pltpu.get_barrier_semaphore()
    for other in (mate, over, cater):
        pl.semaphore_signal(barrier, inc=1, device_id={"tp": other}, device_id_type=MESH)
    pl.semaphore_signal(barrier, inc=1, device_id={"ctx": beyond}, device_id_type=MESH)
    pl.semaphore_wait(barrier, 4)

    def cut(c):
        return pl.ds(pl.multiple_of(c * rows, rows), rows)

    def hop(kind, c, src, dst, where):
        return pltpu.make_async_remote_copy(
            src_ref=src,
            dst_ref=dst,
            send_sem=send_sem.at[kind, c],
            recv_sem=recv_sem.at[kind, c],
            device_id=where,
            device_id_type=MESH,
        )

    def stat(c, k):
        other = (mate, over, cater)[k - 1]
        return hop(2 + k, c, stats.at[c, 0], stats.at[c, k], {"tp": other})

    def roll(c):
        return hop(6, c, encoded_ref.at[cut(c)], g0.at[cut(c)], {"ctx": beyond})

    def enc_mate(c):
        return hop(7, c, g0.at[cut(c)], g1.at[cut(c)], {"tp": mate})

    def enc_over(c):
        return hop(8, c, g0.at[cut(c)], g2.at[cut(c)], {"tp": over})

    def enc_on(c):
        return hop(9, c, g2.at[cut(c)], g3.at[cut(c)], {"tp": mate})

    for k, w in enumerate((own_cols, w1, w2, w3)):
        pltpu.make_async_copy(w, w_all.at[k], w_sem.at[k]).wait()

    def step(t, carry):
        def at(delay, body):
            c = t - delay

            @pl.when((c >= 0) & (c < chunks))
            def _():
                body(c)

        def relay_enc(c):
            roll(c).wait_recv()
            enc_over(c).start()
            enc_mate(c).start()

        def relay_on(c):
            enc_over(c).wait_recv()
            enc_on(c).start()

        def normalize(c):
            for k in (1, 2, 3):
                stat(c, k).wait_recv()
            both = stats[c, 0] + stats[c, 1] + stats[c, 2] + stats[c, 3]
            total = jnp.transpose(jnp.broadcast_to(both[0:1], (rows, rows)))[:, 0:1]
            square = jnp.transpose(jnp.broadcast_to(both[8:9], (rows, rows)))[:, 0:1]
            mean = total / width
            variance = square / width - mean * mean
            scaled = (mixed[cut(c), :] - mean) * lax.rsqrt(variance + norm_eps)
            encoded_ref[cut(c), :] = (
                scaled * gain_ref[...].astype(jnp.float32) + bias_ref[...].astype(jnp.float32)
            ).astype(encoded_ref.dtype)

        def mix(c):
            part = residual_ref[cut(c), :].astype(jnp.float32)
            for k, a in enumerate((att_ref, a1, a2, a3)):
                part = part + jnp.dot(
                    a[cut(c), :], w_all[k], preferred_element_type=jnp.float32
                )
            mixed[cut(c), :] = part
            lane = lax.broadcasted_iota(jnp.int32, (rows, rows), 1)
            total = jnp.sum(part, axis=1, keepdims=True)
            square = jnp.sum(part * part, axis=1, keepdims=True)
            turned = jnp.transpose(jnp.where(lane < rows // 2, total, square))
            stats[c, 0, 0:8, :] = turned[0:8]
            stats[c, 0, 8:16, :] = turned[rows // 2 : rows // 2 + 8]

        def cast(c):
            enc_mate(c).wait_recv()
            enc_on(c).wait_recv()
            acc = jnp.zeros((rows, cross.shape[2]), jnp.float32)
            for k, g in enumerate((g0, g1, g2, g3)):
                acc = acc + jnp.dot(g[cut(c), :], cross[k], preferred_element_type=jnp.float32)
            out_ref[cut(c)] = acc.astype(out_ref.dtype).reshape(rows, 2, acc.shape[1] // 2)

        at(ROLL, relay_enc)
        at(ROLL + 1, relay_on)
        at(1, normalize)
        at(0, mix)

        def send_rows(c):
            roll(c).start()

        def send_stats(c):
            for k in (1, 2, 3):
                stat(c, k).start()

        at(1, send_rows)
        at(0, send_stats)

        for i in range(3):
            piece = t * 3 + i

            @pl.when(piece < 4 * PIECES)
            def _():
                k = piece // PIECES

                @pl.when(lax.rem(piece, PIECES) == 0)
                def _():
                    pltpu.make_async_copy(
                        cross_ref.at[pl.ds(0, cols)], raw.at[k], cross_sem.at[k]
                    ).wait()

                span = cols // PIECES
                some = pl.ds(pl.multiple_of(lax.rem(piece, PIECES) * span, span), span)
                cross[k, some] = raw[k, some].reshape(span, cross.shape[2])

        at(ROLL + 2, cast)
        return carry

    lax.fori_loop(0, chunks + ROLL + 2, step, 0)

    def finish(c, carry):
        for k in (1, 2, 3):
            stat(c, k).wait_send()
        roll(c).wait_send()
        enc_mate(c).wait_send()
        enc_over(c).wait_send()
        enc_on(c).wait_send()
        return carry

    lax.fori_loop(0, chunks, finish, 0)


ROLL = 3
PIECES = 4
CHUNKS = 6


def project(att, residual, gain, bias, out_weight, weights, cross_weight, ctx_count, tp_count):
    rows, depth = att[0].shape
    cols = residual.shape[1]
    half = cross_weight.shape[2]
    wide = 2 * half
    vmem = pl.BlockSpec(memory_space=VMEM)
    hbm = pl.BlockSpec(memory_space=pl.ANY)
    kept = jnp.bfloat16
    return pl.pallas_call(
        functools.partial(project_kernel, ctx_count, tp_count, CHUNKS, cols * tp_count),
        name="project",
        out_shape=(
            jax.ShapeDtypeStruct((rows, cols), kept),
            jax.ShapeDtypeStruct((rows, 2, half), kept),
        ),
        in_specs=[vmem] * 7 + [hbm] * 5,
        out_specs=(vmem, vmem),
        scratch_shapes=[
            VMEM((4, depth, cols), kept),
            VMEM((4, cols, 2, half), kept),
            VMEM((4, cols, wide), kept),
            VMEM((rows, cols), jnp.float32),
            VMEM((CHUNKS, 4, 16, rows // CHUNKS), jnp.float32),
            VMEM((rows, cols), kept),
            VMEM((rows, cols), kept),
            VMEM((rows, cols), kept),
            VMEM((rows, cols), kept),
            pltpu.SemaphoreType.DMA((4,)),
            pltpu.SemaphoreType.DMA((4,)),
            pltpu.SemaphoreType.DMA((10, CHUNKS)),
            pltpu.SemaphoreType.DMA((10, CHUNKS)),
        ],
        compiler_params=pltpu.CompilerParams(
            collective_id=2, has_side_effects=True, vmem_limit_bytes=60 * 2**20
        ),
    )(*att, residual, gain, bias, out_weight, *weights, cross_weight)


FIRST = 14
SECOND = 12
LINE = 4
HEAD_COLS = 128


def front_kernel(
    count,
    scale,
    list_ref,
    raw_ref,
    q_ref,
    weight_ref,
    out_ref,
    w1_ref,
    w2_ref,
    w3_ref,
    a1_ref,
    a2_ref,
    a3_ref,
    kv_ref,
    ext,
    cand,
    got,
    full,
    gkv,
    gq,
    part,
    far_got,
    far,
    pool0,
    pool1,
    pool2,
    pool3,
    pool4,
    pool5,
    pool6,
    pool7,
    hold0,
    hold1,
    hold2,
    hold3,
    hold4,
    hold5,
    hold6,
    hold7,
    last0,
    last1,
    last2,
    last3,
    last4,
    last5,
    last6,
    last7,
    stage1,
    stage2,
    sums,
    stats,
    att_send,
    att_recv,
    pair_send,
    pair_recv,
    halo_send,
    halo_recv,
    weight_send,
    weight_recv,
    small_send,
    small_recv,
    bulk_send,
    bulk_recv,
):
    me = lax.axis_index("ctx")
    tp = lax.axis_index("tp")
    units, blocks = ext.shape[0], kv_ref.shape[0]
    rows, size = ext.shape[2:]
    heads, pair = units // 2, 2 * size
    spot = (me // 8, lax.rem(me // 2, LINE))
    level = lax.rem(me, 2)
    twin = me + 1 - 2 * level
    mates = (tp + 1 - 2 * lax.rem(tp, 2), lax.rem(tp + 2, 4), 3 - tp)
    pools = (pool0, pool1, pool2, pool3, pool4, pool5, pool6, pool7)
    holds = (hold0, hold1, hold2, hold3, hold4, hold5, hold6, hold7)
    lasts = (last0, last1, last2, last3, last4, last5, last6, last7)
    wcols = w1_ref.shape[1]
    near = SPAN * rows

    barrier = pltpu.get_barrier_semaphore()

    def greeting(k, carry):
        pl.semaphore_signal(
            barrier, inc=1, device_id={"ctx": lax.rem(me + k, count)}, device_id_type=MESH
        )
        return carry

    lax.fori_loop(1, count, greeting, 0)
    for other in mates[:2]:
        pl.semaphore_signal(barrier, inc=1, device_id={"tp": other}, device_id_type=MESH)
    pl.semaphore_signal(
        barrier, inc=1, device_id={"ctx": twin, "tp": mates[2]}, device_id_type=MESH
    )

    def base(c):
        return HEADER + (c % 2) * ROUTE

    def along(c, stage, d):
        x, z = spot
        if (c + stage) % 2 == 0:
            x = lax.rem(x + d, LINE)
            return x, x * 8 + z * 2 + level
        z = lax.rem(z + d, LINE)
        return z, x * 8 + z * 2 + level

    def pair_copy(c):
        return pltpu.make_async_remote_copy(
            src_ref=ext.at[c, pl.ds(MAXR, blocks)],
            dst_ref=pools[c].at[pl.ds(level * blocks, blocks)],
            send_sem=pair_send.at[c],
            recv_sem=pair_recv.at[c],
            device_id={"ctx": twin},
            device_id_type=MESH,
        )

    def halo_copy(c):
        return pltpu.make_async_remote_copy(
            src_ref=pools[c].at[pl.ds((2 * blocks - MAXR) * (1 - level), MAXR)],
            dst_ref=ext.at[c, pl.ds((blocks + MAXR) * level, MAXR)],
            send_sem=halo_send.at[c],
            recv_sem=halo_recv.at[c],
            device_id={"ctx": lax.rem(me + 2 - 4 * level + count, count)},
            device_id_type=MESH,
        )

    def weight_copy(k):
        other = mates[k]
        return pltpu.make_async_remote_copy(
            src_ref=weight_ref.at[:, pl.ds(pl.multiple_of(other * wcols, wcols), wcols)],
            dst_ref=(w1_ref, w2_ref, w3_ref)[k],
            send_sem=weight_send.at[k],
            recv_sem=weight_recv.at[k],
            device_id={"tp": other} if k < 2 else {"ctx": twin, "tp": other},
            device_id_type=MESH,
        )

    def small(kind, k, scattered, src, dst):
        to = lax.rem(me + k, count)
        return pltpu.make_async_remote_copy(
            src_ref=src.at[to if scattered else me],
            dst_ref=dst.at[me],
            send_sem=small_send.at[kind, k],
            recv_sem=small_recv.at[kind, k],
            device_id={"ctx": to},
            device_id_type=MESH,
        )

    def bulk(c, stage, d):
        slots = (FIRST, SECOND)[stage]
        mine = spot[(c + stage) % 2]
        buffer = (stage1, stage2)[stage]
        return pltpu.make_async_remote_copy(
            src_ref=buffer.at[c, pl.ds((d - 1) * slots, slots)],
            dst_ref=(holds, lasts)[stage][c].at[pl.ds(mine * slots, slots)],
            send_sem=bulk_send.at[stage, c, d - 1],
            recv_sem=bulk_recv.at[stage, c, d - 1],
            device_id={"ctx": along(c, stage, d)[1]},
            device_id_type=MESH,
        )

    def each(action):
        def body(k, carry):
            action(k)
            return carry

        lax.fori_loop(1, count, body, 0)

    for b in range(blocks):
        kv_ref[b] = raw_ref[b * rows : (b + 1) * rows].reshape(rows, heads * pair)
    for g in range(G):
        local = list_ref[G + g]
        row = jnp.concatenate([kv_ref[local], q_ref[local]], axis=1)
        cut = row.shape[1] // 4
        for r in range(4):
            for s in range(4):
                cand[(g * 4 + r) * 4 + s] = row[r * 16 : r * 16 + 16, s * cut : (s + 1) * cut]
    for c in range(units):
        begin = (c % 2 * heads + c // 2) * size
        own = kv_ref[:, :, begin : begin + size]
        pools[c][pl.ds(level * blocks, blocks)] = own
        ext[c, pl.ds(MAXR, blocks)] = own
    pl.semaphore_wait(barrier, count - 1 + 3)

    def scatter(c):
        if c + 3 < units:
            pair_copy(c + 3).start()
        pair_copy(c).wait()
        halo_copy(c).start()
        ext[c, pl.ds((blocks + MAXR) * (1 - level), MAXR)] = pools[c][
            pl.ds(blocks - MAXR * level, MAXR)
        ]
        for d in range(1, LINE):
            target, _ = along(c, 0, d)

            def fill(j, carry):
                source = list_ref[base(c) + target * STRIDE + j]
                stage1[c, (d - 1) * FIRST + j] = pools[c][source]
                return carry

            lax.fori_loop(0, FIRST, fill, 0, unroll=2)
        for d in (1, 3, 2):
            bulk(c, 0, d).start()

    def forward(c):
        for d in range(1, LINE):
            bulk(c, 0, d).wait()
        for d in range(1, LINE):
            target, _ = along(c, 1, d)

            def fill(j, carry):
                source = list_ref[base(c) + (LINE + target) * STRIDE + j]
                stage2[c, (d - 1) * SECOND + j] = jnp.where(
                    source < held,
                    pools[c][jnp.minimum(source, held - 1)],
                    holds[c][jnp.maximum(source - held, 0)],
                )
                return carry

            lax.fori_loop(0, SECOND, fill, 0, unroll=2)
        for d in (1, 3, 2):
            bulk(c, 1, d).start()

    held = 2 * blocks
    ended = held + LINE * FIRST

    place = lax.broadcasted_iota(jnp.int32, (rows, near), 1) // rows - MAXR
    left = lax.broadcasted_iota(jnp.int32, (rows, size), 1) < size // 2

    def score(q, keys):
        return (
            lax.dot_general(q, keys, (((1,), (1,)), ((), ())), preferred_element_type=jnp.float32)
            * scale
        )

    def nearby(c):
        halo_copy(2 * c).wait()
        halo_copy(2 * c + 1).wait()
        lanes = slice(c * size, (c + 1) * size)
        allowed = jnp.abs(place) <= list_ref[2 * G + c]
        g_k = gkv[:, :, c * size : (c + 1) * size].reshape(G * rows, size)
        g_v = gkv[:, :, (heads + c) * size : (heads + c + 1) * size].reshape(G * rows, size)

        def attend(b, carry):
            block = me * blocks + b
            inside = (place + block >= 0) & (place + block < count * blocks)
            q = q_ref[b, :, lanes]
            window_k = ext[2 * c, pl.ds(b, SPAN)].reshape(near, size)
            window_v = ext[2 * c + 1, pl.ds(b, SPAN)].reshape(near, size)
            s1 = jnp.where(inside & allowed, score(q, window_k), -jnp.inf)
            s2 = score(q, g_k)
            peak = jnp.maximum(
                jnp.max(s1, axis=1, keepdims=True), jnp.max(s2, axis=1, keepdims=True)
            )
            p1 = jnp.exp(s1 - peak)
            p2 = jnp.exp(s2 - peak)
            total = jnp.sum(p1, axis=1, keepdims=True) + jnp.sum(p2, axis=1, keepdims=True)
            sums[c, b] = jnp.dot(
                p1.astype(jnp.bfloat16), window_v, preferred_element_type=jnp.float32
            ) + jnp.dot(p2.astype(jnp.bfloat16), g_v, preferred_element_type=jnp.float32)
            stats[c, b] = jnp.where(left, peak, total)
            return carry

        lax.fori_loop(0, blocks, attend, 0)

    def distant(c):
        for d in range(1, LINE):
            bulk(2 * c, 1, d).wait()
            bulk(2 * c + 1, 1, d).wait()
        lanes = slice(c * size, (c + 1) * size)
        swap = [
            jnp.concatenate([far[c * 8 + g * 4 + r] for r in range(4)], axis=0) for g in range(G)
        ]

        def collect(u, b):
            picked = []
            for r in range(R):
                at = list_ref[base(u) + 2 * LINE * STRIDE + b * R + r]
                picked.append(
                    jnp.where(
                        at < held,
                        pools[u][jnp.minimum(at, held - 1)],
                        jnp.where(
                            at < ended,
                            holds[u][jnp.clip(at - held, 0, LINE * FIRST - 1)],
                            lasts[u][jnp.maximum(at - ended, 0)],
                        ),
                    )
                )
            return jnp.concatenate(picked, axis=0)

        def attend(b, carry):
            q = q_ref[b, :, lanes]
            extra_v = collect(2 * c + 1, b)
            s2 = score(q, collect(2 * c, b))
            first_peak = stats[c, b, :, 0:1]
            peak = jnp.maximum(first_peak, jnp.max(s2, axis=1, keepdims=True))
            factor = jnp.exp(first_peak - peak)
            p2 = jnp.exp(s2 - peak)
            total = stats[c, b, :, size // 2 : size // 2 + 1] * factor + jnp.sum(
                p2, axis=1, keepdims=True
            )
            acc = sums[c, b] * factor + jnp.dot(
                p2.astype(jnp.bfloat16), extra_v, preferred_element_type=jnp.float32
            )
            which = list_ref[2 * G + heads + b]
            result = (acc / total).astype(out_ref.dtype)
            out_ref[b, :, lanes] = jnp.where(
                which == 0, swap[0], jnp.where(which == 1, swap[1], result)
            )
            return carry

        lax.fori_loop(0, blocks, attend, 0)

    def att_copy(kind, c, src, dst, other):
        lanes = pl.ds(c * size, size)
        return pltpu.make_async_remote_copy(
            src_ref=src.at[:, :, lanes],
            dst_ref=dst.at[:, :, lanes],
            send_sem=att_send.at[kind, c],
            recv_sem=att_recv.at[kind, c],
            device_id={"tp": other},
            device_id_type=MESH,
        )

    def att_mate(c):
        return att_copy(0, c, out_ref, a1_ref, mates[0])

    def att_over(c):
        return att_copy(1, c, out_ref, a2_ref, mates[1])

    def att_on(c):
        return att_copy(2, c, a2_ref, a3_ref, mates[0])

    each(lambda k: small(0, k, True, cand, got).start())
    for c in range(3):
        pair_copy(c).start()
    got[me] = cand[me]
    each(lambda k: small(0, k, True, cand, got).wait())
    full[me] = got[list_ref[me // (count // G)]]
    each(lambda k: small(1, k, False, full, full).start())
    for c in range(3):
        scatter(c)

    each(lambda k: small(1, k, False, full, full).wait())
    for g in range(G):
        for r in range(4):
            row = jnp.concatenate([full[(g * 4 + r) * 4 + s] for s in range(4)], axis=1)
            gkv[g, r * 16 : r * 16 + 16, :] = row[:, : heads * pair]
            gq[g, r * 16 : r * 16 + 16, :] = row[:, heads * pair :]

    half_lane = lax.broadcasted_iota(jnp.int32, (G * rows, size), 1) < size // 2
    last_lane = lax.broadcasted_iota(jnp.int32, (G * rows, size), 1) >= 3 * size // 4
    for h in range(heads):
        gq_h = gq[:, :, h * size : (h + 1) * size].reshape(G * rows, size)
        k_h = kv_ref[:, :, h * size : (h + 1) * size].reshape(blocks * rows, size)
        v_h = kv_ref[:, :, (heads + h) * size : (heads + h + 1) * size].reshape(
            blocks * rows, size
        )
        s = (
            lax.dot_general(gq_h, k_h, (((1,), (1,)), ((), ())), preferred_element_type=jnp.float32)
            * scale
        )
        peak = jnp.max(s, axis=1, keepdims=True).astype(jnp.bfloat16).astype(jnp.float32)
        p = jnp.exp(s - peak)
        total = jnp.sum(p, axis=1, keepdims=True)
        acc = jnp.dot(p.astype(jnp.bfloat16), v_h, preferred_element_type=jnp.float32)
        acc = acc.astype(part.dtype)
        high = total.astype(part.dtype).astype(jnp.float32)
        both = jnp.where(half_lane, peak, jnp.where(last_lane, total - high, high))
        both = both.astype(part.dtype)
        for r in range(8):
            cut = slice(r * 16, r * 16 + 16)
            part[h * 8 + r, 0:16, :] = acc[cut]
            part[h * 8 + r, 16:32, :] = both[cut]
    far_got[me] = part[me]
    each(lambda k: small(2, k, True, part, far_got).start())
    for c in range(3, units):
        scatter(c)
    for k in range(3):
        weight_copy(k).start()
    forward(0)
    forward(1)
    nearby(0)
    forward(2)
    forward(3)
    nearby(1)

    each(lambda k: small(2, k, True, part, far_got).wait())

    def terms(i):
        both = far_got[i, 16:32, :].astype(jnp.float32)
        total = both[:, size // 2 : size // 2 + 1] + both[:, size - 1 : size]
        return far_got[i, 0:16, :].astype(jnp.float32), both[:, 0:1], total

    far_peak = lax.fori_loop(
        1, count, lambda i, m: jnp.maximum(m, terms(i)[1]), terms(0)[1], unroll=4
    )

    def add(i, so_far):
        acc, peak, total = terms(i)
        factor = jnp.exp(peak - far_peak)
        return so_far[0] + acc * factor, so_far[1] + total * factor

    far_acc, far_total = lax.fori_loop(
        0,
        count,
        add,
        (jnp.zeros((16, size), jnp.float32), jnp.zeros((16, 1), jnp.float32)),
        unroll=4,
    )
    far[me] = (far_acc / far_total).astype(far.dtype)
    each(lambda k: small(3, k, False, far, far).start())
    for c in range(heads, units):
        forward(c)

    nearby(2)
    nearby(3)

    each(lambda k: small(3, k, False, far, far).wait())
    for c in range(heads):
        distant(c)
        if c > 0:
            att_over(c - 1).wait_recv()
            att_on(c - 1).start()
        att_over(c).start()
        att_mate(c).start()
    att_over(heads - 1).wait_recv()
    att_on(heads - 1).start()
    for c in range(heads):
        att_over(c).wait_send()
        att_mate(c).wait()
        att_on(c).wait()
    for k in range(3):
        weight_copy(k).wait()


def front(lists, kv, q, heads, weight, scale, count, tp_count):
    blocks, rows, half = q.shape
    size = half // heads
    pair = 2 * size
    kept = kv.dtype
    vmem = pl.BlockSpec(memory_space=VMEM)
    hbm = pl.BlockSpec(memory_space=pl.ANY)
    cols = weight.shape[1] // tp_count
    moved = jax.ShapeDtypeStruct((weight.shape[0], cols), kept)
    same = jax.ShapeDtypeStruct(q.shape, kept)
    cut = (heads * pair + heads * size) // 4
    dma = pltpu.SemaphoreType.DMA
    return pl.pallas_call(
        functools.partial(front_kernel, count, scale),
        name="front",
        out_shape=(jax.ShapeDtypeStruct(q.shape, kept),) + (moved,) * 3 + (same,) * 3,
        in_specs=[pl.BlockSpec(memory_space=SMEM), vmem, vmem, hbm],
        out_specs=(vmem,) + (hbm,) * 6,
        scratch_shapes=[
            VMEM((blocks, rows, 2 * half), kept),
            VMEM((2 * heads, blocks + 2 * MAXR, rows, size), kept),
            VMEM((count, 16, cut), kept),
            VMEM((count, 16, cut), kept),
            VMEM((count, 16, cut), kept),
            VMEM((G, rows, heads * pair), kept),
            VMEM((G, rows, heads * size), kept),
            VMEM((count, 32, size), kept),
            VMEM((count, 32, size), kept),
            VMEM((count, 16, size), kept),
        ]
        + [VMEM((2 * blocks, rows, size), kept)] * (2 * heads)
        + [VMEM((LINE * FIRST, rows, size), kept)] * (2 * heads)
        + [VMEM((LINE * SECOND, rows, size), kept)] * (2 * heads)
        + [
            VMEM((2 * heads, (LINE - 1) * FIRST, rows, size), kept),
            VMEM((2 * heads, (LINE - 1) * SECOND, rows, size), kept),
            VMEM((heads, blocks, rows, size), jnp.float32),
            VMEM((heads, blocks, rows, size), jnp.float32),
            dma((3, heads)),
            dma((3, heads)),
            dma((2 * heads,)),
            dma((2 * heads,)),
            dma((2 * heads,)),
            dma((2 * heads,)),
            dma((3,)),
            dma((3,)),
            dma((4, count)),
            dma((4, count)),
            dma((2, 2 * heads, LINE - 1)),
            dma((2, 2 * heads, LINE - 1)),
        ],
        compiler_params=pltpu.CompilerParams(
            collective_id=3, has_side_effects=True, vmem_limit_bytes=60 * 2**20
        ),
    )(lists, kv, q, weight)


STRIDE = 16
HEADER = 24
ROUTE = 2 * LINE * STRIDE + 40


def plan_kernel(count, blocks, row_ref, col_ref, req_ref, reqt_ref, reach_ref, gb_ref, out_ref):
    me = lax.axis_index("ctx")
    x, z, level = me // 8, lax.rem(me // 2, LINE), lax.rem(me, 2)
    many = 2 * blocks
    total = count * blocks
    low = jnp.bfloat16

    def iota(shape, dim):
        return lax.broadcasted_iota(jnp.int32, shape, dim)

    def product(a, b):
        return jnp.dot(a.astype(low), b.astype(low), preferred_element_type=jnp.float32)

    def flag(condition):
        return jnp.where(condition, 1.0, 0.0)

    ids = iota((count, total), 1)
    asked = jnp.zeros((count, total), jnp.float32)
    for e in range(blocks * R):
        asked = jnp.where(req_ref[:, e : e + 1] == ids, 1.0, asked)

    place = {"x": row_ref[0:1, :], "z": row_ref[1:2, :]}
    inner = row_ref[2:3, :].astype(jnp.float32)
    group = row_ref[3:4, :]
    place_col = {"x": col_ref[:, 0:1], "z": col_ref[:, 1:2]}
    group_col = col_ref[:, 3:4]
    before = iota((total, total), 0) < iota((total, total), 1)

    r8, s8 = iota((8, count), 0), iota((8, count), 1)
    where_of = {"x": s8 >> 3, "z": (s8 >> 1) & 3}
    lane = iota((8, 128), 1)
    line8 = iota((8, 128), 0) >> 1
    lane32 = iota((count, 128), 1)
    row32 = iota((count, 128), 0)
    own32 = {"x": row32 >> 3, "z": (row32 >> 1) & 3}
    pair_of = {"x": lane >> 2, "z": lane & 3}
    seats = flag(group_col == iota((total, 128), 1))
    longest = []
    for first, second in (("x", "z"), ("z", "x")):
        same = (where_of[first] == r8 >> 1) & ((s8 & 1) == (r8 & 1))
        need = flag(product(flag(same), asked) > 0)
        counts = product(need, seats)
        apart = (lane < LINE * LINE) & (pair_of[first] != line8)
        longest.append(jnp.max(jnp.where(apart, counts - FIRST, -1.0)))
        counts = product(asked, flag(place_col[second] == iota((total, 128), 1)))
        apart = (lane32 < LINE) & (lane32 != own32[second])
        longest.append(jnp.max(jnp.where(apart, counts - SECOND, -1.0)))
    over = jnp.maximum(
        jnp.maximum(longest[0], longest[1]), jnp.maximum(longest[2], longest[3])
    )

    head = iota((HEADER, 128), 0)
    top = jnp.where(head == 20, jnp.where(over > 0, 0, 1), 0)
    entries = []
    for g in range(G):
        entries.append((g, gb_ref[g] // blocks))
        entries.append((G + g, lax.rem(gb_ref[g], blocks)))
    for h in range(4):
        entries.append((2 * G + h, reach_ref[h]))
    for b in range(blocks):
        block = me * blocks + b
        which = jnp.where(block == gb_ref[0], 0, jnp.where(block == gb_ref[1], 1, -1))
        entries.append((2 * G + 4 + b, which))
    for k, value in entries:
        top = jnp.where(head == k, value, top)
    out_ref[0:HEADER, :] = top

    spots = {"x": x, "z": z}
    mine = (place["x"] == x) & (place["z"] == z)
    turn = iota((8, total), 0)
    asked_col = jnp.sum(
        jnp.where(iota(reqt_ref.shape, 1) == me, reqt_ref[...], 0), axis=1, keepdims=True
    )

    def store(offset, column):
        out_ref[offset : offset + column.shape[0], :] = jnp.broadcast_to(
            column.astype(jnp.int32), (column.shape[0], 128)
        )

    for o, (first, second) in enumerate((("x", "z"), ("z", "x"))):
        start = HEADER + o * ROUTE
        line_first = place[first].astype(jnp.float32)
        line_second = place[second].astype(jnp.float32)
        same = (where_of[first] == r8) & ((s8 & 1) == level)
        need = flag(product(flag(same), asked) > 0)
        rank = product(need, flag(before & (group_col == group)))
        slot = iota((STRIDE, total), 0).astype(jnp.float32)
        for t in range(LINE):
            hit = (need[t : t + 1] > 0) & mine & (rank[t : t + 1] == slot)
            column = jnp.sum(jnp.where(hit, inner, 0.0), axis=1, keepdims=True)
            store(start + t * STRIDE, column)
        my_rank = jnp.sum(jnp.where(turn == spots[first], rank, 0.0), axis=0, keepdims=True)
        found = jnp.where(
            place[first] == spots[first],
            inner,
            many + line_first * FIRST + jnp.minimum(my_rank, FIRST - 1),
        )
        line = (where_of[first] == spots[first]) & (where_of[second] == r8)
        here = product(flag(line & ((s8 & 1) == level)), asked)
        wanted = flag((here > 0) & (place[second] == spots[second]))
        rank = product(wanted, flag(before))
        for t in range(LINE):
            hit = (wanted[t : t + 1] > 0) & (rank[t : t + 1] == slot)
            column = jnp.sum(jnp.where(hit, found, 0.0), axis=1, keepdims=True)
            store(start + (LINE + t) * STRIDE, column)
        own = jnp.sum(jnp.where(turn == spots[second], here, 0.0), axis=0, keepdims=True)
        rank = product(
            jnp.broadcast_to(own, (8, total)),
            flag(before & (place_col[second] == place[second])),
        )[0:1]
        final = jnp.where(
            place[second] == spots[second],
            found,
            many + LINE * FIRST + line_second * SECOND + jnp.minimum(rank, SECOND - 1),
        )
        hit = asked_col == iota((reqt_ref.shape[0], total), 1)
        column = jnp.sum(jnp.where(hit, final, 0.0), axis=1, keepdims=True)
        store(start + 2 * LINE * STRIDE, column)


def plan(random_blocks, global_blocks, window_reach, blocks, count):
    requests = random_blocks.reshape(count, blocks * R)
    total = count * blocks
    ids = np.arange(total)
    table = np.zeros((8, total), np.int32)
    table[0] = ids // (LINE * 2 * blocks)
    table[1] = ids // (2 * blocks) % LINE
    table[2] = ids % (2 * blocks)
    table[3] = ids // (2 * blocks)
    turned = jnp.pad(requests.T, ((0, 40 - blocks * R), (0, 0)), constant_values=-1)
    vmem = pl.BlockSpec(memory_space=VMEM)
    smem = pl.BlockSpec(memory_space=SMEM)
    out = pl.pallas_call(
        functools.partial(plan_kernel, count, blocks),
        name="plan",
        out_shape=jax.ShapeDtypeStruct((HEADER + 2 * ROUTE, 128), jnp.int32),
        in_specs=[vmem] * 4 + [smem] * 2,
        out_specs=vmem,
        compiler_params=pltpu.CompilerParams(vmem_limit_bytes=48 * 2**20),
    )(table, np.ascontiguousarray(table.T), requests, turned, window_reach, global_blocks)
    return out[:, 0]


def direct(place, info, source_ids, my_index, kv, q, out_weight, scale, count, slots):
    block_count = q.shape[0]
    heads = info.shape[0] - block_count
    ext, gkv, gq = edges(place, kv, q, count)
    partials = far_partials(gq, kv, scale, heads, count)
    random, far = exchange(source_ids, kv, partials, count, slots)
    attended = attention(
        my_index, info, q, ext, gkv, far, random, scale, heads, count * block_count
    )
    tp = lax.axis_index("tp")
    tp_count = lax.axis_size("tp")
    cols = out_weight.shape[1] // tp_count
    mates = (tp, tp + 1 - 2 * lax.rem(tp, 2), lax.rem(tp + 2, tp_count), tp_count - 1 - tp)
    weights = []
    for k in range(1, tp_count):
        block = lax.dynamic_slice_in_dim(out_weight, mates[k] * cols, cols, axis=1)
        weights.append(lax.ppermute(block, "tp", [(i, i ^ k) for i in range(tp_count)]))
    for k in range(1, tp_count):
        weights.append(lax.ppermute(attended, "tp", [(i, i ^ k) for i in range(tp_count)]))
    return (attended, *weights)


def shards(
    queries,
    keyvals,
    residual,
    out_weight,
    norm_gain,
    norm_bias,
    cross_weight,
    window_reach,
    global_blocks,
    random_blocks,
):
    tok_rows, head_cols = queries.shape
    head_count = window_reach.shape[0]
    head_size = head_cols // head_count
    ctx_count = lax.axis_size("ctx")
    tp_count = lax.axis_size("tp")
    me = lax.axis_index("ctx")
    block_count = tok_rows // BLOCK
    scale = 1.0 / math.sqrt(head_size)
    q = queries.reshape(block_count, BLOCK, head_cols)
    lists = plan(random_blocks, global_blocks, window_reach, block_count, ctx_count)
    fits = lists[20] > 0

    def staged(keyvals, q, out_weight):
        return tuple(front(lists, keyvals, q, head_count, out_weight, scale, ctx_count, tp_count))

    def plain(keyvals, q, out_weight):
        req_count = block_count * R
        slots = 1 + (req_count + ctx_count - 2) // ctx_count
        requests = random_blocks.reshape(ctx_count, req_count)
        owners = requests // block_count
        local_ids = requests % block_count
        positions = jnp.arange(req_count, dtype=jnp.int32)
        earlier = positions[None, :] < positions[:, None]
        ranks = jnp.sum(
            ((owners[:, :, None] == owners[:, None, :]) & earlier[None, :, :]).astype(jnp.int32),
            axis=2,
        )
        slot_ids = jnp.arange(slots, dtype=jnp.int32)
        matches = (owners[:, None, :] == me) & (ranks[:, None, :] == slot_ids[None, :, None])
        source_ids = jnp.sum(jnp.where(matches, local_ids[:, None, :], 0), axis=2).reshape(-1)
        my_index = lax.dynamic_index_in_dim(owners * slots + ranks, me, 0, keepdims=False)
        place = lists[: 2 * G]
        info = lists[2 * G : 2 * G + head_count + block_count]
        return direct(
            place,
            info,
            source_ids,
            my_index,
            keyvals.reshape(block_count, BLOCK, 2 * head_cols),
            q, out_weight, scale, ctx_count, slots
        )

    attended, *rest = lax.cond(fits, staged, plain, keyvals, q, out_weight)
    weights = rest[: tp_count - 1]
    gathered = [x.reshape(tok_rows, head_cols) for x in [attended] + rest[tp_count - 1 :]]
    cols = residual.shape[1]
    encoded, cross_kv = project(
        gathered,
        residual,
        norm_gain.reshape(1, cols),
        norm_bias.reshape(1, cols),
        out_weight,
        weights,
        cross_weight,
        ctx_count,
        tp_count,
    )
    return (encoded, cross_kv)


def solution(mesh):
    placed = (
        P("ctx", "tp"),
        P("ctx", None, "tp"),
        P("ctx", "tp"),
        P("tp", None),
        P("tp"),
        P("tp"),
        P(None, None, "tp"),
        P("tp"),
        P(),
        P(),
    )
    return jax.shard_map(
        shards,
        mesh=mesh,
        in_specs=placed,
        out_specs=(P("ctx", "tp"), P("ctx", None, "tp")),
        check_vma=False,
    )
```

```python
import functools
import math

import jax
import jax.numpy as jnp
from jax import lax
from jax.experimental import pallas as pl
from jax.experimental.pallas import tpu as pltpu
from jax.sharding import PartitionSpec as P

D = 4096
BLOCK = 64
MAXR = 3
G = 2
R = 3
SPAN = 2 * MAXR + 1
MESH = pl.DeviceIdType.MESH
VMEM = pltpu.VMEM
SMEM = pltpu.SMEM

norm_eps = 1e-05


def greet(axis, count):
    me = lax.axis_index(axis)
    barrier = pltpu.get_barrier_semaphore()

    def signal(k, carry):
        pl.semaphore_signal(
            barrier, inc=1, device_id={axis: lax.rem(me + k, count)}, device_id_type=MESH
        )
        return carry

    lax.fori_loop(1, count, signal, 0)
    pl.semaphore_wait(barrier, count - 1)


def edges_kernel(
    count,
    place_ref,
    kv_ref,
    q_ref,
    ext_ref,
    gkv_ref,
    gq_ref,
    cand,
    got,
    full,
    halo_send,
    halo_recv,
    send1,
    recv1,
    send2,
    recv2,
):
    me = lax.axis_index("ctx")
    blocks = kv_ref.shape[0]
    wide = kv_ref.shape[2]
    half = q_ref.shape[2]
    part = (wide + half) // 4
    greet("ctx", count)
    after = lax.rem(me + 1, count)
    before = lax.rem(me + count - 1, count)
    to_after = pltpu.make_async_remote_copy(
        src_ref=kv_ref.at[pl.ds(blocks - MAXR, MAXR)],
        dst_ref=ext_ref.at[pl.ds(0, MAXR)],
        send_sem=halo_send.at[0],
        recv_sem=halo_recv.at[0],
        device_id={"ctx": after},
        device_id_type=MESH,
    )
    to_before = pltpu.make_async_remote_copy(
        src_ref=kv_ref.at[pl.ds(0, MAXR)],
        dst_ref=ext_ref.at[pl.ds(blocks + MAXR, MAXR)],
        send_sem=halo_send.at[1],
        recv_sem=halo_recv.at[1],
        device_id={"ctx": before},
        device_id_type=MESH,
    )
    for g in range(G):
        local = place_ref[G + g]
        row = jnp.concatenate([kv_ref[local], q_ref[local]], axis=1)
        for r in range(4):
            for c in range(4):
                cand[(g * 4 + r) * 4 + c] = row[r * 16 : r * 16 + 16, c * part : (c + 1) * part]

    def first(k):
        to = lax.rem(me + k, count)
        return pltpu.make_async_remote_copy(
            src_ref=cand.at[to],
            dst_ref=got.at[me],
            send_sem=send1.at[k],
            recv_sem=recv1.at[k],
            device_id={"ctx": to},
            device_id_type=MESH,
        )

    def second(k):
        to = lax.rem(me + k, count)
        return pltpu.make_async_remote_copy(
            src_ref=full.at[me],
            dst_ref=full.at[me],
            send_sem=send2.at[k],
            recv_sem=recv2.at[k],
            device_id={"ctx": to},
            device_id_type=MESH,
        )

    def each(action):
        def body(k, carry):
            action(k)
            return carry

        lax.fori_loop(1, count, body, 0)

    each(lambda k: first(k).start())
    to_after.start()
    to_before.start()
    got[me] = cand[me]
    ext_ref[pl.ds(MAXR, blocks)] = kv_ref[...]
    each(lambda k: first(k).wait())
    full[me] = got[place_ref[me // (count // G)]]
    each(lambda k: second(k).start())
    each(lambda k: second(k).wait())
    for g in range(G):
        for r in range(4):
            row = jnp.concatenate([full[(g * 4 + r) * 4 + c] for c in range(4)], axis=1)
            gkv_ref[g, r * 16 : r * 16 + 16, :] = row[:, :wide]
            gq_ref[g, r * 16 : r * 16 + 16, :] = row[:, wide:]
    to_after.wait()
    to_before.wait()


def edges(place, kv, q, count):
    blocks, rows, wide = kv.shape
    half = q.shape[2]
    part = (wide + half) // 4
    return pl.pallas_call(
        functools.partial(edges_kernel, count),
        name="edges",
        out_shape=(
            jax.ShapeDtypeStruct((blocks + 2 * MAXR, rows, wide), kv.dtype),
            jax.ShapeDtypeStruct((G, rows, wide), kv.dtype),
            jax.ShapeDtypeStruct((G, rows, half), kv.dtype),
        ),
        in_specs=[
            pl.BlockSpec(memory_space=SMEM),
            pl.BlockSpec(memory_space=VMEM),
            pl.BlockSpec(memory_space=VMEM),
        ],
        out_specs=(pl.BlockSpec(memory_space=VMEM),) * 3,
        scratch_shapes=[
            VMEM((count, 16, part), kv.dtype),
            VMEM((count, 16, part), kv.dtype),
            VMEM((count, 16, part), kv.dtype),
            pltpu.SemaphoreType.DMA((2,)),
            pltpu.SemaphoreType.DMA((2,)),
            pltpu.SemaphoreType.DMA((count,)),
            pltpu.SemaphoreType.DMA((count,)),
            pltpu.SemaphoreType.DMA((count,)),
            pltpu.SemaphoreType.DMA((count,)),
        ],
        compiler_params=pltpu.CompilerParams(
            collective_id=0, has_side_effects=True, vmem_limit_bytes=48 * 2**20
        ),
    )(place, kv, q)


def far_kernel(scale, head_count, gq_ref, kv_ref, out_ref):
    blocks, rows, wide = kv_ref.shape
    size = wide // (2 * head_count)
    for h in range(head_count):
        lanes = slice(h * size, (h + 1) * size)
        q = gq_ref[:, :, lanes].reshape(G * rows, size)
        k = kv_ref[:, :, lanes].reshape(blocks * rows, size)
        v = kv_ref[:, :, wide // 2 + h * size : wide // 2 + (h + 1) * size].reshape(
            blocks * rows, size
        )
        s = (
            lax.dot_general(q, k, (((1,), (1,)), ((), ())), preferred_element_type=jnp.float32)
            * scale
        )
        peak = jnp.max(s, axis=1, keepdims=True)
        p = jnp.exp(s - peak)
        total = jnp.sum(p, axis=1, keepdims=True)
        acc = jnp.dot(p.astype(jnp.bfloat16), v, preferred_element_type=jnp.float32)
        peak = jnp.broadcast_to(peak, acc.shape)
        total = jnp.broadcast_to(total, acc.shape)
        for r in range(8):
            cut = slice(r * 16, r * 16 + 16)
            out_ref[h * 8 + r, 0:16, :] = acc[cut]
            out_ref[h * 8 + r, 16:32, :] = peak[cut]
            out_ref[h * 8 + r, 32:48, :] = total[cut]


def far_partials(gq, kv, scale, head_count, count):
    size = gq.shape[2] // head_count
    return pl.pallas_call(
        functools.partial(far_kernel, scale, head_count),
        name="far_partials",
        out_shape=jax.ShapeDtypeStruct((count, 48, size), jnp.float32),
        in_specs=[pl.BlockSpec(memory_space=VMEM)] * 2,
        out_specs=pl.BlockSpec(memory_space=VMEM),
        compiler_params=pltpu.CompilerParams(vmem_limit_bytes=48 * 2**20),
    )(gq, kv)


def exchange_kernel(
    count,
    slots,
    source_ref,
    kv_ref,
    part_ref,
    random_ref,
    far_ref,
    stage,
    got,
    bulk_send,
    bulk_recv,
    send1,
    recv1,
    send2,
    recv2,
    own_sem,
):
    me = lax.axis_index("ctx")
    greet("ctx", count)

    def first(k):
        to = lax.rem(me + k, count)
        return pltpu.make_async_remote_copy(
            src_ref=part_ref.at[to],
            dst_ref=got.at[me],
            send_sem=send1.at[k],
            recv_sem=recv1.at[k],
            device_id={"ctx": to},
            device_id_type=MESH,
        )

    def second(k):
        to = lax.rem(me + k, count)
        return pltpu.make_async_remote_copy(
            src_ref=far_ref.at[me],
            dst_ref=far_ref.at[me],
            send_sem=send2.at[k],
            recv_sem=recv2.at[k],
            device_id={"ctx": to},
            device_id_type=MESH,
        )

    def bulk(k):
        to = lax.rem(me + k, count)
        return pltpu.make_async_remote_copy(
            src_ref=stage.at[pl.ds(to * slots, slots)],
            dst_ref=random_ref.at[pl.ds(me * slots, slots)],
            send_sem=bulk_send.at[k],
            recv_sem=bulk_recv.at[k],
            device_id={"ctx": to},
            device_id_type=MESH,
        )

    def each(action):
        def body(k, carry):
            action(k)
            return carry

        lax.fori_loop(1, count, body, 0)

    each(lambda k: first(k).start())
    got[me] = part_ref[me]

    def place(i, carry):
        stage[i] = kv_ref[source_ref[i]]
        return carry

    lax.fori_loop(0, count * slots, place, 0)
    each(lambda k: bulk(k).start())
    own = pltpu.make_async_copy(
        stage.at[pl.ds(me * slots, slots)], random_ref.at[pl.ds(me * slots, slots)], own_sem
    )
    own.start()
    each(lambda k: first(k).wait())

    def top(i, so_far):
        return jnp.maximum(so_far, got[i, 16:32, :])

    peak = lax.fori_loop(1, count, top, got[0, 16:32, :])

    def add(i, so_far):
        acc, total = so_far
        factor = jnp.exp(got[i, 16:32, :] - peak)
        return acc + got[i, 0:16, :] * factor, total + got[i, 32:48, :] * factor

    zero = jnp.zeros_like(peak)
    acc, total = lax.fori_loop(0, count, add, (zero, zero))
    far_ref[me] = (acc / total).astype(far_ref.dtype)
    each(lambda k: second(k).start())
    own.wait()
    each(lambda k: bulk(k).wait())
    each(lambda k: second(k).wait())


def exchange(source, kv, partials, count, slots):
    blocks, rows, wide = kv.shape
    size = partials.shape[2]
    dma = pltpu.SemaphoreType.DMA((count,))
    return pl.pallas_call(
        functools.partial(exchange_kernel, count, slots),
        name="exchange",
        out_shape=(
            jax.ShapeDtypeStruct((count * slots, rows, wide), kv.dtype),
            jax.ShapeDtypeStruct((count, 16, size), kv.dtype),
        ),
        in_specs=[
            pl.BlockSpec(memory_space=SMEM),
            pl.BlockSpec(memory_space=VMEM),
            pl.BlockSpec(memory_space=VMEM),
        ],
        out_specs=(pl.BlockSpec(memory_space=pl.ANY), pl.BlockSpec(memory_space=VMEM)),
        scratch_shapes=[
            VMEM((count * slots, rows, wide), kv.dtype),
            VMEM((count, 48, size), jnp.float32),
            dma,
            dma,
            dma,
            dma,
            dma,
            dma,
            pltpu.SemaphoreType.DMA,
        ],
        compiler_params=pltpu.CompilerParams(
            collective_id=1, has_side_effects=True, vmem_limit_bytes=56 * 2**20
        ),
    )(source, kv, partials)


def attention_kernel(
    scale,
    head_count,
    all_blocks,
    index_ref,
    info_ref,
    q_ref,
    ext_ref,
    gkv_ref,
    far_ref,
    rand0,
    rand1,
    rand2,
    out_ref,
):
    b = pl.program_id(0)
    rows = q_ref.shape[1]
    wide = gkv_ref.shape[2]
    half = wide // 2
    size = half // head_count
    me = lax.axis_index("ctx")
    block = me * pl.num_programs(0) + b
    replaced = info_ref[head_count + b]
    near = SPAN * rows
    spot = lax.broadcasted_iota(jnp.int32, (rows, near), 1) // rows - MAXR
    inside = (spot + block >= 0) & (spot + block < all_blocks)
    for h in range(head_count):
        kl = slice(h * size, (h + 1) * size)
        vl = slice(half + h * size, half + (h + 1) * size)
        reach = info_ref[h]
        q = q_ref[0, :, kl]

        def listed(lanes):
            return jnp.concatenate(
                [
                    gkv_ref[0, :, lanes],
                    gkv_ref[1, :, lanes],
                    rand0[0, :, lanes],
                    rand1[0, :, lanes],
                    rand2[0, :, lanes],
                ],
                axis=0,
            )

        def score(keys):
            return (
                lax.dot_general(
                    q, keys, (((1,), (1,)), ((), ())), preferred_element_type=jnp.float32
                )
                * scale
            )

        window_k = ext_ref[pl.ds(b, SPAN), :, kl].reshape(near, size)
        window_v = ext_ref[pl.ds(b, SPAN), :, vl].reshape(near, size)
        s1 = jnp.where(inside & (jnp.abs(spot) <= reach), score(window_k), -jnp.inf)
        s2 = score(listed(kl))
        peak = jnp.maximum(
            jnp.max(s1, axis=1, keepdims=True), jnp.max(s2, axis=1, keepdims=True)
        )
        p1 = jnp.exp(s1 - peak)
        p2 = jnp.exp(s2 - peak)
        total = jnp.sum(p1, axis=1, keepdims=True) + jnp.sum(p2, axis=1, keepdims=True)
        acc = jnp.dot(p1.astype(jnp.bfloat16), window_v, preferred_element_type=jnp.float32)
        acc = acc + jnp.dot(
            p2.astype(jnp.bfloat16), listed(vl), preferred_element_type=jnp.float32
        )
        out_ref[0, :, kl] = (acc / total).astype(out_ref.dtype)

    for g in range(G):

        @pl.when(replaced == g)
        def _():
            for h in range(head_count):
                for r in range(4):
                    out_ref[0, r * 16 : r * 16 + 16, h * size : (h + 1) * size] = far_ref[
                        h * 8 + g * 4 + r
                    ]


def attention(index, info, q, ext, gkv, far, random, scale, head_count, all_blocks):
    blocks, rows, half = q.shape
    wide = 2 * half

    def whole(x):
        return pl.BlockSpec(x.shape, lambda b, *_: (0,) * x.ndim)

    def pick(r):
        return pl.BlockSpec((1, rows, wide), lambda b, index, info: (index[b * R + r], 0, 0))

    one = pl.BlockSpec((1, rows, half), lambda b, *_: (b, 0, 0))
    return pl.pallas_call(
        functools.partial(attention_kernel, scale, head_count, all_blocks),
        name="attention",
        grid_spec=pltpu.PrefetchScalarGridSpec(
            num_scalar_prefetch=2,
            grid=(blocks,),
            in_specs=[one, whole(ext), whole(gkv), whole(far), pick(0), pick(1), pick(2)],
            out_specs=one,
        ),
        out_shape=jax.ShapeDtypeStruct(q.shape, q.dtype),
        compiler_params=pltpu.CompilerParams(vmem_limit_bytes=48 * 2**20),
    )(index, info, q, ext, gkv, far, random, random, random)


def project_kernel(
    ctx_count,
    tp_count,
    chunks,
    width,
    att_ref,
    a1,
    a2,
    a3,
    residual_ref,
    scale_ref,
    w0,
    w1,
    w2,
    w3,
    cross_ref,
    encoded_ref,
    out_ref,
    w_all,
    raw,
    cross,
    mixed,
    stats,
    g0,
    g1,
    g2,
    g3,
    w_sem,
    cross_sem,
    send_sem,
    recv_sem,
):
    ctx = lax.axis_index("ctx")
    tp = lax.axis_index("tp")
    mate = tp + 1 - 2 * lax.rem(tp, 2)
    over = lax.rem(tp + 2, tp_count)
    cater = tp_count - 1 - tp
    beyond = lax.rem(ctx + ctx_count // 2, ctx_count)
    rows = att_ref.shape[0] // chunks
    cols = residual_ref.shape[1]

    own_cols = w0.at[:, pl.ds(pl.multiple_of(tp * residual_ref.shape[1], residual_ref.shape[1]), residual_ref.shape[1])]
    for k, w in enumerate((own_cols, w1, w2, w3)):
        pltpu.make_async_copy(w, w_all.at[k], w_sem.at[k]).start()
    for k, block in enumerate((tp, mate, over, cater)):
        pltpu.make_async_copy(
            cross_ref.at[pl.ds(block * cols, cols)], raw.at[k], cross_sem.at[k]
        ).start()

    barrier = pltpu.get_barrier_semaphore()
    for other in (mate, over, cater):
        pl.semaphore_signal(barrier, inc=1, device_id={"tp": other}, device_id_type=MESH)
    pl.semaphore_signal(barrier, inc=1, device_id={"ctx": beyond}, device_id_type=MESH)
    pl.semaphore_wait(barrier, 4)

    def cut(c):
        return pl.ds(pl.multiple_of(c * rows, rows), rows)

    def hop(kind, c, src, dst, where):
        return pltpu.make_async_remote_copy(
            src_ref=src,
            dst_ref=dst,
            send_sem=send_sem.at[kind, c],
            recv_sem=recv_sem.at[kind, c],
            device_id=where,
            device_id_type=MESH,
        )

    def stat(c, k):
        other = (mate, over, cater)[k - 1]
        return hop(2 + k, c, stats.at[c, 0], stats.at[c, k], {"tp": other})

    def roll(c):
        return hop(6, c, encoded_ref.at[cut(c)], g0.at[cut(c)], {"ctx": beyond})

    def enc_mate(c):
        return hop(7, c, g0.at[cut(c)], g1.at[cut(c)], {"tp": mate})

    def enc_over(c):
        return hop(8, c, g0.at[cut(c)], g2.at[cut(c)], {"tp": over})

    def enc_on(c):
        return hop(9, c, g2.at[cut(c)], g3.at[cut(c)], {"tp": mate})

    for k, w in enumerate((own_cols, w1, w2, w3)):
        pltpu.make_async_copy(w, w_all.at[k], w_sem.at[k]).wait()

    def step(t, carry):
        def at(delay, body):
            c = t - delay

            @pl.when((c >= 0) & (c < chunks))
            def _():
                body(c)

        def relay_enc(c):
            roll(c).wait_recv()
            enc_over(c).start()
            enc_mate(c).start()

        def relay_on(c):
            enc_over(c).wait_recv()
            enc_on(c).start()

        def normalize(c):
            for k in (1, 2, 3):
                stat(c, k).wait_recv()
            both = stats[c, 0] + stats[c, 1] + stats[c, 2] + stats[c, 3]
            total = jnp.transpose(jnp.broadcast_to(both[0:1], (rows, rows)))[:, 0:1]
            square = jnp.transpose(jnp.broadcast_to(both[8:9], (rows, rows)))[:, 0:1]
            mean = total / width
            variance = square / width - mean * mean
            scaled = (mixed[cut(c), :] - mean) * lax.rsqrt(variance + norm_eps)
            encoded_ref[cut(c), :] = (
                scaled * scale_ref[0:1].astype(jnp.float32) + scale_ref[1:2].astype(jnp.float32)
            ).astype(encoded_ref.dtype)

        def mix(c):
            part = residual_ref[cut(c), :].astype(jnp.float32)
            for k, a in enumerate((att_ref, a1, a2, a3)):
                part = part + jnp.dot(
                    a[cut(c), :], w_all[k], preferred_element_type=jnp.float32
                )
            mixed[cut(c), :] = part
            lane = lax.broadcasted_iota(jnp.int32, (rows, rows), 1)
            total = jnp.sum(part, axis=1, keepdims=True)
            square = jnp.sum(part * part, axis=1, keepdims=True)
            turned = jnp.transpose(jnp.where(lane < rows // 2, total, square))
            stats[c, 0, 0:8, :] = turned[0:8]
            stats[c, 0, 8:16, :] = turned[rows // 2 : rows // 2 + 8]

        def cast(c):
            enc_mate(c).wait_recv()
            enc_on(c).wait_recv()
            acc = jnp.zeros((rows, cross.shape[2]), jnp.float32)
            for k, g in enumerate((g0, g1, g2, g3)):
                acc = acc + jnp.dot(g[cut(c), :], cross[k], preferred_element_type=jnp.float32)
            out_ref[cut(c)] = acc.astype(out_ref.dtype).reshape(rows, 2, acc.shape[1] // 2)

        at(ROLL, relay_enc)
        at(ROLL + 1, relay_on)
        at(1, normalize)
        at(0, mix)

        def send_rows(c):
            roll(c).start()

        def send_stats(c):
            for k in (1, 2, 3):
                stat(c, k).start()

        at(1, send_rows)
        at(0, send_stats)

        for i in range(3):
            piece = t * 3 + i

            @pl.when(piece < 4 * PIECES)
            def _():
                k = piece // PIECES

                @pl.when(lax.rem(piece, PIECES) == 0)
                def _():
                    pltpu.make_async_copy(
                        cross_ref.at[pl.ds(0, cols)], raw.at[k], cross_sem.at[k]
                    ).wait()

                span = cols // PIECES
                some = pl.ds(pl.multiple_of(lax.rem(piece, PIECES) * span, span), span)
                cross[k, some] = raw[k, some].reshape(span, cross.shape[2])

        at(ROLL + 2, cast)
        return carry

    lax.fori_loop(0, chunks + ROLL + 2, step, 0)

    def finish(c, carry):
        for k in (1, 2, 3):
            stat(c, k).wait_send()
        roll(c).wait_send()
        enc_mate(c).wait_send()
        enc_over(c).wait_send()
        enc_on(c).wait_send()
        return carry

    lax.fori_loop(0, chunks, finish, 0)


ROLL = 3
PIECES = 4
CHUNKS = 6


def project(att, residual, scales, out_weight, weights, cross_weight, ctx_count, tp_count):
    rows, depth = att[0].shape
    cols = residual.shape[1]
    half = cross_weight.shape[2]
    wide = 2 * half
    vmem = pl.BlockSpec(memory_space=VMEM)
    hbm = pl.BlockSpec(memory_space=pl.ANY)
    kept = jnp.bfloat16
    return pl.pallas_call(
        functools.partial(project_kernel, ctx_count, tp_count, CHUNKS, cols * tp_count),
        name="project",
        out_shape=(
            jax.ShapeDtypeStruct((rows, cols), kept),
            jax.ShapeDtypeStruct((rows, 2, half), kept),
        ),
        in_specs=[vmem] * 6 + [hbm] * 5,
        out_specs=(vmem, vmem),
        scratch_shapes=[
            VMEM((4, depth, cols), kept),
            VMEM((4, cols, 2, half), kept),
            VMEM((4, cols, wide), kept),
            VMEM((rows, cols), jnp.float32),
            VMEM((CHUNKS, 4, 16, rows // CHUNKS), jnp.float32),
            VMEM((rows, cols), kept),
            VMEM((rows, cols), kept),
            VMEM((rows, cols), kept),
            VMEM((rows, cols), kept),
            pltpu.SemaphoreType.DMA((4,)),
            pltpu.SemaphoreType.DMA((4,)),
            pltpu.SemaphoreType.DMA((10, CHUNKS)),
            pltpu.SemaphoreType.DMA((10, CHUNKS)),
        ],
        compiler_params=pltpu.CompilerParams(
            collective_id=2, has_side_effects=True, vmem_limit_bytes=60 * 2**20
        ),
    )(*att, residual, scales, out_weight, *weights, cross_weight)


FIRST = 14
SECOND = 12
LINE = 4
HEAD_COLS = 128


def front_kernel(
    count,
    scale,
    list_ref,
    raw_ref,
    q_ref,
    weight_ref,
    out_ref,
    w1_ref,
    w2_ref,
    w3_ref,
    a1_ref,
    a2_ref,
    a3_ref,
    kv_ref,
    ext,
    cand,
    got,
    full,
    gkv,
    gq,
    part,
    far_got,
    far,
    pool0,
    pool1,
    pool2,
    pool3,
    pool4,
    pool5,
    pool6,
    pool7,
    hold0,
    hold1,
    hold2,
    hold3,
    hold4,
    hold5,
    hold6,
    hold7,
    last0,
    last1,
    last2,
    last3,
    last4,
    last5,
    last6,
    last7,
    stage1,
    stage2,
    sums,
    stats,
    att_send,
    att_recv,
    pair_send,
    pair_recv,
    halo_send,
    halo_recv,
    weight_send,
    weight_recv,
    small_send,
    small_recv,
    bulk_send,
    bulk_recv,
):
    me = lax.axis_index("ctx")
    tp = lax.axis_index("tp")
    units, blocks = ext.shape[0], kv_ref.shape[0]
    rows, size = ext.shape[2:]
    heads, pair = units // 2, 2 * size
    spot = (me // 8, lax.rem(me // 2, LINE))
    level = lax.rem(me, 2)
    twin = me + 1 - 2 * level
    mates = (tp + 1 - 2 * lax.rem(tp, 2), lax.rem(tp + 2, 4), 3 - tp)
    pools = (pool0, pool1, pool2, pool3, pool4, pool5, pool6, pool7)
    holds = (hold0, hold1, hold2, hold3, hold4, hold5, hold6, hold7)
    lasts = (last0, last1, last2, last3, last4, last5, last6, last7)
    wcols = w1_ref.shape[1]
    near = SPAN * rows

    barrier = pltpu.get_barrier_semaphore()

    def greeting(k, carry):
        pl.semaphore_signal(
            barrier, inc=1, device_id={"ctx": lax.rem(me + k, count)}, device_id_type=MESH
        )
        return carry

    lax.fori_loop(1, count, greeting, 0)
    for other in mates[:2]:
        pl.semaphore_signal(barrier, inc=1, device_id={"tp": other}, device_id_type=MESH)
    pl.semaphore_signal(
        barrier, inc=1, device_id={"ctx": twin, "tp": mates[2]}, device_id_type=MESH
    )

    def base(c):
        return HEADER + (c % 2) * ROUTE

    def along(c, stage, d):
        x, z = spot
        if (c + stage) % 2 == 0:
            x = lax.rem(x + d, LINE)
            return x, x * 8 + z * 2 + level
        z = lax.rem(z + d, LINE)
        return z, x * 8 + z * 2 + level

    def pair_copy(c):
        return pltpu.make_async_remote_copy(
            src_ref=ext.at[c, pl.ds(MAXR, blocks)],
            dst_ref=pools[c].at[pl.ds(level * blocks, blocks)],
            send_sem=pair_send.at[c],
            recv_sem=pair_recv.at[c],
            device_id={"ctx": twin},
            device_id_type=MESH,
        )

    def halo_copy(c):
        return pltpu.make_async_remote_copy(
            src_ref=pools[c].at[pl.ds((2 * blocks - MAXR) * (1 - level), MAXR)],
            dst_ref=ext.at[c, pl.ds((blocks + MAXR) * level, MAXR)],
            send_sem=halo_send.at[c],
            recv_sem=halo_recv.at[c],
            device_id={"ctx": lax.rem(me + 2 - 4 * level + count, count)},
            device_id_type=MESH,
        )

    def weight_copy(k):
        other = mates[k]
        return pltpu.make_async_remote_copy(
            src_ref=weight_ref.at[:, pl.ds(pl.multiple_of(other * wcols, wcols), wcols)],
            dst_ref=(w1_ref, w2_ref, w3_ref)[k],
            send_sem=weight_send.at[k],
            recv_sem=weight_recv.at[k],
            device_id={"tp": other} if k < 2 else {"ctx": twin, "tp": other},
            device_id_type=MESH,
        )

    def small(kind, k, scattered, src, dst):
        to = lax.rem(me + k, count)
        return pltpu.make_async_remote_copy(
            src_ref=src.at[to if scattered else me],
            dst_ref=dst.at[me],
            send_sem=small_send.at[kind, k],
            recv_sem=small_recv.at[kind, k],
            device_id={"ctx": to},
            device_id_type=MESH,
        )

    def bulk(c, stage, d):
        slots = (FIRST, SECOND)[stage]
        mine = spot[(c + stage) % 2]
        buffer = (stage1, stage2)[stage]
        return pltpu.make_async_remote_copy(
            src_ref=buffer.at[c, pl.ds((d - 1) * slots, slots)],
            dst_ref=(holds, lasts)[stage][c].at[pl.ds(mine * slots, slots)],
            send_sem=bulk_send.at[stage, c, d - 1],
            recv_sem=bulk_recv.at[stage, c, d - 1],
            device_id={"ctx": along(c, stage, d)[1]},
            device_id_type=MESH,
        )

    def each(action):
        def body(k, carry):
            action(k)
            return carry

        lax.fori_loop(1, count, body, 0)

    for b in range(blocks):
        kv_ref[b] = raw_ref[b * rows : (b + 1) * rows].reshape(rows, heads * pair)
    for g in range(G):
        local = list_ref[G + g]
        row = jnp.concatenate([kv_ref[local], q_ref[local]], axis=1)
        cut = row.shape[1] // 4
        for r in range(4):
            for s in range(4):
                cand[(g * 4 + r) * 4 + s] = row[r * 16 : r * 16 + 16, s * cut : (s + 1) * cut]
    for c in range(units):
        begin = (c % 2 * heads + c // 2) * size
        own = kv_ref[:, :, begin : begin + size]
        pools[c][pl.ds(level * blocks, blocks)] = own
        ext[c, pl.ds(MAXR, blocks)] = own
    pl.semaphore_wait(barrier, count - 1 + 3)

    def scatter(c):
        if c + 3 < units:
            pair_copy(c + 3).start()
        pair_copy(c).wait()
        halo_copy(c).start()
        ext[c, pl.ds((blocks + MAXR) * (1 - level), MAXR)] = pools[c][
            pl.ds(blocks - MAXR * level, MAXR)
        ]
        for d in range(1, LINE):
            target, _ = along(c, 0, d)

            def fill(j, carry):
                source = list_ref[base(c) + target * STRIDE + j]
                stage1[c, (d - 1) * FIRST + j] = pools[c][source]
                return carry

            lax.fori_loop(0, FIRST, fill, 0, unroll=2)
        for d in (1, 3, 2):
            bulk(c, 0, d).start()

    def forward(c):
        for d in range(1, LINE):
            bulk(c, 0, d).wait()
        for d in range(1, LINE):
            target, _ = along(c, 1, d)

            def fill(j, carry):
                source = list_ref[base(c) + (LINE + target) * STRIDE + j]
                stage2[c, (d - 1) * SECOND + j] = jnp.where(
                    source < held,
                    pools[c][jnp.minimum(source, held - 1)],
                    holds[c][jnp.maximum(source - held, 0)],
                )
                return carry

            lax.fori_loop(0, SECOND, fill, 0, unroll=2)
        for d in (1, 3, 2):
            bulk(c, 1, d).start()

    held = 2 * blocks
    ended = held + LINE * FIRST

    place = lax.broadcasted_iota(jnp.int32, (rows, near), 1) // rows - MAXR
    left = lax.broadcasted_iota(jnp.int32, (rows, size), 1) < size // 2

    def score(q, keys):
        return (
            lax.dot_general(q, keys, (((1,), (1,)), ((), ())), preferred_element_type=jnp.float32)
            * scale
        )

    def nearby(c):
        halo_copy(2 * c).wait()
        halo_copy(2 * c + 1).wait()
        lanes = slice(c * size, (c + 1) * size)
        allowed = jnp.abs(place) <= list_ref[2 * G + c]
        g_k = gkv[:, :, c * size : (c + 1) * size].reshape(G * rows, size)
        g_v = gkv[:, :, (heads + c) * size : (heads + c + 1) * size].reshape(G * rows, size)

        def attend(b, carry):
            block = me * blocks + b
            inside = (place + block >= 0) & (place + block < count * blocks)
            q = q_ref[b, :, lanes]
            window_k = ext[2 * c, pl.ds(b, SPAN)].reshape(near, size)
            window_v = ext[2 * c + 1, pl.ds(b, SPAN)].reshape(near, size)
            s1 = jnp.where(inside & allowed, score(q, window_k), -jnp.inf)
            s2 = score(q, g_k)
            peak = jnp.maximum(
                jnp.max(s1, axis=1, keepdims=True), jnp.max(s2, axis=1, keepdims=True)
            )
            p1 = jnp.exp(s1 - peak)
            p2 = jnp.exp(s2 - peak)
            total = jnp.sum(p1, axis=1, keepdims=True) + jnp.sum(p2, axis=1, keepdims=True)
            sums[c, b] = jnp.dot(
                p1.astype(jnp.bfloat16), window_v, preferred_element_type=jnp.float32
            ) + jnp.dot(p2.astype(jnp.bfloat16), g_v, preferred_element_type=jnp.float32)
            stats[c, b] = jnp.where(left, peak, total)
            return carry

        lax.fori_loop(0, blocks, attend, 0)

    def distant(c):
        for d in range(1, LINE):
            bulk(2 * c, 1, d).wait()
            bulk(2 * c + 1, 1, d).wait()
        lanes = slice(c * size, (c + 1) * size)
        swap = [
            jnp.concatenate([far[c * 8 + g * 4 + r] for r in range(4)], axis=0) for g in range(G)
        ]

        def collect(u, b):
            picked = []
            for r in range(R):
                at = list_ref[base(u) + 2 * LINE * STRIDE + b * R + r]
                picked.append(
                    jnp.where(
                        at < held,
                        pools[u][jnp.minimum(at, held - 1)],
                        jnp.where(
                            at < ended,
                            holds[u][jnp.clip(at - held, 0, LINE * FIRST - 1)],
                            lasts[u][jnp.maximum(at - ended, 0)],
                        ),
                    )
                )
            return jnp.concatenate(picked, axis=0)

        def attend(b, carry):
            q = q_ref[b, :, lanes]
            extra_v = collect(2 * c + 1, b)
            s2 = score(q, collect(2 * c, b))
            first_peak = stats[c, b, :, 0:1]
            peak = jnp.maximum(first_peak, jnp.max(s2, axis=1, keepdims=True))
            factor = jnp.exp(first_peak - peak)
            p2 = jnp.exp(s2 - peak)
            total = stats[c, b, :, size // 2 : size // 2 + 1] * factor + jnp.sum(
                p2, axis=1, keepdims=True
            )
            acc = sums[c, b] * factor + jnp.dot(
                p2.astype(jnp.bfloat16), extra_v, preferred_element_type=jnp.float32
            )
            which = list_ref[2 * G + heads + b]
            result = (acc / total).astype(out_ref.dtype)
            out_ref[b, :, lanes] = jnp.where(
                which == 0, swap[0], jnp.where(which == 1, swap[1], result)
            )
            return carry

        lax.fori_loop(0, blocks, attend, 0)

    def att_copy(kind, c, src, dst, other):
        lanes = pl.ds(c * size, size)
        return pltpu.make_async_remote_copy(
            src_ref=src.at[:, :, lanes],
            dst_ref=dst.at[:, :, lanes],
            send_sem=att_send.at[kind, c],
            recv_sem=att_recv.at[kind, c],
            device_id={"tp": other},
            device_id_type=MESH,
        )

    def att_mate(c):
        return att_copy(0, c, out_ref, a1_ref, mates[0])

    def att_over(c):
        return att_copy(1, c, out_ref, a2_ref, mates[1])

    def att_on(c):
        return att_copy(2, c, a2_ref, a3_ref, mates[0])

    each(lambda k: small(0, k, True, cand, got).start())
    for c in range(3):
        pair_copy(c).start()
    got[me] = cand[me]
    each(lambda k: small(0, k, True, cand, got).wait())
    full[me] = got[list_ref[me // (count // G)]]
    each(lambda k: small(1, k, False, full, full).start())
    for c in range(3):
        scatter(c)

    each(lambda k: small(1, k, False, full, full).wait())
    for g in range(G):
        for r in range(4):
            row = jnp.concatenate([full[(g * 4 + r) * 4 + s] for s in range(4)], axis=1)
            gkv[g, r * 16 : r * 16 + 16, :] = row[:, : heads * pair]
            gq[g, r * 16 : r * 16 + 16, :] = row[:, heads * pair :]

    half_lane = lax.broadcasted_iota(jnp.int32, (G * rows, size), 1) < size // 2
    last_lane = lax.broadcasted_iota(jnp.int32, (G * rows, size), 1) >= 3 * size // 4
    for h in range(heads):
        gq_h = gq[:, :, h * size : (h + 1) * size].reshape(G * rows, size)
        k_h = kv_ref[:, :, h * size : (h + 1) * size].reshape(blocks * rows, size)
        v_h = kv_ref[:, :, (heads + h) * size : (heads + h + 1) * size].reshape(
            blocks * rows, size
        )
        s = (
            lax.dot_general(gq_h, k_h, (((1,), (1,)), ((), ())), preferred_element_type=jnp.float32)
            * scale
        )
        peak = jnp.max(s, axis=1, keepdims=True).astype(jnp.bfloat16).astype(jnp.float32)
        p = jnp.exp(s - peak)
        total = jnp.sum(p, axis=1, keepdims=True)
        acc = jnp.dot(p.astype(jnp.bfloat16), v_h, preferred_element_type=jnp.float32)
        acc = acc.astype(part.dtype)
        high = total.astype(part.dtype).astype(jnp.float32)
        both = jnp.where(half_lane, peak, jnp.where(last_lane, total - high, high))
        both = both.astype(part.dtype)
        for r in range(8):
            cut = slice(r * 16, r * 16 + 16)
            part[h * 8 + r, 0:16, :] = acc[cut]
            part[h * 8 + r, 16:32, :] = both[cut]
    far_got[me] = part[me]
    each(lambda k: small(2, k, True, part, far_got).start())
    for c in range(3, units):
        scatter(c)
    for k in range(3):
        weight_copy(k).start()
    forward(0)
    forward(1)
    nearby(0)
    each(lambda k: small(2, k, True, part, far_got).wait())

    def terms(i):
        both = far_got[i, 16:32, :].astype(jnp.float32)
        total = both[:, size // 2 : size // 2 + 1] + both[:, size - 1 : size]
        return far_got[i, 0:16, :].astype(jnp.float32), both[:, 0:1], total

    far_peak = lax.fori_loop(
        1, count, lambda i, m: jnp.maximum(m, terms(i)[1]), terms(0)[1], unroll=4
    )

    def add(i, so_far):
        acc, peak, total = terms(i)
        factor = jnp.exp(peak - far_peak)
        return so_far[0] + acc * factor, so_far[1] + total * factor

    far_acc, far_total = lax.fori_loop(
        0,
        count,
        add,
        (jnp.zeros((16, size), jnp.float32), jnp.zeros((16, 1), jnp.float32)),
        unroll=4,
    )
    far[me] = (far_acc / far_total).astype(far.dtype)
    each(lambda k: small(3, k, False, far, far).start())
    forward(2)
    forward(3)
    nearby(1)

    for c in range(heads, units):
        forward(c)

    nearby(2)
    nearby(3)

    each(lambda k: small(3, k, False, far, far).wait())
    for c in range(heads):
        distant(c)
        if c > 0:
            att_over(c - 1).wait_recv()
            att_on(c - 1).start()
        att_over(c).start()
        att_mate(c).start()
    att_over(heads - 1).wait_recv()
    att_on(heads - 1).start()
    for c in range(heads):
        att_over(c).wait_send()
        att_mate(c).wait()
        att_on(c).wait()
    for k in range(3):
        weight_copy(k).wait()


def front(lists, kv, q, heads, weight, scale, count, tp_count):
    blocks, rows, half = q.shape
    size = half // heads
    pair = 2 * size
    kept = kv.dtype
    vmem = pl.BlockSpec(memory_space=VMEM)
    hbm = pl.BlockSpec(memory_space=pl.ANY)
    cols = weight.shape[1] // tp_count
    moved = jax.ShapeDtypeStruct((weight.shape[0], cols), kept)
    same = jax.ShapeDtypeStruct(q.shape, kept)
    cut = (heads * pair + heads * size) // 4
    dma = pltpu.SemaphoreType.DMA
    return pl.pallas_call(
        functools.partial(front_kernel, count, scale),
        name="front",
        out_shape=(jax.ShapeDtypeStruct(q.shape, kept),) + (moved,) * 3 + (same,) * 3,
        in_specs=[pl.BlockSpec(memory_space=SMEM), vmem, vmem, hbm],
        out_specs=(vmem,) + (hbm,) * 6,
        scratch_shapes=[
            VMEM((blocks, rows, 2 * half), kept),
            VMEM((2 * heads, blocks + 2 * MAXR, rows, size), kept),
            VMEM((count, 16, cut), kept),
            VMEM((count, 16, cut), kept),
            VMEM((count, 16, cut), kept),
            VMEM((G, rows, heads * pair), kept),
            VMEM((G, rows, heads * size), kept),
            VMEM((count, 32, size), kept),
            VMEM((count, 32, size), kept),
            VMEM((count, 16, size), kept),
        ]
        + [VMEM((2 * blocks, rows, size), kept)] * (2 * heads)
        + [VMEM((LINE * FIRST, rows, size), kept)] * (2 * heads)
        + [VMEM((LINE * SECOND, rows, size), kept)] * (2 * heads)
        + [
            VMEM((2 * heads, (LINE - 1) * FIRST, rows, size), kept),
            VMEM((2 * heads, (LINE - 1) * SECOND, rows, size), kept),
            VMEM((heads, blocks, rows, size), jnp.float32),
            VMEM((heads, blocks, rows, size), jnp.float32),
            dma((3, heads)),
            dma((3, heads)),
            dma((2 * heads,)),
            dma((2 * heads,)),
            dma((2 * heads,)),
            dma((2 * heads,)),
            dma((3,)),
            dma((3,)),
            dma((4, count)),
            dma((4, count)),
            dma((2, 2 * heads, LINE - 1)),
            dma((2, 2 * heads, LINE - 1)),
        ],
        compiler_params=pltpu.CompilerParams(
            collective_id=3, has_side_effects=True, vmem_limit_bytes=60 * 2**20
        ),
    )(lists, kv, q, weight)


STRIDE = 16
HEADER = 24
ROUTE = 2 * LINE * STRIDE + 40


def plan_kernel(count, blocks, req_ref, reach_ref, gb_ref, out_ref):
    me = lax.axis_index("ctx")
    x, z, level = me // 8, lax.rem(me // 2, LINE), lax.rem(me, 2)
    many = 2 * blocks
    total = count * blocks
    low = jnp.bfloat16

    def iota(shape, dim):
        return lax.broadcasted_iota(jnp.int32, shape, dim)

    def product(a, b):
        return jnp.dot(a.astype(low), b.astype(low), preferred_element_type=jnp.float32)

    def flag(condition):
        return jnp.where(condition, 1.0, 0.0)

    ids = iota((count, total), 1)
    asked = jnp.zeros((count, total), jnp.float32)
    for e in range(blocks * R):
        asked = jnp.where(req_ref[:, e : e + 1] == ids, 1.0, asked)

    def groups(shape, dim):
        index = iota(shape, dim)
        group = jnp.floor((index.astype(jnp.float32) + 0.5) / many).astype(jnp.int32)
        return index, group

    index, group = groups((1, total), 1)
    place = {"x": group >> 2, "z": group & 3}
    inner = (index - group * many).astype(jnp.float32)
    group_col = groups((total, 1), 0)[1]
    place_col = {"x": group_col >> 2, "z": group_col & 3}
    before = iota((total, total), 0) < iota((total, total), 1)

    r8, s8 = iota((8, count), 0), iota((8, count), 1)
    where_of = {"x": s8 >> 3, "z": (s8 >> 1) & 3}
    lane = iota((8, 128), 1)
    line8 = iota((8, 128), 0) >> 1
    lane32 = iota((count, 128), 1)
    row32 = iota((count, 128), 0)
    own32 = {"x": row32 >> 3, "z": (row32 >> 1) & 3}
    pair_of = {"x": lane >> 2, "z": lane & 3}
    seats = flag(group_col == iota((total, 128), 1))
    longest = []
    for first, second in (("x", "z"), ("z", "x")):
        same = (where_of[first] == r8 >> 1) & ((s8 & 1) == (r8 & 1))
        need = flag(product(flag(same), asked) > 0)
        counts = product(need, seats)
        apart = (lane < LINE * LINE) & (pair_of[first] != line8)
        longest.append(jnp.max(jnp.where(apart, counts - FIRST, -1.0)))
        counts = product(asked, flag(place_col[second] == iota((total, 128), 1)))
        apart = (lane32 < LINE) & (lane32 != own32[second])
        longest.append(jnp.max(jnp.where(apart, counts - SECOND, -1.0)))
    over = jnp.maximum(
        jnp.maximum(longest[0], longest[1]), jnp.maximum(longest[2], longest[3])
    )

    head = iota((HEADER, 128), 0)
    top = jnp.where(head == 20, jnp.where(over > 0, 0, 1), 0)
    entries = []
    for g in range(G):
        entries.append((g, gb_ref[g] // blocks))
        entries.append((G + g, lax.rem(gb_ref[g], blocks)))
    for h in range(4):
        entries.append((2 * G + h, reach_ref[h]))
    for b in range(blocks):
        block = me * blocks + b
        which = jnp.where(block == gb_ref[0], 0, jnp.where(block == gb_ref[1], 1, -1))
        entries.append((2 * G + 4 + b, which))
    for k, value in entries:
        top = jnp.where(head == k, value, top)
    out_ref[0:HEADER, :] = top

    spots = {"x": x, "z": z}
    mine = (place["x"] == x) & (place["z"] == z)
    turn = iota((8, total), 0)
    listed = blocks * R
    own_row = jnp.sum(
        jnp.where(iota((count, listed), 0) == me, req_ref[...], 0), axis=0, keepdims=True
    )
    asked_col = jnp.sum(
        jnp.where(iota((40, listed), 0) == iota((40, listed), 1), own_row, 0), axis=1, keepdims=True
    )

    def store(offset, column):
        out_ref[offset : offset + column.shape[0], :] = jnp.broadcast_to(
            column.astype(jnp.int32), (column.shape[0], 128)
        )

    for o, (first, second) in enumerate((("x", "z"), ("z", "x"))):
        start = HEADER + o * ROUTE
        line_first = place[first].astype(jnp.float32)
        line_second = place[second].astype(jnp.float32)
        same = (where_of[first] == r8) & ((s8 & 1) == level)
        need = flag(product(flag(same), asked) > 0)
        rank = product(need, flag(before & (group_col == group)))
        slot = iota((STRIDE, total), 0).astype(jnp.float32)
        for t in range(LINE):
            hit = (need[t : t + 1] > 0) & mine & (rank[t : t + 1] == slot)
            column = jnp.sum(jnp.where(hit, inner, 0.0), axis=1, keepdims=True)
            store(start + t * STRIDE, column)
        my_rank = jnp.sum(jnp.where(turn == spots[first], rank, 0.0), axis=0, keepdims=True)
        found = jnp.where(
            place[first] == spots[first],
            inner,
            many + line_first * FIRST + jnp.minimum(my_rank, FIRST - 1),
        )
        line = (where_of[first] == spots[first]) & (where_of[second] == r8)
        here = product(flag(line & ((s8 & 1) == level)), asked)
        wanted = flag((here > 0) & (place[second] == spots[second]))
        rank = product(wanted, flag(before))
        for t in range(LINE):
            hit = (wanted[t : t + 1] > 0) & (rank[t : t + 1] == slot)
            column = jnp.sum(jnp.where(hit, found, 0.0), axis=1, keepdims=True)
            store(start + (LINE + t) * STRIDE, column)
        own = jnp.sum(jnp.where(turn == spots[second], here, 0.0), axis=0, keepdims=True)
        rank = product(
            jnp.broadcast_to(own, (8, total)),
            flag(before & (place_col[second] == place[second])),
        )[0:1]
        final = jnp.where(
            place[second] == spots[second],
            found,
            many + LINE * FIRST + line_second * SECOND + jnp.minimum(rank, SECOND - 1),
        )
        hit = asked_col == iota((40, total), 1)
        column = jnp.sum(jnp.where(hit, final, 0.0), axis=1, keepdims=True)
        store(start + 2 * LINE * STRIDE, column)


def plan(random_blocks, global_blocks, window_reach, blocks, count):
    requests = random_blocks.reshape(count, blocks * R)
    vmem = pl.BlockSpec(memory_space=VMEM)
    smem = pl.BlockSpec(memory_space=SMEM)
    out = pl.pallas_call(
        functools.partial(plan_kernel, count, blocks),
        name="plan",
        out_shape=jax.ShapeDtypeStruct((HEADER + 2 * ROUTE, 128), jnp.int32),
        in_specs=[vmem] + [smem] * 2,
        out_specs=vmem,
        compiler_params=pltpu.CompilerParams(vmem_limit_bytes=48 * 2**20),
    )(requests, window_reach, global_blocks)
    return out[:, 0]


def direct(place, info, source_ids, my_index, kv, q, out_weight, scale, count, slots):
    block_count = q.shape[0]
    heads = info.shape[0] - block_count
    ext, gkv, gq = edges(place, kv, q, count)
    partials = far_partials(gq, kv, scale, heads, count)
    random, far = exchange(source_ids, kv, partials, count, slots)
    attended = attention(
        my_index, info, q, ext, gkv, far, random, scale, heads, count * block_count
    )
    tp = lax.axis_index("tp")
    tp_count = lax.axis_size("tp")
    cols = out_weight.shape[1] // tp_count
    mates = (tp, tp + 1 - 2 * lax.rem(tp, 2), lax.rem(tp + 2, tp_count), tp_count - 1 - tp)
    weights = []
    for k in range(1, tp_count):
        block = lax.dynamic_slice_in_dim(out_weight, mates[k] * cols, cols, axis=1)
        weights.append(lax.ppermute(block, "tp", [(i, i ^ k) for i in range(tp_count)]))
    for k in range(1, tp_count):
        weights.append(lax.ppermute(attended, "tp", [(i, i ^ k) for i in range(tp_count)]))
    return (attended, *weights)


def shards(
    queries,
    keyvals,
    residual,
    out_weight,
    norm_gain,
    norm_bias,
    cross_weight,
    window_reach,
    global_blocks,
    random_blocks,
):
    tok_rows, head_cols = queries.shape
    head_count = window_reach.shape[0]
    head_size = head_cols // head_count
    ctx_count = lax.axis_size("ctx")
    tp_count = lax.axis_size("tp")
    me = lax.axis_index("ctx")
    block_count = tok_rows // BLOCK
    scale = 1.0 / math.sqrt(head_size)
    q = queries.reshape(block_count, BLOCK, head_cols)
    lists = plan(random_blocks, global_blocks, window_reach, block_count, ctx_count)
    fits = lists[20] > 0

    def staged(keyvals, q, out_weight):
        return tuple(front(lists, keyvals, q, head_count, out_weight, scale, ctx_count, tp_count))

    def plain(keyvals, q, out_weight):
        req_count = block_count * R
        slots = 1 + (req_count + ctx_count - 2) // ctx_count
        requests = random_blocks.reshape(ctx_count, req_count)
        owners = requests // block_count
        local_ids = requests % block_count
        positions = jnp.arange(req_count, dtype=jnp.int32)
        earlier = positions[None, :] < positions[:, None]
        ranks = jnp.sum(
            ((owners[:, :, None] == owners[:, None, :]) & earlier[None, :, :]).astype(jnp.int32),
            axis=2,
        )
        slot_ids = jnp.arange(slots, dtype=jnp.int32)
        matches = (owners[:, None, :] == me) & (ranks[:, None, :] == slot_ids[None, :, None])
        source_ids = jnp.sum(jnp.where(matches, local_ids[:, None, :], 0), axis=2).reshape(-1)
        my_index = lax.dynamic_index_in_dim(owners * slots + ranks, me, 0, keepdims=False)
        place = lists[: 2 * G]
        info = lists[2 * G : 2 * G + head_count + block_count]
        return direct(
            place,
            info,
            source_ids,
            my_index,
            keyvals.reshape(block_count, BLOCK, 2 * head_cols),
            q, out_weight, scale, ctx_count, slots
        )

    attended, *rest = lax.cond(fits, staged, plain, keyvals, q, out_weight)
    weights = rest[: tp_count - 1]
    gathered = [x.reshape(tok_rows, head_cols) for x in [attended] + rest[tp_count - 1 :]]
    cols = residual.shape[1]
    encoded, cross_kv = project(
        gathered,
        residual,
        jnp.stack([norm_gain, norm_bias]),
        out_weight,
        weights,
        cross_weight,
        ctx_count,
        tp_count,
    )
    return (encoded, cross_kv)


def solution(mesh):
    placed = (
        P("ctx", "tp"),
        P("ctx", None, "tp"),
        P("ctx", "tp"),
        P("tp", None),
        P("tp"),
        P("tp"),
        P(None, None, "tp"),
        P("tp"),
        P(),
        P(),
    )
    return jax.shard_map(
        shards,
        mesh=mesh,
        in_specs=placed,
        out_specs=(P("ctx", "tp"), P("ctx", None, "tp")),
        check_vma=False,
    )
```
